32 devices in a mesh: dp: 8 (over y, x, core), seq: 4 (over z).
Axes of the slice: x: 2, y: 2, z: 4, core: 2. Of those that a mesh axis runs over, the one named last changes fastest.
Arguments:
- hidden_in: bfloat16 [8, 2048, 2048], P('dp', 'seq'), may hold values from -6 to 6
- memory: bfloat16 [8, 2048, 2048], P('dp', 'seq'), may hold values from -6 to 6
- segments: int32 [8, 2048], P('dp'), may hold values from 0 to 3, never falling along the last dimension, each value on 1 to 1200 neighbouring positions
- gain_attn: bfloat16 [2048], P(('dp', 'seq')), may hold values from 0.25 to 1.75
- w_query: bfloat16 [2048, 2048], P(('dp', 'seq')), may hold values from -0.125 to 0.125
- w_key: bfloat16 [2048, 2048], P(('dp', 'seq')), may hold values from -0.125 to 0.125
- w_value: bfloat16 [2048, 2048], P(('dp', 'seq')), may hold values from -0.125 to 0.125
- w_out: bfloat16 [2048, 2048], P(('dp', 'seq')), may hold values from -0.75 to 0.75
- gain_ffn: bfloat16 [2048], P(('dp', 'seq')), may hold values from 0.25 to 1.75
- w_gate: bfloat16 [5504, 2048], P(('dp', 'seq')), may hold values from -0.125 to 0.125
- w_up: bfloat16 [5504, 2048], P(('dp', 'seq')), may hold values from -0.125 to 0.125
- w_down: bfloat16 [5504, 2048], P(('dp', 'seq')), may hold values from -0.078125 to 0.078125
- cotangent: bfloat16 [8, 2048, 2048], P('dp', 'seq'), may hold values from -6 to 6
Outputs:
- layer_out: bfloat16 [8, 2048, 2048], P('dp', 'seq')
- grad_hidden: float32 [8, 2048, 2048], P('dp', 'seq')
- grad_memory: float32 [8, 2048, 2048], P('dp', 'seq')
- grad_gain_attn: float32 [2048], P(('dp', 'seq'))
- grad_w_query: float32 [2048, 2048], P(('dp', 'seq'))
- grad_w_key: float32 [2048, 2048], P(('dp', 'seq'))
- grad_w_value: float32 [2048, 2048], P(('dp', 'seq'))
- grad_w_out: float32 [2048, 2048], P(('dp', 'seq'))
- grad_gain_ffn: float32 [2048], P(('dp', 'seq'))
- grad_w_gate: float32 [5504, 2048], P(('dp', 'seq'))
- grad_w_up: float32 [5504, 2048], P(('dp', 'seq'))
- grad_w_down: float32 [5504, 2048], P(('dp', 'seq'))
The draws below stay inside these ranges and needn't reach their ends.
Inputs may be any that keep to these rules, and one draw needn't show every extreme that they name: `segments`: along each sequence the numbers never fall; each number is held by 1 to 1200 consecutive tokens, and in every draw some document has exactly 1200.
All inputs are finite; a program needn't handle non-finite values.
Results may differ from the reference program's by a relative error of at most 0.019.
Values may be sent and summed in bfloat16 or wider, within the bound.
A program may use at most 384 MiB of HBM per device.

```python
import math
import jax
import jax.numpy as jnp
import numpy as np
from jax import lax

D = 2048
HEAD_DIM = 128
FF = 5504
LEN = 2048
DOCS = 4
DOC_MOST = 1200
SEQS = 8


def block_levels(own_key, extent, cuts, low, largest):
    factor_of, own = 1.0, jax.random.fold_in(own_key, 6)
    for axis_at, parts in cuts:
        draws = jnp.exp(jax.random.uniform(jax.random.fold_in(own, axis_at), (parts,), jnp.float32, low / len(cuts), largest / len(cuts)))
        factor_of = factor_of * jnp.repeat(draws, extent[axis_at] // parts).reshape([-1 if axis == axis_at else 1 for axis in range(len(extent))])
    return factor_of


def split_up(count, total, most, lean):
    portions = [(1 << 20) // math.isqrt(grade ** lean) + 1 for grade in range(2, count + 1)]
    spare, holding = total - most - (count - 1), [1] * (count - 1)
    while spare > 0:
        candidates = [i for i in range(count - 1) if holding[i] < most]
        mass, remaining = sum([portions[i] for i in candidates]), spare
        for i in candidates:
            addition = min(most - holding[i], max(1, remaining * portions[i] // mass), spare)
            holding[i] = holding[i] + addition
            spare = spare - addition
    return np.array([most] + holding)


def ragged(own_key, count, total, most, lean):
    if count == 2:
        one = jax.random.randint(own_key, (), max(1, total - most), min(most, total - 1) + 1)
        return jnp.stack([one, total - one])
    sizes = jnp.asarray(split_up(count, total, most, lean), jnp.int32)
    twos = (count - 1) // 2
    donor, sink = sizes[1:1 + 2 * twos:2], sizes[2:2 + 2 * twos:2]
    room = jnp.minimum(donor - 1, most - sink)
    moved = jax.random.randint(jax.random.fold_in(own_key, 1), (twos,), 0, 1 << 20) % (room + 1)
    sizes = sizes.at[1:1 + 2 * twos:2].set(donor - moved).at[2:2 + 2 * twos:2].set(sink + moved)
    return sizes[jax.random.permutation(jax.random.fold_in(own_key, 2), count)]


def scatter_about(key, dims, scale, limit, shards=(), kind=jnp.bfloat16):
    values = jax.random.normal(key, dims, jnp.float32) * scale
    if len(shards) > 0:
        values = block_levels(key, dims, shards, -0.22, 0.18) * values
    return jnp.clip(values, min=-limit, max=limit).astype(kind)


def setup_inputs(seed: int = 0) -> dict:
    arg_keys = jax.random.split(jax.random.key(seed), 14)
    return {
        "hidden_in": scatter_about(arg_keys[0], (SEQS, LEN, D), 1.0, 6.0, ((0, 8), (1, 4))),
        "memory": scatter_about(arg_keys[1], (SEQS, LEN, D), 1.0, 6.0, ((0, 8), (1, 4))),
        "segments": jax.vmap(lambda own: jnp.searchsorted(jnp.cumsum(ragged(own, DOCS, LEN, DOC_MOST, 1)), jnp.arange(LEN), side="right"))(jax.random.split(arg_keys[2], SEQS)).reshape((SEQS, LEN)).astype(jnp.int32),
        "gain_attn": jnp.clip(1.0 + 0.15 * jax.random.normal(arg_keys[3], (D,), jnp.float32), 0.25, 1.75).astype(jnp.bfloat16),
        "w_query": scatter_about(arg_keys[4], (D, D), D ** -0.5, 0.125, ((0, 32),)),
        "w_key": scatter_about(arg_keys[5], (D, D), D ** -0.5, 0.125, ((0, 32),)),
        "w_value": scatter_about(arg_keys[6], (D, D), D ** -0.5, 0.125, ((0, 32),)),
        "w_out": scatter_about(arg_keys[7], (D, D), (D // 32) ** -0.5, 0.75, ((0, 32),)),
        "gain_ffn": jnp.clip(1.0 + 0.15 * jax.random.normal(arg_keys[8], (D,), jnp.float32), 0.25, 1.75).astype(jnp.bfloat16),
        "w_gate": scatter_about(arg_keys[9], (FF, D), D ** -0.5, 0.125, ((0, 32),)),
        "w_up": scatter_about(arg_keys[10], (FF, D), D ** -0.5, 0.125, ((0, 32),)),
        "w_down": scatter_about(arg_keys[11], (FF, D), FF ** -0.5, 0.078125, ((0, 32),)),
        "cotangent": scatter_about(arg_keys[12], (SEQS, LEN, D), 1.0, 6.0, ((0, 8), (1, 4))),
    }


EPSILON = 1e-06
MASKED = -1e+30

@jax.custom_vjp
def low(v):
    return lax.optimization_barrier(v.astype(jnp.bfloat16)).astype(jnp.float32)

@jax.custom_vjp
def low_back(v):
    return v

def low_keep(v):
    return (low(v), None)

def low_pass(kept, grad):
    return (grad,)

def back_keep(v):
    return (v, None)

def back_low(kept, grad):
    return (low(grad),)
low.defvjp(low_keep, low_pass)
low_back.defvjp(back_keep, back_low)

def product(left, right):
    return jnp.dot(left, right, precision=lax.Precision.HIGHEST, preferred_element_type=jnp.float32)

def normalize(values):
    return values * lax.rsqrt(lax.optimization_barrier(jnp.mean(values * values, axis=-1, keepdims=True)) + EPSILON)

def attend_sequence(item):
    query, key, value, segment_ids = item
    length = query.shape[0]
    score = jnp.einsum('qhd,khd->hqk', query, key, precision=lax.Precision.HIGHEST) * HEAD_DIM ** (-0.5)
    score = low_back(score)
    position = jnp.arange(length)
    keep = (position[None, :] <= position[:, None]) & (segment_ids[:, None] == segment_ids[None, :])
    score = jnp.where(keep[None], score, MASKED)
    top = lax.optimization_barrier(jnp.max(score, axis=-1, keepdims=True))
    expo = jnp.exp(score - top)
    prob = expo / lax.optimization_barrier(jnp.sum(expo, axis=-1, keepdims=True))
    context = jnp.einsum('hqk,khd->qhd', low(prob), value, precision=lax.Precision.HIGHEST)
    return low_back(low(context))

def layer(hidden, memory, segment_ids, gain_attn, w_query, w_key, w_value, w_out, gain_ffn, w_gate, w_up, w_down):
    group, length, width = hidden.shape
    heads = width // HEAD_DIM
    flat_hidden = hidden.reshape(group * length, width)
    flat_memory = memory.reshape(group * length, width)
    attn_in = low(normalize(flat_hidden) * gain_attn)
    query = low_back(low(product(attn_in, w_query)))
    key = low_back(low(product(flat_memory, w_key)))
    value = low_back(low(product(flat_memory, w_value)))
    shape = (group, length, heads, HEAD_DIM)
    context = lax.map(jax.checkpoint(attend_sequence), (query.reshape(shape), key.reshape(shape), value.reshape(shape), segment_ids))
    context = context.reshape(group * length, width)
    mid = flat_hidden + low_back(product(context, w_out))
    ffn_in = low(normalize(mid) * gain_ffn)
    gate = low_back(product(ffn_in, w_gate.T))
    up = low_back(product(ffn_in, w_up.T))
    act = low(gate * jax.nn.sigmoid(gate) * up)
    result = mid + low_back(product(act, w_down))
    return result.reshape(group, length, width)

def reference(hidden_in, memory, segments, gain_attn, w_query, w_key, w_value, w_out, gain_ffn, w_gate, w_up, w_down, cotangent):
    params = tuple((weight.astype(jnp.float32) for weight in (gain_attn, w_query, w_key, w_value, w_out, gain_ffn, w_gate, w_up, w_down)))
    group = math.gcd(SEQS, max(1, 4096 // LEN))
    rounds = SEQS // group

    def split(values):
        return values.reshape((rounds, group) + values.shape[1:])

    def one_group(totals, item):
        hidden, mem_part, segment_ids, grad_out = item

        def forward(hidden_part, memory_part, *weights):
            return layer(hidden_part, memory_part, segment_ids, *weights)
        result, pull = jax.vjp(forward, hidden.astype(jnp.float32), mem_part.astype(jnp.float32), *params)
        grads = pull(grad_out.astype(jnp.float32))
        totals = tuple((total + grad for total, grad in zip(totals, grads[2:])))
        return (totals, (result.astype(jnp.bfloat16), grads[0], grads[1]))
    initial = tuple((jnp.zeros(weight.shape, jnp.float32) for weight in params))
    totals, (outputs, grad_hidden, grad_memory) = lax.scan(one_group, initial, (split(hidden_in), split(memory), split(segments), split(cotangent)))
    shape = (SEQS, LEN, D)
    return (outputs.reshape(shape), grad_hidden.reshape(shape), grad_memory.reshape(shape), totals[0], totals[1], totals[2], totals[3], totals[4], totals[5], totals[6], totals[7], totals[8])
```

```python
import functools
import math

import jax
import jax.numpy as jnp
from jax import lax
from jax.experimental import pallas as pl
from jax.experimental.pallas import tpu as pltpu
from jax.sharding import PartitionSpec as P

HEAD_DIM = 128
EPSILON = 1e-06
MASKED = -1e30
ALL = ("dp", "seq")
F32 = jnp.float32
BF16 = jnp.bfloat16
EXP2_SCALE = HEAD_DIM ** (-0.5) * math.log2(math.e)
NT = (((1,), (1,)), ((), ()))
TN = (((0,), (0,)), ((), ()))
NN = (((1,), (0,)), ((), ()))


def mxu(left, right, dims):
    return lax.dot_general(left, right, dims, preferred_element_type=F32)


def rms_scale(values):
    return lax.rsqrt(jnp.mean(values * values, axis=-1, keepdims=True) + EPSILON)


def norm_back(grad_normed, normed, rstd, gain):
    scaled = grad_normed * gain
    return rstd * (scaled - normed * jnp.mean(scaled * normed, axis=-1, keepdims=True))


def forward_kernel(block, low_ref, start_ref, q_ref, k_ref, v_ref, out_ref, lse_ref):
    length = q_ref.shape[0]

    def one_query_block(qb, _):
        q0 = pl.multiple_of(qb * block, block)
        rows = pl.ds(q0, block)
        query = q_ref[rows, :]
        start = start_ref[:, rows]
        query_pos = q0 + lax.broadcasted_iota(jnp.int32, (block, block), 1)

        def one_key_block(kb, carry):
            top, total, acc = carry
            k0 = pl.multiple_of(kb * block, block)
            keys = pl.ds(k0, block)
            score = mxu(k_ref[keys, :], query, NT)
            key_pos = k0 + lax.broadcasted_iota(jnp.int32, (block, block), 0)
            score = jnp.where((key_pos >= start) & (key_pos <= query_pos), score, MASKED)
            new_top = jnp.maximum(top, jnp.max(score, axis=0, keepdims=True))
            shrink = jnp.exp2((top - new_top) * EXP2_SCALE)
            raised = jnp.exp2((score - new_top) * EXP2_SCALE)
            total = total * shrink + jnp.sum(raised, axis=0, keepdims=True)
            acc = acc * shrink + mxu(v_ref[keys, :], raised.astype(BF16), TN)
            return new_top, total, acc

        top, total, acc = lax.fori_loop(
            low_ref[qb],
            qb + 1,
            one_key_block,
            (
                jnp.full((1, block), MASKED, F32),
                jnp.zeros((1, block), F32),
                jnp.zeros((HEAD_DIM, block), F32),
            ),
        )
        out_ref[rows, :] = (acc / total).T.astype(BF16)
        lse_ref[0, :, rows] = top * EXP2_SCALE + jnp.log2(total)
        return 0

    lax.fori_loop(0, length // block, one_query_block, 0)


def backward_kernel(
    block, high_ref, start_ref, q_ref, k_ref, v_ref, ctx_ref, grad_ref, lse_ref,
    dq_ref, dk_ref, dv_ref, dq_acc, delta_acc,
):
    length = q_ref.shape[0]
    blocks = length // block
    scale = HEAD_DIM ** (-0.5)
    dq_acc[...] = jnp.zeros_like(dq_acc)

    def one_delta(qb, _):
        rows = pl.ds(pl.multiple_of(qb * block, block), block)
        both = ctx_ref[rows, :].astype(F32) * grad_ref[rows, :].astype(F32)
        delta_acc[:, rows] = jnp.sum(both.T, axis=0, keepdims=True)
        return 0

    lax.fori_loop(0, blocks, one_delta, 0)

    def one_key_block(kb, _):
        k0 = pl.multiple_of(kb * block, block)
        keys = pl.ds(k0, block)
        key = k_ref[keys, :]
        value = v_ref[keys, :]
        key_pos = k0 + lax.broadcasted_iota(jnp.int32, (block, block), 0)

        def one_query_block(qb, carry):
            dk, dv = carry
            q0 = pl.multiple_of(qb * block, block)
            rows = pl.ds(q0, block)
            query = q_ref[rows, :]
            grad = grad_ref[rows, :]
            start = start_ref[:, rows]
            query_pos = q0 + lax.broadcasted_iota(jnp.int32, (block, block), 1)
            score = mxu(key, query, NT)
            prob = jnp.exp2(score * EXP2_SCALE - lse_ref[0, :, rows])
            prob = jnp.where((key_pos >= start) & (key_pos <= query_pos), prob, 0.0)
            grad_prob = mxu(value, grad, NT)
            grad_score = (prob * (grad_prob - delta_acc[:, rows])).astype(BF16)
            dv = dv + mxu(prob.astype(BF16), grad, NN)
            dk = dk + mxu(grad_score, query, NN)
            dq_acc[rows, :] += mxu(grad_score, key, TN)
            return dk, dv

        zeros = jnp.zeros((block, HEAD_DIM), F32)
        dk, dv = lax.fori_loop(kb, high_ref[kb], one_query_block, (zeros, zeros))
        dk_ref[keys, :] = (dk * scale).astype(BF16)
        dv_ref[keys, :] = dv.astype(BF16)
        return 0

    lax.fori_loop(0, blocks, one_key_block, 0)
    dq_ref[...] = (dq_acc[...] * scale).astype(BF16)


def attention_calls(length, heads, block):
    column = pl.BlockSpec((length, HEAD_DIM), lambda h, *_: (0, h))
    row = pl.BlockSpec((1, length), lambda h, *_: (0, 0))
    stat = pl.BlockSpec((1, 1, length), lambda h, *_: (h, 0, 0))
    flat = jax.ShapeDtypeStruct((length, heads * HEAD_DIM), BF16)
    pairs = heads * length * length // 4
    forward = pl.pallas_call(
        functools.partial(forward_kernel, block),
        grid_spec=pltpu.PrefetchScalarGridSpec(
            num_scalar_prefetch=1,
            grid=(heads,),
            in_specs=[row, column, column, column],
            out_specs=[column, stat],
        ),
        out_shape=(flat, jax.ShapeDtypeStruct((heads, 1, length), F32)),
        cost_estimate=pl.CostEstimate(
            flops=16 * pairs * HEAD_DIM, transcendentals=pairs, bytes_accessed=8 * length * heads * HEAD_DIM
        ),
        name="attend_forward",
    )
    backward = pl.pallas_call(
        functools.partial(backward_kernel, block),
        grid_spec=pltpu.PrefetchScalarGridSpec(
            num_scalar_prefetch=1,
            grid=(heads,),
            in_specs=[row, column, column, column, column, column, stat],
            out_specs=[column, column, column],
            scratch_shapes=[pltpu.VMEM((length, HEAD_DIM), F32), pltpu.VMEM((1, length), F32)],
        ),
        out_shape=(flat, flat, flat),
        cost_estimate=pl.CostEstimate(
            flops=40 * pairs * HEAD_DIM, transcendentals=pairs, bytes_accessed=16 * length * heads * HEAD_DIM
        ),
        name="attend_backward",
    )
    return forward, backward


def document_bounds(segment_ids, block):
    length = segment_ids.shape[0]
    position = jnp.arange(length, dtype=jnp.int32)
    same = segment_ids[:, None] == segment_ids[None, :]
    first = jnp.min(jnp.where(same, position[None, :], length), axis=1)
    last = jnp.max(jnp.where(same, position[None, :], -1), axis=1)
    low = first[::block] // block
    high = last[block - 1 :: block] // block + 1
    return first[None, :], low, high


def shards(
    hidden_in, memory, segments, gain_attn, w_query, w_key, w_value, w_out, gain_ffn, w_gate, w_up, w_down, cotangent
):
    seqs, piece, width = hidden_in.shape
    groups = lax.axis_size("seq")
    assert seqs == 1
    length = piece * groups
    share = width // groups
    heads = share // HEAD_DIM
    block = min(512, length)
    tokens = hidden_in.reshape(piece, width)
    mem = memory.reshape(piece, width)
    grad_out = cotangent.reshape(piece, width)

    def gather_all(value):
        return lax.all_gather(value, ALL, axis=0, tiled=True)

    def gather_dp(value):
        return lax.all_gather(value, "dp", axis=0, tiled=True)

    def to_heads(value):
        return lax.all_to_all(value, "seq", split_axis=0, concat_axis=0, tiled=True)

    attend_forward, attend_backward = attention_calls(length, heads, block)
    start, low, high = document_bounds(segments[0], block)

    hidden32 = tokens.astype(F32)
    rstd_in = rms_scale(hidden32)
    normed_in = hidden32 * rstd_in
    gain_attn32 = gather_all(gain_attn).astype(F32)
    gain_ffn32 = gather_all(gain_ffn).astype(F32)
    attn_in = (normed_in * gain_attn32).astype(BF16)

    key_rows = gather_all(w_key)
    value_rows = gather_all(w_value)
    query_rows = gather_all(w_query)
    out_rows = gather_all(w_out)

    def project(left, rows):
        return jnp.einsum(
            "td,dge->gte", left, rows.reshape(width, groups, share), preferred_element_type=F32
        ).astype(BF16)

    flat = (length, share)
    split = (groups, piece, share)
    key = to_heads(project(mem, key_rows)).reshape(flat)
    value = to_heads(project(mem, value_rows)).reshape(flat)
    query = to_heads(project(attn_in, query_rows)).reshape(flat)
    context_heads, lse = attend_forward(low, start, query, key, value)
    context = to_heads(context_heads.reshape(split))

    out_split = out_rows.reshape(groups, share, width)
    mid = hidden32 + jnp.einsum("gte,ged->td", context, out_split, preferred_element_type=F32)
    rstd_mid = rms_scale(mid)
    normed_mid = mid * rstd_mid
    ffn_in = (normed_mid * gain_ffn32).astype(BF16)

    def gather_units(weight):
        return lax.all_gather(weight, "seq", axis=0, tiled=True)

    gate_rows, up_rows, down_rows = gather_units(w_gate), gather_units(w_up), gather_units(w_down)
    dy = gather_dp(grad_out)
    ffn_all = gather_dp(ffn_in)
    gate = mxu(ffn_all, gate_rows, NT)
    up = mxu(ffn_all, up_rows, NT)
    sig = jax.nn.sigmoid(gate)
    act = (gate * sig * up).astype(BF16)
    grad_act = mxu(dy, down_rows, NT)
    grad_gate = (grad_act * up * sig * (1.0 + gate * (1.0 - sig))).astype(BF16)
    grad_up = (grad_act * gate * sig).astype(BF16)

    def scatter_dp(value):
        return lax.psum_scatter(value, "dp", scatter_dimension=0, tiled=True)

    grad_ffn_in = scatter_dp((mxu(grad_gate, gate_rows, NN) + mxu(grad_up, up_rows, NN)).astype(BF16)).astype(F32)
    branch = scatter_dp(mxu(act, down_rows, NN).astype(BF16)).astype(F32)
    layer_out = (mid + branch).astype(BF16)

    def scatter_units(value):
        return lax.psum_scatter(value.astype(BF16), "seq", scatter_dimension=0, tiled=True).astype(F32)

    grad_w_down = scatter_units(mxu(act, dy, TN))
    grad_w_gate = scatter_units(mxu(grad_gate, ffn_all, TN))
    grad_w_up = scatter_units(mxu(grad_up, ffn_all, TN))

    grad_gain_ffn_all = jnp.sum(normed_mid * grad_ffn_in, axis=0)
    grad_mid = grad_out.astype(F32) + norm_back(grad_ffn_in, normed_mid, rstd_mid, gain_ffn32)
    grad_branch = grad_mid.astype(BF16)
    grad_context = jnp.einsum("td,ged->gte", grad_branch, out_split, preferred_element_type=F32).astype(BF16)
    grad_context_heads = to_heads(grad_context).reshape(flat)
    dq, dk, dv = attend_backward(high, start, query, key, value, context_heads, grad_context_heads, lse)
    dq, dk, dv = [to_heads(part.reshape(split)) for part in (dq, dk, dv)]

    def unproject(part, rows):
        return jnp.einsum(
            "gte,dge->td", part, rows.reshape(width, groups, share), preferred_element_type=F32
        )

    grad_attn_in = unproject(dq, query_rows)
    grad_memory = unproject(dk, key_rows) + unproject(dv, value_rows)
    grad_gain_attn_all = jnp.sum(normed_in * grad_attn_in, axis=0)
    grad_hidden = grad_mid + norm_back(grad_attn_in, normed_in, rstd_in, gain_attn32)

    def weight_term(left, part):
        return jnp.einsum("td,gte->dge", left, part, preferred_element_type=F32).reshape(width, width)

    def scatter_rows(value):
        part = lax.psum_scatter(value.astype(BF16), "dp", scatter_dimension=0, tiled=True)
        return lax.psum_scatter(part, "seq", scatter_dimension=0, tiled=True).astype(F32)

    grad_w_out = scatter_rows(
        jnp.einsum("gte,td->ged", context, grad_branch, preferred_element_type=F32).reshape(width, width)
    )
    grad_w_query = scatter_rows(weight_term(attn_in, dq))
    grad_w_key = scatter_rows(weight_term(mem, dk))
    grad_w_value = scatter_rows(weight_term(mem, dv))

    gains = lax.psum((grad_gain_attn_all, grad_gain_ffn_all), ALL)
    owner = lax.axis_index("dp") * groups + lax.axis_index("seq")
    here = gain_attn.shape[0]
    grad_gain_attn, grad_gain_ffn = [lax.dynamic_slice_in_dim(g, owner * here, here) for g in gains]
    cube = (seqs, piece, width)
    return (
        layer_out.reshape(cube),
        grad_hidden.reshape(cube),
        grad_memory.reshape(cube),
        grad_gain_attn,
        grad_w_query,
        grad_w_key,
        grad_w_value,
        grad_w_out,
        grad_gain_ffn,
        grad_w_gate,
        grad_w_up,
        grad_w_down,
    )


def solution(mesh):
    tokens = P("dp", "seq", None)
    rows = P(ALL, None)
    gain = P(ALL)
    in_specs = (tokens, tokens, P("dp", None), gain, rows, rows, rows, rows, gain, rows, rows, rows, tokens)
    out_specs = (tokens, tokens, tokens, gain, rows, rows, rows, rows, gain, rows, rows, rows)
    return jax.shard_map(shards, mesh=mesh, in_specs=in_specs, out_specs=out_specs, check_vma=False)
```

```python
import functools
import math

import jax
import jax.numpy as jnp
from jax import lax
from jax.experimental import pallas as pl
from jax.experimental.pallas import tpu as pltpu
from jax.sharding import PartitionSpec as P

HEAD_DIM = 128
EPSILON = 1e-06
MASKED = -1e30
ALL = ("dp", "seq")
F32 = jnp.float32
BF16 = jnp.bfloat16
EXP2_SCALE = HEAD_DIM ** (-0.5) * math.log2(math.e)
NT = (((1,), (1,)), ((), ()))
TN = (((0,), (0,)), ((), ()))
NN = (((1,), (0,)), ((), ()))
BY_MESH = pl.DeviceIdType.MESH


def mxu(left, right, dims):
    return lax.dot_general(left, right, dims, preferred_element_type=F32)


def rms_scale(values):
    return lax.rsqrt(jnp.mean(values * values, axis=-1, keepdims=True) + EPSILON)


def norm_back(grad_normed, normed, rstd, gain):
    scaled = grad_normed * gain
    return rstd * (scaled - normed * jnp.mean(scaled * normed, axis=-1, keepdims=True))


def forward_kernel(block, low_ref, start_ref, q_ref, k_ref, v_ref, out_ref, lse_ref):
    length = q_ref.shape[0]

    def one_query_block(qb, _):
        q0 = pl.multiple_of(qb * block, block)
        rows = pl.ds(q0, block)
        query = q_ref[rows, :]
        start = start_ref[:, rows]
        query_pos = q0 + lax.broadcasted_iota(jnp.int32, (block, block), 1)

        def one_key_block(kb, carry):
            top, total, acc = carry
            k0 = pl.multiple_of(kb * block, block)
            keys = pl.ds(k0, block)
            score = mxu(k_ref[keys, :], query, NT)
            key_pos = k0 + lax.broadcasted_iota(jnp.int32, (block, block), 0)
            score = jnp.where((key_pos >= start) & (key_pos <= query_pos), score, MASKED)
            new_top = jnp.maximum(top, jnp.max(score, axis=0, keepdims=True))
            shrink = jnp.exp2((top - new_top) * EXP2_SCALE)
            raised = jnp.exp2((score - new_top) * EXP2_SCALE)
            total = total * shrink + jnp.sum(raised, axis=0, keepdims=True)
            acc = acc * shrink + mxu(v_ref[keys, :], raised.astype(BF16), TN)
            return new_top, total, acc

        top, total, acc = lax.fori_loop(
            low_ref[qb],
            qb + 1,
            one_key_block,
            (
                jnp.full((1, block), MASKED, F32),
                jnp.zeros((1, block), F32),
                jnp.zeros((HEAD_DIM, block), F32),
            ),
        )
        out_ref[rows, :] = (acc / total).T.astype(BF16)
        lse_ref[0, :, rows] = top * EXP2_SCALE + jnp.log2(total)
        return 0

    lax.fori_loop(0, length // block, one_query_block, 0)


def backward_kernel(
    block, high_ref, start_ref, q_ref, k_ref, v_ref, ctx_ref, grad_ref, lse_ref,
    dq_ref, dk_ref, dv_ref, dq_acc, delta_acc,
):
    length = q_ref.shape[0]
    blocks = length // block
    scale = HEAD_DIM ** (-0.5)
    dq_acc[...] = jnp.zeros_like(dq_acc)

    def one_delta(qb, _):
        rows = pl.ds(pl.multiple_of(qb * block, block), block)
        both = ctx_ref[rows, :].astype(F32) * grad_ref[rows, :].astype(F32)
        delta_acc[:, rows] = jnp.sum(both.T, axis=0, keepdims=True)
        return 0

    lax.fori_loop(0, blocks, one_delta, 0)

    def one_key_block(kb, _):
        k0 = pl.multiple_of(kb * block, block)
        keys = pl.ds(k0, block)
        key = k_ref[keys, :]
        value = v_ref[keys, :]
        key_pos = k0 + lax.broadcasted_iota(jnp.int32, (block, block), 0)

        def one_query_block(qb, carry):
            dk, dv = carry
            q0 = pl.multiple_of(qb * block, block)
            rows = pl.ds(q0, block)
            query = q_ref[rows, :]
            grad = grad_ref[rows, :]
            start = start_ref[:, rows]
            query_pos = q0 + lax.broadcasted_iota(jnp.int32, (block, block), 1)
            score = mxu(key, query, NT)
            prob = jnp.exp2(score * EXP2_SCALE - lse_ref[0, :, rows])
            prob = jnp.where((key_pos >= start) & (key_pos <= query_pos), prob, 0.0)
            grad_prob = mxu(value, grad, NT)
            grad_score = (prob * (grad_prob - delta_acc[:, rows])).astype(BF16)
            dv = dv + mxu(prob.astype(BF16), grad, NN)
            dk = dk + mxu(grad_score, query, NN)
            dq_acc[rows, :] += mxu(grad_score, key, TN)
            return dk, dv

        zeros = jnp.zeros((block, HEAD_DIM), F32)
        dk, dv = lax.fori_loop(kb, high_ref[kb], one_query_block, (zeros, zeros))
        dk_ref[keys, :] = (dk * scale).astype(BF16)
        dv_ref[keys, :] = dv.astype(BF16)
        return 0

    lax.fori_loop(0, blocks, one_key_block, 0)
    dq_ref[...] = (dq_acc[...] * scale).astype(BF16)


def attention_calls(length, heads, block):
    column = pl.BlockSpec((length, HEAD_DIM), lambda h, *_: (0, h))
    row = pl.BlockSpec((1, length), lambda h, *_: (0, 0))
    stat = pl.BlockSpec((1, 1, length), lambda h, *_: (h, 0, 0))
    flat = jax.ShapeDtypeStruct((length, heads * HEAD_DIM), BF16)
    pairs = heads * length * length // 4
    forward = pl.pallas_call(
        functools.partial(forward_kernel, block),
        grid_spec=pltpu.PrefetchScalarGridSpec(
            num_scalar_prefetch=1,
            grid=(heads,),
            in_specs=[row, column, column, column],
            out_specs=[column, stat],
        ),
        out_shape=(flat, jax.ShapeDtypeStruct((heads, 1, length), F32)),
        cost_estimate=pl.CostEstimate(
            flops=64 * pairs * HEAD_DIM, transcendentals=pairs, bytes_accessed=8 * length * heads * HEAD_DIM
        ),
        name="attend_forward",
    )
    backward = pl.pallas_call(
        functools.partial(backward_kernel, block),
        grid_spec=pltpu.PrefetchScalarGridSpec(
            num_scalar_prefetch=1,
            grid=(heads,),
            in_specs=[row, column, column, column, column, column, stat],
            out_specs=[column, column, column],
            scratch_shapes=[pltpu.VMEM((length, HEAD_DIM), F32), pltpu.VMEM((1, length), F32)],
        ),
        out_shape=(flat, flat, flat),
        cost_estimate=pl.CostEstimate(
            flops=96 * pairs * HEAD_DIM, transcendentals=pairs, bytes_accessed=16 * length * heads * HEAD_DIM
        ),
        name="attend_backward",
    )
    return forward, backward


def document_bounds(segment_ids, block):
    length = segment_ids.shape[0]
    position = jnp.arange(length, dtype=jnp.int32)
    same = segment_ids[:, None] == segment_ids[None, :]
    first = jnp.min(jnp.where(same, position[None, :], length), axis=1)
    last = jnp.max(jnp.where(same, position[None, :], -1), axis=1)
    low = first[::block] // block
    high = last[block - 1 :: block] // block + 1
    return first[None, :], low, high


def remote(src, dst, send, recv, device):
    return pltpu.make_async_remote_copy(
        src_ref=src, dst_ref=dst, send_sem=send, recv_sem=recv, device_id=device, device_id_type=BY_MESH
    )


class Place:
    def __init__(self, dp_count, groups):
        self.groups = groups
        self.chips = dp_count // 2
        self.dp = lax.axis_index("dp")
        self.seq = lax.axis_index("seq")
        self.core = lax.rem(self.dp, 2)
        self.chip = self.dp // 2
        self.sibling = {"dp": self.dp + 1 - 2 * self.core, "seq": self.seq}

    def chip_at(self, step):
        return lax.rem(self.chip + step, self.chips)

    def chip_device(self, chip):
        return {"dp": 2 * chip + self.core, "seq": self.seq}

    def line_at(self, step):
        return lax.rem(self.seq + step, self.groups)

    def line_device(self, seq):
        return {"dp": self.dp, "seq": seq}

    def barrier(self):
        everyone = pltpu.get_barrier_semaphore()
        for step in range(1, self.groups):
            pl.semaphore_signal(everyone, inc=1, device_id=self.line_device(self.line_at(step)), device_id_type=BY_MESH)
        for step in range(1, self.chips):
            pl.semaphore_signal(everyone, inc=1, device_id=self.chip_device(self.chip_at(step)), device_id_type=BY_MESH)
        pl.semaphore_signal(everyone, inc=1, device_id=self.sibling, device_id_type=BY_MESH)
        pl.semaphore_wait(everyone, self.groups + self.chips - 1)


def project_kernel(
    dp_count, groups, hidden, memory, gains, w_key, w_value, w_query, w_out,
    attn_in, gain_rows, key, value, query, all_gains, all_key, all_value, all_query, all_out,
    weight, parts, line_send, line_recv, chip_send, chip_recv, core_send, core_recv,
    own_sem, load_sem, part_send, part_recv, part_own,
):
    place = Place(dp_count, groups)
    chips, seq = place.chips, place.seq
    shards = (gains, w_key, w_value, w_query, w_out)
    wholes = (all_gains, all_key, all_value, all_query, all_out)
    count = len(shards)
    own = place.dp * groups + seq
    above, below = seq < groups - 1, seq > 0
    up, down = place.line_device(lax.rem(seq + 1, groups)), place.line_device(lax.rem(seq + groups - 1, groups))

    def line(m, dp):
        return wholes[m].at[pl.ds(dp * groups, groups)]

    def along(m, src, block, distance, upward):
        slot = 0 if upward else 1
        return remote(
            src, wholes[m].at[block], line_send.at[m, slot, distance - 1], line_recv.at[m, slot, distance - 1],
            up if upward else down,
        )

    def to_chip(m, src, block, step):
        return remote(
            src, wholes[m].at[block], chip_send.at[m, step - 1], chip_recv.at[m, step - 1],
            place.chip_device(place.chip_at(step)),
        )

    def to_sibling(m, src, dst, step):
        return remote(src, dst, core_send.at[m, step], core_recv.at[m, step], place.sibling)

    def spread(m, src, block):
        for step in range(1, chips):
            to_chip(m, src, block, step).start()
        to_sibling(m, src, wholes[m].at[block], 0).start()

    def own_copy(m):
        return pltpu.make_async_copy(shards[m], wholes[m].at[own], own_sem.at[m])

    def start_own(m):
        own_copy(m).start()

        @pl.when(above)
        def _():
            along(m, shards[m], own, 1, True).start()

        @pl.when(below)
        def _():
            along(m, shards[m], own, 1, False).start()

        spread(m, shards[m], own)

    def serve_line(m):
        for distance in range(1, groups):
            for upward in (True, False):
                block = own - distance if upward else own + distance
                there = seq >= distance if upward else seq < groups - distance
                onward = above if upward else below

                @pl.when(there)
                def _():
                    landed = wholes[m].at[block]
                    along(m, landed, block, distance, upward).wait_recv()

                    @pl.when(onward)
                    def _():
                        along(m, landed, block, distance + 1, upward).start()

                    spread(m, landed, block)

    def serve_chips(m):
        for step in range(1, chips):
            dp = 2 * lax.rem(place.chip + chips - step, chips) + place.core
            remote(
                line(m, dp), line(m, dp), chip_send.at[m, step - 1], chip_recv.at[m, step - 1], place.sibling
            ).wait_recv()
            to_sibling(m, line(m, dp), line(m, dp), step).start()

    def finish(m):
        for step in range(chips):
            dp = 2 * lax.rem(place.chip + chips - step, chips) + 1 - place.core
            to_sibling(m, line(m, dp), line(m, dp), step).wait_recv()
        own_copy(m).wait()

    targets = (None, key, value, query, None)
    lefts = (None, memory, memory, attn_in, None)
    share = weight.shape[2] // groups

    def part_copy(m, step):
        other = place.line_at(step)
        return remote(
            parts.at[m - 1, other], targets[m].at[seq], part_send.at[m - 1, step - 1], part_recv.at[m - 1, step - 1],
            place.line_device(other),
        )

    def own_part(m):
        return pltpu.make_async_copy(parts.at[m - 1, seq], targets[m].at[seq], part_own.at[m - 1])

    def load(m):
        return pltpu.make_async_copy(wholes[m], weight, load_sem)

    def project(m):
        load(m).start()
        load(m).wait()
        rows = weight.shape[0] * weight.shape[1]
        left = lefts[m][...]

        def one(step, _):
            group = place.line_at(step)
            columns = pl.ds(pl.multiple_of(group * share, share), share)
            right = weight[:, :, columns].reshape(rows, share)
            parts[m - 1, group] = jnp.dot(left, right, preferred_element_type=F32).astype(BF16)

            @pl.when(step > 0)
            def _():
                remote(
                    parts.at[m - 1, group], targets[m].at[seq], part_send.at[m - 1, step - 1],
                    part_recv.at[m - 1, step - 1], place.line_device(group),
                ).start()

            return 0

        lax.fori_loop(1, groups, one, 0)
        one(0, 0)
        own_part(m).start()

    def normalize():
        here = 128 // (weight.shape[1])
        tiles = weight.shape[2] // 128
        for tile in range(tiles):
            total = all_gains_v[tile * here]
            for i in range(1, here):
                total = total + pltpu.roll(all_gains_v[tile * here + i], i * weight.shape[1], 1)
            gain_rows[:, tile * 128 : (tile + 1) * 128] = total
        step_rows = 128 if hidden.shape[0] % 128 == 0 else hidden.shape[0]

        def some(i, _):
            rows = pl.ds(pl.multiple_of(i * step_rows, step_rows), step_rows)
            x = hidden[rows, :].astype(F32)
            normed = x * lax.rsqrt(jnp.mean(x * x, axis=-1, keepdims=True) + EPSILON)
            attn_in[rows, :] = (normed * gain_rows[0:1, :]).astype(BF16)
            return 0

        lax.fori_loop(0, hidden.shape[0] // step_rows, some, 0)

    all_gains_v = all_gains
    place.barrier()
    start_own(0)
    start_own(1)
    serve_line(0)
    start_own(2)
    serve_line(1)
    serve_chips(0)
    serve_chips(1)
    start_own(3)
    serve_line(2)
    finish(0)
    normalize()
    finish(1)
    project(1)
    serve_chips(2)
    start_own(4)
    serve_line(3)
    finish(2)
    project(2)
    serve_chips(3)
    serve_line(4)
    finish(3)
    project(3)
    serve_chips(4)
    finish(4)
    for m in range(count):
        for distance in range(1, groups):
            for upward in (True, False):
                came = seq >= distance - 1 if upward else seq < groups - distance + 1
                onward = above if upward else below

                @pl.when(came & onward)
                def _():
                    along(m, wholes[m].at[own], own, distance, upward).wait_send()

        mine = line(m, place.dp)
        for step in range(1, chips):
            remote(
                mine, mine, chip_send.at[m, step - 1], chip_recv.at[m, step - 1], place.sibling
            ).wait_send()
        for step in range(chips):
            to_sibling(m, mine, mine, step).wait_send()
    for m in (1, 2, 3):
        own_part(m).wait()
        for step in range(1, groups):
            part_copy(m, step).wait()


def project_call(dp_count, groups, piece, width, here):
    chips = dp_count // 2
    blocks = dp_count * groups
    share = width // groups
    hbm = pl.BlockSpec(memory_space=pl.ANY)
    vmem = pl.BlockSpec(memory_space=pltpu.VMEM)
    heads = jax.ShapeDtypeStruct((groups, piece, share), BF16)
    whole = jax.ShapeDtypeStruct((blocks, here, width), BF16)
    dma = pltpu.SemaphoreType.DMA
    return pl.pallas_call(
        functools.partial(project_kernel, dp_count, groups),
        in_specs=[vmem, vmem, hbm, hbm, hbm, hbm, hbm],
        out_specs=[vmem, vmem, hbm, hbm, hbm, vmem, hbm, hbm, hbm, hbm],
        out_shape=(
            jax.ShapeDtypeStruct((piece, width), BF16),
            jax.ShapeDtypeStruct((8, width), F32),
            heads, heads, heads,
            jax.ShapeDtypeStruct((blocks, 8, 128), F32),
            whole, whole, whole, whole,
        ),
        scratch_shapes=[
            pltpu.VMEM((blocks, here, width), BF16),
            pltpu.VMEM((3, groups, piece, share), BF16),
            dma((5, 2, groups)), dma((5, 2, groups)),
            dma((5, max(chips - 1, 1))), dma((5, max(chips - 1, 1))),
            dma((5, chips)), dma((5, chips)),
            dma((5,)), dma, dma((3, groups - 1)), dma((3, groups - 1)), dma((3,)),
        ],
        compiler_params=pltpu.CompilerParams(
            collective_id=1, has_side_effects=True, vmem_limit_bytes=48 * 1024 * 1024
        ),
        cost_estimate=pl.CostEstimate(
            flops=128 * piece * width * width, transcendentals=0, bytes_accessed=16 * width * width
        ),
        name="gather_project",
    )


def gain_tile(gain_attn, gain_ffn):
    here = gain_attn.shape[0]
    both = jnp.stack((gain_attn, gain_ffn)).astype(F32)
    return jnp.pad(both, ((0, 6), (0, 128 - here)))


def reduce_kernel(
    dp_count, groups, here, context, memory, attn_in, gain_rows, gain_ffn_term, grad_branch, dv, dk, dq,
    all_value, all_key, all_query, hidden, grad_mid,
    out_v, out_k, out_q, grad_out, grad_value, grad_key, grad_query, grad_memory, grad_hidden, grad_gains,
    right, core_buf, core_in, chip_buf, chip_in, kept, line_buf, line_in, line_own,
    part_send, part_recv, part_own, load_sem, core_send, core_recv, chip_send, chip_recv,
    line_send, line_recv, store_sem, core_free, chip_free,
    weight, panel_out, grad_attn_in, mid_buf, hidden_buf, gain_term, gain_buf, gain_in,
    weight_sem, panel_sem, mid_sem, hidden_sem, gain_send, gain_recv,
):
    place = Place(dp_count, groups)
    chips, seq = place.chips, place.seq
    panel = groups * here
    share = right.shape[3]
    lefts = (context, memory, memory, attn_in)
    parts = (None, dv, dk, dq)
    wholes = (None, out_v, out_k, out_q)
    grads = (grad_out, grad_value, grad_key, grad_query)
    count = 4

    def part_copy(m, step):
        other = place.line_at(step)
        return remote(
            parts[m].at[other], wholes[m].at[seq], part_send.at[m, step - 1], part_recv.at[m, step - 1],
            place.line_device(other),
        )

    def own_part(m):
        return pltpu.make_async_copy(parts[m].at[seq], wholes[m].at[seq], part_own.at[m])

    def send_parts(m):
        own_part(m).start()
        for step in range(1, groups):
            part_copy(m, step).start()

    def sent_parts(m):
        for step in range(1, groups):
            part_copy(m, step).wait_send()

    def load_copy(m, group):
        source = grad_branch.at[:, pl.ds(group * share, share)] if m == 0 else wholes[m].at[group]
        return pltpu.make_async_copy(source, right.at[m % 2, group], load_sem.at[group])

    def load_right(m):
        if m > 0:
            own_part(m).wait()
            for step in range(1, groups):
                part_copy(m, step).wait_recv()
        for group in range(groups):
            load_copy(m, group).start()
        for group in range(groups):
            load_copy(m, group).wait()

    def product(m, dp, store):
        rows = pl.ds(pl.multiple_of(dp * panel, panel), panel)
        left = lefts[m][:, rows].T

        def one(group, _):
            columns = pl.ds(pl.multiple_of(group * share, share), share)
            store(columns, jnp.dot(left, right[m % 2, group], preferred_element_type=F32))
            return 0

        lax.fori_loop(0, groups, one, 0)

    def core_copy(m, step):
        return remote(
            core_buf.at[step], core_in.at[m % 2, step], core_send.at[step], core_recv.at[m % 2, step], place.sibling
        )

    def chip_copy(m, step):
        return remote(
            chip_buf.at[m % 2, step - 1], chip_in.at[m % 2, step - 1], chip_send.at[m % 2, step - 1],
            chip_recv.at[m % 2, step - 1], place.chip_device(place.chip_at(step)),
        )

    def line_copy(m, step):
        return remote(
            line_buf.at[m, step - 1], line_in.at[m, step - 1], line_send.at[m, step - 1], line_recv.at[m, step - 1],
            place.line_device(place.line_at(step)),
        )

    order = tuple(range(1, chips)) + (0,)

    def to_sibling(m):
        if m >= 2:
            pl.semaphore_wait(core_free, 1)
        for step in order:
            if m >= 1:
                core_copy(m - 1, step).wait_send()
            dp = 2 * place.chip_at(step) + 1 - place.core

            def store(columns, value, step=step):
                core_buf[step, :, columns] = value.astype(BF16)

            product(m, dp, store)
            core_copy(m, step).start()

    def to_chips(m):
        for step in order:
            dp = 2 * place.chip_at(step) + place.core
            core_copy(m, step).wait_recv()
            if step > 0:
                if m >= 2:
                    chip_copy(m - 2, step).wait_send()
                    pl.semaphore_wait(chip_free.at[step - 1], 1)

                def store(columns, value, step=step):
                    total = value + core_in[m % 2, step, :, columns].astype(F32)
                    chip_buf[m % 2, step - 1, :, columns] = total.astype(BF16)

            else:

                def store(columns, value):
                    kept[m % 2, :, columns] = value + core_in[m % 2, 0, :, columns].astype(F32)

            product(m, dp, store)
            if step > 0:
                chip_copy(m, step).start()
        if m + 2 < count:
            pl.semaphore_signal(core_free, inc=1, device_id=place.sibling, device_id_type=BY_MESH)

    def to_line(m):
        for step in range(1, chips):
            chip_copy(m, step).wait_recv()
        for step in tuple(range(1, groups)) + (0,):
            block = place.line_at(step)
            rows = pl.ds(pl.multiple_of(block * here, here), here)
            total = kept[m % 2, rows, :]
            for other in range(1, chips):
                total = total + chip_in[m % 2, other - 1, rows, :].astype(F32)
            if step > 0:
                line_buf[m, step - 1] = total.astype(BF16)
                line_copy(m, step).start()
            else:
                line_own[m] = total
        if m + 2 < count:
            for step in range(1, chips):
                behind = lax.rem(place.chip + chips - step, chips)
                pl.semaphore_signal(
                    chip_free.at[step - 1], inc=1, device_id=place.chip_device(behind), device_id_type=BY_MESH
                )

    def store_grad(m):
        return pltpu.make_async_copy(line_own.at[m], grads[m], store_sem.at[m])

    def settle(m):
        total = line_own[m]
        for step in range(1, groups):
            line_copy(m, step).wait_recv()
            total = total + line_in[m, step - 1].astype(F32)
        line_own[m] = total
        store_grad(m).start()

    width = memory.shape[1]
    panels = width // panel
    piece = memory.shape[0]

    def weight_copy(slot, which, source, index):
        rows = pl.ds(pl.multiple_of(index * panel, panel), panel)
        return pltpu.make_async_copy(source.at[rows, :], weight.at[slot, which], weight_sem.at[slot, which])

    def panel_copy(slot, index):
        columns = pl.ds(pl.multiple_of(index * panel, panel), panel)
        return pltpu.make_async_copy(panel_out.at[slot], grad_memory.at[:, columns], panel_sem.at[slot])

    def back(slot, which, m):
        total = jnp.zeros((piece, panel), F32)
        for group in range(groups):
            columns = slice(group * share, (group + 1) * share)
            total = total + lax.dot_general(
                right[m % 2, group], weight[slot, which, :, columns], NT, preferred_element_type=F32
            )
        return total

    def memory_gradient():
        weight_copy(0, 0, all_value, 0).start()
        weight_copy(0, 1, all_key, 0).start()

        def one(index, _):
            slot = lax.rem(index, 2)

            @pl.when(index + 1 < panels)
            def _():
                weight_copy(1 - slot, 0, all_value, index + 1).start()
                weight_copy(1 - slot, 1, all_key, index + 1).start()

            weight_copy(slot, 0, all_value, index).wait()
            weight_copy(slot, 1, all_key, index).wait()

            @pl.when(index >= 2)
            def _():
                panel_copy(slot, index - 2).wait()

            panel_out[slot] = back(slot, 0, 1) + back(slot, 1, 2)
            panel_copy(slot, index).start()
            return 0

        lax.fori_loop(0, panels, one, 0)
        for index in range(max(panels - 2, 0), panels):
            panel_copy(index % 2, index).wait()

    def query_gradient():
        weight_copy(0, 0, all_query, 0).start()

        def one(index, _):
            slot = lax.rem(index, 2)

            @pl.when(index + 1 < panels)
            def _():
                weight_copy(1 - slot, 0, all_query, index + 1).start()

            weight_copy(slot, 0, all_query, index).wait()
            columns = pl.ds(pl.multiple_of(index * panel, panel), panel)
            grad_attn_in[:, columns] = back(slot, 0, 3)
            return 0

        lax.fori_loop(0, panels, one, 0)

    some = mid_buf.shape[1]
    batches = piece // some

    def batch_rows(index):
        return pl.ds(pl.multiple_of(index * some, some), some)

    def mid_copy(slot, index):
        return pltpu.make_async_copy(grad_mid.at[batch_rows(index), :], mid_buf.at[slot], mid_sem.at[slot])

    def hidden_copy(slot, index):
        return pltpu.make_async_copy(hidden.at[batch_rows(index), :], hidden_buf.at[slot], hidden_sem.at[slot])

    def hidden_store(index):
        rows = batch_rows(index)
        return pltpu.make_async_copy(grad_attn_in.at[rows, :], grad_hidden.at[rows, :], panel_sem.at[0])

    def hidden_gradient():
        gain_term[...] = jnp.zeros_like(gain_term)
        mid_copy(0, 0).start()
        hidden_copy(0, 0).start()

        def one(index, _):
            slot = lax.rem(index, 2)

            @pl.when(index + 1 < batches)
            def _():
                mid_copy(1 - slot, index + 1).start()
                hidden_copy(1 - slot, index + 1).start()

            mid_copy(slot, index).wait()
            hidden_copy(slot, index).wait()
            rows = batch_rows(index)
            x = hidden_buf[slot].astype(F32)
            rstd = lax.rsqrt(jnp.mean(x * x, axis=-1, keepdims=True) + EPSILON)
            normed = x * rstd
            grad = grad_attn_in[rows, :]
            gain_term[0:1, :] += jnp.sum(normed * grad, axis=0, keepdims=True)
            scaled = grad * gain_rows[0:1, :]
            shift = jnp.mean(scaled * normed, axis=-1, keepdims=True)
            grad_attn_in[rows, :] = mid_buf[slot] + rstd * (scaled - normed * shift)
            hidden_store(index).start()
            return 0

        lax.fori_loop(0, batches, one, 0)

    devices = dp_count * groups
    me = place.dp * groups + seq

    def gain_copy(step):
        owner = lax.rem(me + step, devices)
        return remote(
            gain_buf.at[owner], gain_in.at[step], gain_send, gain_recv, {"dp": owner // groups, "seq": owner % groups}
        )

    def send_gains():
        gain_term[1:2, :] = gain_ffn_term[0:1, :]
        per = 128 // here
        for owner in range(devices):
            tile = gain_term[:, owner // per * 128 : (owner // per + 1) * 128]
            shift = owner % per * here
            gain_buf[owner] = pltpu.roll(tile, 128 - shift, 1) if shift else tile

        def one(step, _):
            gain_copy(step).start()
            return 0

        lax.fori_loop(1, devices, one, 0)

    def sum_gains():
        remote(
            gain_buf.at[pl.ds(0, devices - 1)], gain_in.at[pl.ds(1, devices - 1)], gain_send, gain_recv, place.sibling
        ).wait()
        total = gain_buf[me]
        for step in range(1, devices):
            total = total + gain_in[step]
        grad_gains[...] = total

    everyone = pltpu.get_barrier_semaphore()

    def greet(step, _):
        other = lax.rem(me + step, devices)
        pl.semaphore_signal(
            everyone, inc=1, device_id={"dp": other // groups, "seq": other % groups}, device_id_type=BY_MESH
        )
        return 0

    lax.fori_loop(1, devices, greet, 0)
    pl.semaphore_wait(everyone, devices - 1)
    send_parts(1)
    load_right(0)
    to_sibling(0)
    to_chips(0)
    sent_parts(1)
    send_parts(2)
    load_right(1)
    to_sibling(1)
    to_chips(1)
    to_line(0)
    sent_parts(2)
    send_parts(3)
    load_right(2)
    to_sibling(2)
    to_chips(2)
    to_line(1)
    settle(0)
    memory_gradient()
    sent_parts(3)
    load_right(3)
    to_sibling(3)
    to_chips(3)
    to_line(2)
    settle(1)
    query_gradient()
    hidden_gradient()
    send_gains()
    to_line(3)
    settle(2)
    settle(3)
    sum_gains()
    pltpu.make_async_copy(grad_attn_in, grad_hidden, panel_sem.at[0]).wait()
    for step in range(chips):
        core_copy(3, step).wait_send()
    for m in (2, 3):
        for step in range(1, chips):
            chip_copy(m, step).wait_send()
    for m in range(count):
        for step in range(1, groups):
            line_copy(m, step).wait_send()
        store_grad(m).wait()


def reduce_call(dp_count, groups, piece, width, here):
    chips = dp_count // 2
    share = width // groups
    panel = groups * here
    hbm = pl.BlockSpec(memory_space=pl.ANY)
    vmem = pl.BlockSpec(memory_space=pltpu.VMEM)
    part = jax.ShapeDtypeStruct((groups, piece, share), BF16)
    grad = jax.ShapeDtypeStruct((here, width), F32)
    tokens = jax.ShapeDtypeStruct((piece, width), F32)
    some = min(64, piece)
    devices = dp_count * groups
    dma = pltpu.SemaphoreType.DMA
    others = max(chips - 1, 1)
    return pl.pallas_call(
        functools.partial(reduce_kernel, dp_count, groups, here),
        in_specs=[vmem] * 5 + [hbm] * 9,
        out_specs=[hbm] * 9 + [vmem],
        out_shape=(part, part, part, grad, grad, grad, grad, tokens, tokens, jax.ShapeDtypeStruct((8, 128), F32)),
        scratch_shapes=[
            pltpu.VMEM((2, groups, piece, share), BF16),
            pltpu.VMEM((chips, panel, width), BF16),
            pltpu.VMEM((2, chips, panel, width), BF16),
            pltpu.VMEM((2, others, panel, width), BF16),
            pltpu.VMEM((2, others, panel, width), BF16),
            pltpu.VMEM((2, panel, width), F32),
            pltpu.VMEM((4, groups - 1, here, width), BF16),
            pltpu.VMEM((4, groups - 1, here, width), BF16),
            pltpu.VMEM((4, here, width), F32),
            dma((4, groups - 1)), dma((4, groups - 1)), dma((4,)), dma((groups,)),
            dma((chips,)), dma((2, chips)),
            dma((2, others)), dma((2, others)),
            dma((4, groups - 1)), dma((4, groups - 1)), dma((4,)),
            pltpu.SemaphoreType.REGULAR, pltpu.SemaphoreType.REGULAR((others,)),
            pltpu.VMEM((2, 2, panel, width), BF16),
            pltpu.VMEM((2, piece, panel), F32),
            pltpu.VMEM((piece, width), F32),
            pltpu.VMEM((2, some, width), F32),
            pltpu.VMEM((2, some, width), BF16),
            pltpu.VMEM((8, width), F32),
            pltpu.VMEM((devices, 8, 128), F32),
            pltpu.VMEM((devices, 8, 128), F32),
            dma((2, 2)), dma((2,)), dma((2,)), dma((2,)), dma, dma,
        ],
        compiler_params=pltpu.CompilerParams(
            collective_id=2, has_side_effects=True, vmem_limit_bytes=63 * 1024 * 1024
        ),
        cost_estimate=pl.CostEstimate(
            flops=128 * piece * width * width, transcendentals=0, bytes_accessed=16 * width * width
        ),
        name="weight_gradients",
    )


def exchange_kernel(dp_count, groups, spread, source, target, send_sem, recv_sem, own_sem):
    place = Place(dp_count, groups)
    share = source.shape[1] // groups if spread else source.shape[2]
    everyone = pltpu.get_barrier_semaphore()
    for step in range(1, groups):
        pl.semaphore_signal(
            everyone, inc=1, device_id=place.line_device(place.line_at(step)), device_id_type=BY_MESH
        )
    pl.semaphore_wait(everyone, groups - 1)

    def columns(group):
        return pl.ds(pl.multiple_of(group * share, share), share)

    def ends(other):
        if spread:
            return source.at[:, columns(other)], target.at[place.seq]
        return source.at[other], target.at[:, columns(place.seq)]

    def copy(step):
        other = place.line_at(step)
        src, dst = ends(other)
        return remote(src, dst, send_sem.at[step - 1], recv_sem.at[step - 1], place.line_device(other))

    own = pltpu.make_async_copy(*ends(place.seq), own_sem)
    for step in range(1, groups):
        copy(step).start()
    own.start()
    own.wait()
    for step in range(1, groups):
        copy(step).wait()


def exchange_call(dp_count, groups, piece, width, spread):
    share = width // groups
    hbm = pl.BlockSpec(memory_space=pl.ANY)
    dma = pltpu.SemaphoreType.DMA
    shape = (groups, piece, share) if spread else (piece, width)
    return pl.pallas_call(
        functools.partial(exchange_kernel, dp_count, groups, spread),
        in_specs=[hbm],
        out_specs=hbm,
        out_shape=jax.ShapeDtypeStruct(shape, BF16),
        scratch_shapes=[dma((groups - 1,)), dma((groups - 1,)), dma],
        compiler_params=pltpu.CompilerParams(collective_id=3 + spread, has_side_effects=True),
        cost_estimate=pl.CostEstimate(flops=32 * piece * width * width // 8, transcendentals=0, bytes_accessed=4 * piece * width),
        name="spread_features" if spread else "collect_features",
    )


def shards(
    hidden_in, memory, segments, gain_attn, w_query, w_key, w_value, w_out, gain_ffn, w_gate, w_up, w_down, cotangent
):
    seqs, piece, width = hidden_in.shape
    groups = lax.axis_size("seq")
    dp_count = lax.axis_size("dp")
    assert seqs == 1
    length = piece * groups
    share = width // groups
    heads = share // HEAD_DIM
    here = w_query.shape[0]
    block = min(512, length)
    chunks = 2
    tokens = hidden_in.reshape(piece, width)
    mem = memory.reshape(piece, width)
    grad_out = cotangent.reshape(piece, width)

    def gather_dp(value):
        return lax.all_gather(value, "dp", axis=0, tiled=True)

    def pieces(value):
        return [value[i * piece // chunks : (i + 1) * piece // chunks] for i in range(chunks)]

    attend_forward, attend_backward = attention_calls(length, heads, block)
    start, low, high = document_bounds(segments[0], block)
    flat = (length, share)
    split = (groups, piece, share)

    attn_in, gain_rows, key, value, query, _, key_rows, value_rows, query_rows, out_rows = project_call(
        dp_count, groups, piece, width, here
    )(tokens, mem, gain_tile(gain_attn, gain_ffn), w_key, w_value, w_query, w_out)
    gain_attn32, gain_ffn32 = gain_rows[0], gain_rows[1]
    key, value, query = [part.reshape(flat) for part in (key, value, query)]
    key_rows, value_rows, query_rows, out_rows = [
        rows.reshape(width, width) for rows in (key_rows, value_rows, query_rows, out_rows)
    ]

    units = w_gate.shape[0]
    padded = -(-units // 16) * 16

    units_here = jnp.pad(jnp.stack((w_gate, w_up, w_down)), ((0, 0), (0, padded - units), (0, 0)))
    units_all = lax.all_gather(units_here, "seq", axis=0, tiled=False)
    gate_rows, up_rows, down_rows = [units_all[:, i].reshape(groups * padded, width) for i in range(3)]
    dy = [gather_dp(part) for part in pieces(grad_out)]

    context_heads, lse = attend_forward(low, start, query, key, value)
    context = exchange_call(dp_count, groups, piece, width, False)(context_heads.reshape(split))

    hidden32 = tokens.astype(F32)
    mid = hidden32 + mxu(context, out_rows, NN)
    rstd_mid = rms_scale(mid)
    normed_mid = mid * rstd_mid
    ffn_in = (normed_mid * gain_ffn32).astype(BF16)

    def scatter_dp(value):
        return lax.psum_scatter(value, "dp", scatter_dimension=0, tiled=True)

    ffn_all = [gather_dp(part) for part in pieces(ffn_in)]
    acts, grad_gates, grad_ups, scattered = [], [], [], []
    for part, dy_part in zip(ffn_all, dy):
        gate = mxu(part, gate_rows, NT)
        up = mxu(part, up_rows, NT)
        sig = jax.nn.sigmoid(gate)
        acts.append((gate * sig * up).astype(BF16))
        grad_act = mxu(dy_part, down_rows, NT)
        grad_gates.append((grad_act * up * sig * (1.0 + gate * (1.0 - sig))).astype(BF16))
        grad_ups.append((grad_act * gate * sig).astype(BF16))
        scattered.append(
            scatter_dp((mxu(grad_gates[-1], gate_rows, NN) + mxu(grad_ups[-1], up_rows, NN)).astype(BF16))
        )

    first, acts, grad_gates, grad_ups = lax.optimization_barrier((scattered[0], acts, grad_gates, grad_ups))

    def unit_terms(lefts, rights):
        return sum(mxu(left, right, TN) for left, right in zip(lefts, rights)).astype(BF16)

    terms = [unit_terms(acts, dy), unit_terms(grad_gates, ffn_all), unit_terms(grad_ups, ffn_all)]
    branches = [mxu(act, down_rows, NN).astype(BF16) for act in acts]
    second, terms, branches = lax.optimization_barrier((scattered[1], terms, branches))
    grad_ffn_in = jnp.concatenate((first, second)).astype(F32)
    terms = [lax.psum_scatter(term, "seq", scatter_dimension=0, tiled=True) for term in terms]
    branches = [scatter_dp(part) for part in branches]

    grad_gain_ffn_all = jnp.sum(normed_mid * grad_ffn_in, axis=0)
    grad_mid = grad_out.astype(F32) + norm_back(grad_ffn_in, normed_mid, rstd_mid, gain_ffn32)
    grad_branch = grad_mid.astype(BF16)
    grad_context = mxu(grad_branch, out_rows, NT).astype(BF16)
    grad_context_heads = exchange_call(dp_count, groups, piece, width, True)(grad_context).reshape(flat)
    dq, dk, dv = attend_backward(high, start, query, key, value, context_heads, grad_context_heads, lse)

    gain_term = jnp.pad(grad_gain_ffn_all[None], ((0, 7), (0, 0)))
    _, _, _, grad_w_out, grad_w_value, grad_w_key, grad_w_query, grad_memory, grad_hidden, gains = reduce_call(
        dp_count, groups, piece, width, here
    )(
        context, mem, attn_in, gain_rows, gain_term, grad_branch, dv.reshape(split), dk.reshape(split),
        dq.reshape(split), value_rows, key_rows, query_rows, tokens, grad_mid,
    )
    gains, terms, branches, mid = lax.optimization_barrier((gains, terms, branches, mid))
    grad_w_down, grad_w_gate, grad_w_up = [term[:units].astype(F32) for term in terms]
    layer_out = (mid + jnp.concatenate(branches).astype(F32)).astype(BF16)
    grad_gain_attn, grad_gain_ffn = gains[0, :here], gains[1, :here]
    cube = (seqs, piece, width)
    return (
        layer_out.reshape(cube),
        grad_hidden.reshape(cube),
        grad_memory.reshape(cube),
        grad_gain_attn,
        grad_w_query,
        grad_w_key,
        grad_w_value,
        grad_w_out,
        grad_gain_ffn,
        grad_w_gate,
        grad_w_up,
        grad_w_down,
    )


def solution(mesh):
    tokens = P("dp", "seq", None)
    rows = P(ALL, None)
    gain = P(ALL)
    in_specs = (tokens, tokens, P("dp", None), gain, rows, rows, rows, rows, gain, rows, rows, rows, tokens)
    out_specs = (tokens, tokens, tokens, gain, rows, rows, rows, rows, gain, rows, rows, rows)
    return jax.shard_map(shards, mesh=mesh, in_specs=in_specs, out_specs=out_specs, check_vma=False)
```

```python
import functools
import math

import jax
import jax.numpy as jnp
from jax import lax
from jax.experimental import pallas as pl
from jax.experimental.pallas import tpu as pltpu
from jax.sharding import PartitionSpec as P

HEAD_DIM = 128
EPSILON = 1e-06
MASKED = -1e30
ALL = ("dp", "seq")
F32 = jnp.float32
BF16 = jnp.bfloat16
EXP2_SCALE = HEAD_DIM ** (-0.5) * math.log2(math.e)
NT = (((1,), (1,)), ((), ()))
TN = (((0,), (0,)), ((), ()))
NN = (((1,), (0,)), ((), ()))
BY_MESH = pl.DeviceIdType.MESH


def mxu(left, right, dims):
    return lax.dot_general(left, right, dims, preferred_element_type=F32)


def rms_scale(values):
    return lax.rsqrt(jnp.mean(values * values, axis=-1, keepdims=True) + EPSILON)


def norm_back(grad_normed, normed, rstd, gain):
    scaled = grad_normed * gain
    return rstd * (scaled - normed * jnp.mean(scaled * normed, axis=-1, keepdims=True))


def forward_kernel(block, low_ref, start_ref, q_ref, k_ref, v_ref, out_ref, lse_ref):
    length = q_ref.shape[0]

    def one_query_block(qb, _):
        q0 = pl.multiple_of(qb * block, block)
        rows = pl.ds(q0, block)
        query = q_ref[rows, :]
        start = start_ref[:, rows]
        query_pos = q0 + lax.broadcasted_iota(jnp.int32, (block, block), 1)

        def one_key_block(kb, carry):
            top, total, acc = carry
            k0 = pl.multiple_of(kb * block, block)
            keys = pl.ds(k0, block)
            score = mxu(k_ref[keys, :], query, NT)
            key_pos = k0 + lax.broadcasted_iota(jnp.int32, (block, block), 0)
            score = jnp.where((key_pos >= start) & (key_pos <= query_pos), score, MASKED)
            new_top = jnp.maximum(top, jnp.max(score, axis=0, keepdims=True))
            shrink = jnp.exp2((top - new_top) * EXP2_SCALE)
            raised = jnp.exp2((score - new_top) * EXP2_SCALE)
            total = total * shrink + jnp.sum(raised, axis=0, keepdims=True)
            acc = acc * shrink + mxu(v_ref[keys, :], raised.astype(BF16), TN)
            return new_top, total, acc

        top, total, acc = lax.fori_loop(
            low_ref[qb],
            qb + 1,
            one_key_block,
            (
                jnp.full((1, block), MASKED, F32),
                jnp.zeros((1, block), F32),
                jnp.zeros((HEAD_DIM, block), F32),
            ),
        )
        out_ref[rows, :] = (acc / total).T.astype(BF16)
        lse_ref[0, :, rows] = top * EXP2_SCALE + jnp.log2(total)
        return 0

    lax.fori_loop(0, length // block, one_query_block, 0)


def backward_kernel(
    block, high_ref, start_ref, q_ref, k_ref, v_ref, ctx_ref, grad_ref, lse_ref,
    dq_ref, dk_ref, dv_ref, dq_acc, delta_acc,
):
    length = q_ref.shape[0]
    blocks = length // block
    scale = HEAD_DIM ** (-0.5)
    dq_acc[...] = jnp.zeros_like(dq_acc)

    def one_delta(qb, _):
        rows = pl.ds(pl.multiple_of(qb * block, block), block)
        both = ctx_ref[rows, :].astype(F32) * grad_ref[rows, :].astype(F32)
        delta_acc[:, rows] = jnp.sum(both.T, axis=0, keepdims=True)
        return 0

    lax.fori_loop(0, blocks, one_delta, 0)

    def one_key_block(kb, _):
        k0 = pl.multiple_of(kb * block, block)
        keys = pl.ds(k0, block)
        key = k_ref[keys, :]
        value = v_ref[keys, :]
        key_pos = k0 + lax.broadcasted_iota(jnp.int32, (block, block), 0)

        def one_query_block(qb, carry):
            dk, dv = carry
            q0 = pl.multiple_of(qb * block, block)
            rows = pl.ds(q0, block)
            query = q_ref[rows, :]
            grad = grad_ref[rows, :]
            start = start_ref[:, rows]
            query_pos = q0 + lax.broadcasted_iota(jnp.int32, (block, block), 1)
            score = mxu(key, query, NT)
            prob = jnp.exp2(score * EXP2_SCALE - lse_ref[0, :, rows])
            prob = jnp.where((key_pos >= start) & (key_pos <= query_pos), prob, 0.0)
            grad_prob = mxu(value, grad, NT)
            grad_score = (prob * (grad_prob - delta_acc[:, rows])).astype(BF16)
            dv = dv + mxu(prob.astype(BF16), grad, NN)
            dk = dk + mxu(grad_score, query, NN)
            dq_acc[rows, :] += mxu(grad_score, key, TN)
            return dk, dv

        zeros = jnp.zeros((block, HEAD_DIM), F32)
        dk, dv = lax.fori_loop(kb, high_ref[kb], one_query_block, (zeros, zeros))
        dk_ref[keys, :] = (dk * scale).astype(BF16)
        dv_ref[keys, :] = dv.astype(BF16)
        return 0

    lax.fori_loop(0, blocks, one_key_block, 0)
    dq_ref[...] = (dq_acc[...] * scale).astype(BF16)


def attention_calls(length, heads, block):
    column = pl.BlockSpec((length, HEAD_DIM), lambda h, *_: (0, h))
    row = pl.BlockSpec((1, length), lambda h, *_: (0, 0))
    stat = pl.BlockSpec((1, 1, length), lambda h, *_: (h, 0, 0))
    flat = jax.ShapeDtypeStruct((length, heads * HEAD_DIM), BF16)
    pairs = heads * length * length // 4
    forward = pl.pallas_call(
        functools.partial(forward_kernel, block),
        grid_spec=pltpu.PrefetchScalarGridSpec(
            num_scalar_prefetch=1,
            grid=(heads,),
            in_specs=[row, column, column, column],
            out_specs=[column, stat],
        ),
        out_shape=(flat, jax.ShapeDtypeStruct((heads, 1, length), F32)),
        cost_estimate=pl.CostEstimate(
            flops=64 * pairs * HEAD_DIM, transcendentals=pairs, bytes_accessed=8 * length * heads * HEAD_DIM
        ),
        name="attend_forward",
    )
    backward = pl.pallas_call(
        functools.partial(backward_kernel, block),
        grid_spec=pltpu.PrefetchScalarGridSpec(
            num_scalar_prefetch=1,
            grid=(heads,),
            in_specs=[row, column, column, column, column, column, stat],
            out_specs=[column, column, column],
            scratch_shapes=[pltpu.VMEM((length, HEAD_DIM), F32), pltpu.VMEM((1, length), F32)],
        ),
        out_shape=(flat, flat, flat),
        cost_estimate=pl.CostEstimate(
            flops=96 * pairs * HEAD_DIM, transcendentals=pairs, bytes_accessed=16 * length * heads * HEAD_DIM
        ),
        name="attend_backward",
    )
    return forward, backward


def document_bounds(segment_ids, block):
    length = segment_ids.shape[0]
    position = jnp.arange(length, dtype=jnp.int32)
    same = segment_ids[:, None] == segment_ids[None, :]
    first = jnp.min(jnp.where(same, position[None, :], length), axis=1)
    last = jnp.max(jnp.where(same, position[None, :], -1), axis=1)
    low = first[::block] // block
    high = last[block - 1 :: block] // block + 1
    return first[None, :], low, high


def remote(src, dst, send, recv, device):
    return pltpu.make_async_remote_copy(
        src_ref=src, dst_ref=dst, send_sem=send, recv_sem=recv, device_id=device, device_id_type=BY_MESH
    )


class Place:
    def __init__(self, dp_count, groups):
        self.groups = groups
        self.chips = dp_count // 2
        self.dp = lax.axis_index("dp")
        self.seq = lax.axis_index("seq")
        self.core = lax.rem(self.dp, 2)
        self.chip = self.dp // 2
        self.sibling = {"dp": self.dp + 1 - 2 * self.core, "seq": self.seq}

    def chip_at(self, step):
        chip, bit = self.chip, 1
        while bit < self.chips:
            chip = chip + (step // bit % 2) * bit * (1 - 2 * lax.rem(self.chip // bit, 2))
            bit *= 2
        return chip

    def chip_device(self, chip):
        return {"dp": 2 * chip + self.core, "seq": self.seq}

    def line_at(self, step):
        return lax.rem(self.seq + step, self.groups)

    def line_device(self, seq):
        return {"dp": self.dp, "seq": seq}

    def barrier(self):
        everyone = pltpu.get_barrier_semaphore()
        for step in range(1, self.groups):
            pl.semaphore_signal(everyone, inc=1, device_id=self.line_device(self.line_at(step)), device_id_type=BY_MESH)
        for step in range(1, self.chips):
            pl.semaphore_signal(everyone, inc=1, device_id=self.chip_device(self.chip_at(step)), device_id_type=BY_MESH)
        pl.semaphore_signal(everyone, inc=1, device_id=self.sibling, device_id_type=BY_MESH)
        pl.semaphore_wait(everyone, self.groups + self.chips - 1)


def project_kernel(
    dp_count, groups, hidden, memory, gains, w_key, w_value, w_query, w_out, w_gate, w_up, w_down, grad,
    attn_in, gain_rows, key, value, query, all_gains, all_key, all_value, all_query, all_out,
    all_gate, all_up, all_down, all_grad,
    weight, parts, line_send, line_recv, chip_send, chip_recv, core_send, core_recv,
    own_sem, load_sem, part_send, part_recv, part_own,
    dy_own, dy_chip_send, dy_chip_recv, dy_core_send, dy_core_recv,
):
    place = Place(dp_count, groups)
    chips, seq = place.chips, place.seq
    shards = (gains, w_key, w_value, w_query, w_out, w_gate, w_up, w_down)
    wholes = (all_gains, all_key, all_value, all_query, all_out, all_gate, all_up, all_down)
    count = 5
    whole_own = place.dp * groups + seq

    def own_block(m):
        return whole_own if m < count else seq

    above, below = seq < groups - 1, seq > 0
    up, down = place.line_device(lax.rem(seq + 1, groups)), place.line_device(lax.rem(seq + groups - 1, groups))

    def line(m, dp):
        return wholes[m].at[pl.ds(dp * groups, groups)]

    def along(m, src, block, distance, upward):
        slot = 0 if upward else 1
        return remote(
            src, wholes[m].at[block], line_send.at[m, slot, distance - 1], line_recv.at[m, slot, distance - 1],
            up if upward else down,
        )

    def to_chip(m, src, block, step):
        return remote(
            src, wholes[m].at[block], chip_send.at[m, step - 1], chip_recv.at[m, step - 1],
            place.chip_device(place.chip_at(step)),
        )

    def to_sibling(m, src, dst, step):
        return remote(src, dst, core_send.at[m, step], core_recv.at[m, step], place.sibling)

    def spread(m, src, block):
        for step in range(1, chips):
            to_chip(m, src, block, step).start()
        to_sibling(m, src, wholes[m].at[block], 0).start()

    def own_copy(m):
        return pltpu.make_async_copy(shards[m], wholes[m].at[own_block(m)], own_sem.at[m])

    def start_own(m):
        own = own_block(m)
        own_copy(m).start()

        @pl.when(above)
        def _():
            along(m, shards[m], own, 1, True).start()

        @pl.when(below)
        def _():
            along(m, shards[m], own, 1, False).start()

        if m < count:
            spread(m, shards[m], own)

    def serve_line(m):
        for distance in range(1, groups):
            for upward in (True, False):
                block = own_block(m) - distance if upward else own_block(m) + distance
                there = seq >= distance if upward else seq < groups - distance
                onward = above if upward else below

                @pl.when(there)
                def _():
                    landed = wholes[m].at[block]
                    along(m, landed, block, distance, upward).wait_recv()

                    @pl.when(onward)
                    def _():
                        along(m, landed, block, distance + 1, upward).start()

                    if m < count:
                        spread(m, landed, block)

    chunks = all_grad.shape[0]
    chunk_rows = grad.shape[0] // chunks

    def grad_rows(chunk):
        return grad.at[pl.ds(chunk * chunk_rows, chunk_rows), :]

    def grad_own(chunk):
        return pltpu.make_async_copy(grad_rows(chunk), all_grad.at[chunk, place.dp], dy_own.at[chunk])

    def grad_to_chip(chunk, step):
        return remote(
            grad_rows(chunk), all_grad.at[chunk, place.dp], dy_chip_send.at[chunk, step - 1],
            dy_chip_recv.at[chunk, step - 1], place.chip_device(place.chip_at(step)),
        )

    def grad_to_sibling(chunk, step):
        dp = 2 * place.chip_at(step) + place.core
        src = all_grad.at[chunk, dp] if step > 0 else grad_rows(chunk)
        return remote(
            src, all_grad.at[chunk, dp], dy_core_send.at[chunk, step], dy_core_recv.at[chunk, step], place.sibling
        )

    def start_grad(chunk):
        grad_own(chunk).start()
        for step in range(1, chips):
            grad_to_chip(chunk, step).start()
        grad_to_sibling(chunk, 0).start()

    def serve_grad(chunk):
        for step in range(1, chips):
            grad_to_chip(chunk, step).wait_recv()
            grad_to_sibling(chunk, step).start()

    def finish_grad(chunk):
        grad_own(chunk).wait()
        for step in range(1, chips):
            grad_to_chip(chunk, step).wait_send()
        for step in range(chips):
            grad_to_sibling(chunk, step).wait()

    def serve_chips(m):
        for step in range(1, chips):
            dp = 2 * place.chip_at(step) + place.core
            remote(
                line(m, dp), line(m, dp), chip_send.at[m, step - 1], chip_recv.at[m, step - 1], place.sibling
            ).wait_recv()
            to_sibling(m, line(m, dp), line(m, dp), step).start()

    def finish(m):
        for step in range(chips):
            dp = 2 * place.chip_at(step) + 1 - place.core
            to_sibling(m, line(m, dp), line(m, dp), step).wait_recv()
        own_copy(m).wait()

    targets = (None, key, value, query, None)
    lefts = (None, memory, memory, attn_in, None)
    share = weight.shape[2] // groups

    def part_copy(m, step):
        other = place.line_at(step)
        return remote(
            parts.at[m - 1, other], targets[m].at[seq], part_send.at[m - 1, step - 1], part_recv.at[m - 1, step - 1],
            place.line_device(other),
        )

    def own_part(m):
        return pltpu.make_async_copy(parts.at[m - 1, seq], targets[m].at[seq], part_own.at[m - 1])

    def load(m):
        return pltpu.make_async_copy(wholes[m], weight, load_sem)

    def project(m):
        load(m).start()
        load(m).wait()
        rows = weight.shape[0] * weight.shape[1]
        left = lefts[m][...]

        def one(step, _):
            group = place.line_at(step)
            columns = pl.ds(pl.multiple_of(group * share, share), share)
            right = weight[:, :, columns].reshape(rows, share)
            parts[m - 1, group] = jnp.dot(left, right, preferred_element_type=F32).astype(BF16)

            @pl.when(step > 0)
            def _():
                remote(
                    parts.at[m - 1, group], targets[m].at[seq], part_send.at[m - 1, step - 1],
                    part_recv.at[m - 1, step - 1], place.line_device(group),
                ).start()

            return 0

        lax.fori_loop(1, groups, one, 0)
        one(0, 0)
        own_part(m).start()

    def normalize():
        here = 128 // (weight.shape[1])
        tiles = weight.shape[2] // 128
        for tile in range(tiles):
            total = all_gains_v[tile * here]
            for i in range(1, here):
                total = total + pltpu.roll(all_gains_v[tile * here + i], i * weight.shape[1], 1)
            gain_rows[:, tile * 128 : (tile + 1) * 128] = total
        step_rows = 128 if hidden.shape[0] % 128 == 0 else hidden.shape[0]

        def some(i, _):
            rows = pl.ds(pl.multiple_of(i * step_rows, step_rows), step_rows)
            x = hidden[rows, :].astype(F32)
            normed = x * lax.rsqrt(jnp.mean(x * x, axis=-1, keepdims=True) + EPSILON)
            attn_in[rows, :] = (normed * gain_rows[0:1, :]).astype(BF16)
            return 0

        lax.fori_loop(0, hidden.shape[0] // step_rows, some, 0)

    all_gains_v = all_gains
    place.barrier()
    start_own(0)
    start_own(1)
    serve_line(0)
    start_own(2)
    serve_line(1)
    start_own(3)
    serve_chips(0)
    serve_line(2)
    start_own(4)
    serve_chips(1)
    finish(0)
    normalize()
    serve_line(3)
    start_own(5)
    finish(1)
    project(1)
    serve_line(4)
    start_own(6)
    for chunk in range(chunks):
        start_grad(chunk)
    serve_chips(2)
    finish(2)
    project(2)
    serve_line(5)
    start_own(7)
    serve_chips(3)
    finish(3)
    project(3)
    serve_line(6)
    serve_chips(4)
    serve_line(7)
    for chunk in range(chunks):
        serve_grad(chunk)
    finish(4)
    for chunk in range(chunks):
        finish_grad(chunk)
    for m in range(count, len(shards)):
        own_copy(m).wait()
    for m in range(len(shards)):
        for distance in range(1, groups):
            for upward in (True, False):
                came = seq >= distance - 1 if upward else seq < groups - distance + 1
                onward = above if upward else below

                @pl.when(came & onward)
                def _():
                    along(m, wholes[m].at[own_block(m)], own_block(m), distance, upward).wait_send()

        if m >= count:
            continue
        mine = line(m, place.dp)
        for step in range(1, chips):
            remote(
                mine, mine, chip_send.at[m, step - 1], chip_recv.at[m, step - 1], place.sibling
            ).wait_send()
        for step in range(chips):
            to_sibling(m, mine, mine, step).wait_send()
    for m in (1, 2, 3):
        own_part(m).wait()
        for step in range(1, groups):
            part_copy(m, step).wait()


def project_call(dp_count, groups, piece, width, here, padded, chunks):
    chips = dp_count // 2
    blocks = dp_count * groups
    share = width // groups
    hbm = pl.BlockSpec(memory_space=pl.ANY)
    vmem = pl.BlockSpec(memory_space=pltpu.VMEM)
    heads = jax.ShapeDtypeStruct((groups, piece, share), BF16)
    whole = jax.ShapeDtypeStruct((blocks, here, width), BF16)
    units = jax.ShapeDtypeStruct((groups, padded, width), BF16)
    dma = pltpu.SemaphoreType.DMA
    others = max(chips - 1, 1)
    return pl.pallas_call(
        functools.partial(project_kernel, dp_count, groups),
        in_specs=[vmem, vmem] + [hbm] * 9,
        out_specs=[vmem, vmem, hbm, hbm, hbm, vmem] + [hbm] * 8,
        out_shape=(
            jax.ShapeDtypeStruct((piece, width), BF16),
            jax.ShapeDtypeStruct((8, width), F32),
            heads, heads, heads,
            jax.ShapeDtypeStruct((blocks, 8, 128), F32),
            whole, whole, whole, whole, units, units, units,
            jax.ShapeDtypeStruct((chunks, dp_count, piece // chunks, width), BF16),
        ),
        scratch_shapes=[
            pltpu.VMEM((blocks, here, width), BF16),
            pltpu.VMEM((3, groups, piece, share), BF16),
            dma((8, 2, groups)), dma((8, 2, groups)),
            dma((5, others)), dma((5, others)),
            dma((5, chips)), dma((5, chips)),
            dma((8,)), dma, dma((3, groups - 1)), dma((3, groups - 1)), dma((3,)),
            dma((chunks,)), dma((chunks, others)), dma((chunks, others)), dma((chunks, chips)), dma((chunks, chips)),
        ],
        compiler_params=pltpu.CompilerParams(
            collective_id=1, has_side_effects=True, vmem_limit_bytes=48 * 1024 * 1024
        ),
        cost_estimate=pl.CostEstimate(
            flops=128 * piece * width * width, transcendentals=0, bytes_accessed=16 * width * width
        ),
        name="gather_project",
    )


def gain_tile(gain_attn, gain_ffn):
    here = gain_attn.shape[0]
    both = jnp.stack((gain_attn, gain_ffn)).astype(F32)
    return jnp.pad(both, ((0, 6), (0, 128 - here)))


def reduce_kernel(
    dp_count, groups, here, context, memory, attn_in, gain_rows, gain_ffn_term, grad_branch, dv, dk, dq,
    all_value, all_key, all_query, hidden, grad_mid,
    out_v, out_k, out_q, grad_out, grad_value, grad_key, grad_query, grad_memory, grad_hidden, grad_gains,
    right, core_buf, core_in, chip_buf, chip_in, kept, line_buf, line_in, line_own,
    part_send, part_recv, part_own, load_sem, core_send, core_recv, chip_send, chip_recv,
    line_send, line_recv, store_sem, core_free, chip_free,
    weight, panel_out, grad_attn_in, mid_buf, hidden_buf, gain_term, gain_buf, gain_in,
    weight_sem, panel_sem, mid_sem, hidden_sem, gain_send, gain_recv,
):
    place = Place(dp_count, groups)
    chips, seq = place.chips, place.seq
    panel = groups * here
    share = right.shape[3]
    lefts = (context, memory, memory, attn_in)
    parts = (None, dv, dk, dq)
    wholes = (None, out_v, out_k, out_q)
    grads = (grad_out, grad_value, grad_key, grad_query)
    count = 4

    def part_copy(m, step):
        other = place.line_at(step)
        return remote(
            parts[m].at[other], wholes[m].at[seq], part_send.at[m, step - 1], part_recv.at[m, step - 1],
            place.line_device(other),
        )

    def own_part(m):
        return pltpu.make_async_copy(parts[m].at[seq], wholes[m].at[seq], part_own.at[m])

    def send_parts(m):
        own_part(m).start()
        for step in range(1, groups):
            part_copy(m, step).start()

    def sent_parts(m):
        for step in range(1, groups):
            part_copy(m, step).wait_send()

    def load_copy(m, group):
        source = grad_branch.at[:, pl.ds(group * share, share)] if m == 0 else wholes[m].at[group]
        return pltpu.make_async_copy(source, right.at[m % 2, group], load_sem.at[group])

    def load_right(m):
        if m > 0:
            own_part(m).wait()
            for step in range(1, groups):
                part_copy(m, step).wait_recv()
        for group in range(groups):
            load_copy(m, group).start()
        for group in range(groups):
            load_copy(m, group).wait()

    def product(m, dp, store):
        rows = pl.ds(pl.multiple_of(dp * panel, panel), panel)
        left = lefts[m][:, rows].T

        def one(group, _):
            columns = pl.ds(pl.multiple_of(group * share, share), share)
            store(columns, jnp.dot(left, right[m % 2, group], preferred_element_type=F32))
            return 0

        lax.fori_loop(0, groups, one, 0)

    def core_copy(m, step):
        return remote(
            core_buf.at[step], core_in.at[m % 2, step], core_send.at[step], core_recv.at[m % 2, step], place.sibling
        )

    def chip_copy(m, step):
        return remote(
            chip_buf.at[m % 2, step - 1], chip_in.at[m % 2, step - 1], chip_send.at[m % 2, step - 1],
            chip_recv.at[m % 2, step - 1], place.chip_device(place.chip_at(step)),
        )

    def line_copy(m, step):
        return remote(
            line_buf.at[m, step - 1], line_in.at[m, step - 1], line_send.at[m, step - 1], line_recv.at[m, step - 1],
            place.line_device(place.line_at(step)),
        )

    order = tuple(range(1, chips)) + (0,)

    def to_sibling(m):
        if m >= 2:
            pl.semaphore_wait(core_free, 1)
        for step in order:
            if m >= 1:
                core_copy(m - 1, step).wait_send()
            dp = 2 * place.chip_at(step) + 1 - place.core

            def store(columns, value, step=step):
                core_buf[step, :, columns] = value.astype(BF16)

            product(m, dp, store)
            core_copy(m, step).start()

    def to_chips(m):
        for step in order:
            dp = 2 * place.chip_at(step) + place.core
            core_copy(m, step).wait_recv()
            if step > 0:
                if m >= 2:
                    chip_copy(m - 2, step).wait_send()
                    pl.semaphore_wait(chip_free.at[step - 1], 1)

                def store(columns, value, step=step):
                    total = value + core_in[m % 2, step, :, columns].astype(F32)
                    chip_buf[m % 2, step - 1, :, columns] = total.astype(BF16)

            else:

                def store(columns, value):
                    kept[m % 2, :, columns] = value + core_in[m % 2, 0, :, columns].astype(F32)

            product(m, dp, store)
            if step > 0:
                chip_copy(m, step).start()
        if m + 2 < count:
            pl.semaphore_signal(core_free, inc=1, device_id=place.sibling, device_id_type=BY_MESH)

    def to_line(m):
        for step in range(1, chips):
            chip_copy(m, step).wait_recv()
        for step in tuple(range(1, groups)) + (0,):
            block = place.line_at(step)
            rows = pl.ds(pl.multiple_of(block * here, here), here)
            total = kept[m % 2, rows, :]
            for other in range(1, chips):
                total = total + chip_in[m % 2, other - 1, rows, :].astype(F32)
            if step > 0:
                line_buf[m, step - 1] = total.astype(BF16)
                line_copy(m, step).start()
            else:
                line_own[m] = total
        if m + 2 < count:
            for step in range(1, chips):
                partner = place.chip_at(step)
                pl.semaphore_signal(
                    chip_free.at[step - 1], inc=1, device_id=place.chip_device(partner), device_id_type=BY_MESH
                )

    def store_grad(m):
        return pltpu.make_async_copy(line_own.at[m], grads[m], store_sem.at[m])

    def settle(m):
        total = line_own[m]
        for step in range(1, groups):
            line_copy(m, step).wait_recv()
            total = total + line_in[m, step - 1].astype(F32)
        line_own[m] = total
        store_grad(m).start()

    width = memory.shape[1]
    panels = width // panel
    piece = memory.shape[0]

    def weight_copy(slot, which, source, index):
        rows = pl.ds(pl.multiple_of(index * panel, panel), panel)
        return pltpu.make_async_copy(source.at[rows, :], weight.at[slot, which], weight_sem.at[slot, which])

    def panel_copy(slot, index):
        columns = pl.ds(pl.multiple_of(index * panel, panel), panel)
        return pltpu.make_async_copy(panel_out.at[slot], grad_memory.at[:, columns], panel_sem.at[slot])

    def back(slot, which, m):
        total = jnp.zeros((piece, panel), F32)
        for group in range(groups):
            columns = slice(group * share, (group + 1) * share)
            total = total + lax.dot_general(
                right[m % 2, group], weight[slot, which, :, columns], NT, preferred_element_type=F32
            )
        return total

    def memory_gradient():
        weight_copy(0, 0, all_value, 0).start()
        weight_copy(0, 1, all_key, 0).start()

        def one(index, _):
            slot = lax.rem(index, 2)

            @pl.when(index + 1 < panels)
            def _():
                weight_copy(1 - slot, 0, all_value, index + 1).start()
                weight_copy(1 - slot, 1, all_key, index + 1).start()

            weight_copy(slot, 0, all_value, index).wait()
            weight_copy(slot, 1, all_key, index).wait()

            @pl.when(index >= 2)
            def _():
                panel_copy(slot, index - 2).wait()

            panel_out[slot] = back(slot, 0, 1) + back(slot, 1, 2)
            panel_copy(slot, index).start()
            return 0

        lax.fori_loop(0, panels, one, 0)
        for index in range(max(panels - 2, 0), panels):
            panel_copy(index % 2, index).wait()

    def query_gradient():
        weight_copy(0, 0, all_query, 0).start()

        def one(index, _):
            slot = lax.rem(index, 2)

            @pl.when(index + 1 < panels)
            def _():
                weight_copy(1 - slot, 0, all_query, index + 1).start()

            weight_copy(slot, 0, all_query, index).wait()
            columns = pl.ds(pl.multiple_of(index * panel, panel), panel)
            grad_attn_in[:, columns] = back(slot, 0, 3)
            return 0

        lax.fori_loop(0, panels, one, 0)

    some = mid_buf.shape[1]
    batches = piece // some

    def batch_rows(index):
        return pl.ds(pl.multiple_of(index * some, some), some)

    def mid_copy(slot, index):
        return pltpu.make_async_copy(grad_mid.at[batch_rows(index), :], mid_buf.at[slot], mid_sem.at[slot])

    def hidden_copy(slot, index):
        return pltpu.make_async_copy(hidden.at[batch_rows(index), :], hidden_buf.at[slot], hidden_sem.at[slot])

    def hidden_store(index):
        rows = batch_rows(index)
        return pltpu.make_async_copy(grad_attn_in.at[rows, :], grad_hidden.at[rows, :], panel_sem.at[0])

    def hidden_gradient():
        gain_term[...] = jnp.zeros_like(gain_term)
        mid_copy(0, 0).start()
        hidden_copy(0, 0).start()

        def one(index, _):
            slot = lax.rem(index, 2)

            @pl.when(index + 1 < batches)
            def _():
                mid_copy(1 - slot, index + 1).start()
                hidden_copy(1 - slot, index + 1).start()

            mid_copy(slot, index).wait()
            hidden_copy(slot, index).wait()
            rows = batch_rows(index)
            x = hidden_buf[slot].astype(F32)
            rstd = lax.rsqrt(jnp.mean(x * x, axis=-1, keepdims=True) + EPSILON)
            normed = x * rstd
            grad = grad_attn_in[rows, :]
            gain_term[0:1, :] += jnp.sum(normed * grad, axis=0, keepdims=True)
            scaled = grad * gain_rows[0:1, :]
            shift = jnp.mean(scaled * normed, axis=-1, keepdims=True)
            grad_attn_in[rows, :] = mid_buf[slot] + rstd * (scaled - normed * shift)
            hidden_store(index).start()
            return 0

        lax.fori_loop(0, batches, one, 0)

    devices = dp_count * groups
    me = place.dp * groups + seq

    def gain_copy(step):
        owner = lax.rem(me + step, devices)
        return remote(
            gain_buf.at[owner], gain_in.at[step], gain_send, gain_recv, {"dp": owner // groups, "seq": owner % groups}
        )

    def send_gains():
        gain_term[1:2, :] = gain_ffn_term[0:1, :]
        per = 128 // here
        for owner in range(devices):
            tile = gain_term[:, owner // per * 128 : (owner // per + 1) * 128]
            shift = owner % per * here
            gain_buf[owner] = pltpu.roll(tile, 128 - shift, 1) if shift else tile

        def one(step, _):
            gain_copy(step).start()
            return 0

        lax.fori_loop(1, devices, one, 0)

    def sum_gains():
        remote(
            gain_buf.at[pl.ds(0, devices - 1)], gain_in.at[pl.ds(1, devices - 1)], gain_send, gain_recv, place.sibling
        ).wait()
        total = gain_buf[me]
        for step in range(1, devices):
            total = total + gain_in[step]
        grad_gains[...] = total

    everyone = pltpu.get_barrier_semaphore()

    def greet(step, _):
        other = lax.rem(me + step, devices)
        pl.semaphore_signal(
            everyone, inc=1, device_id={"dp": other // groups, "seq": other % groups}, device_id_type=BY_MESH
        )
        return 0

    lax.fori_loop(1, devices, greet, 0)
    pl.semaphore_wait(everyone, devices - 1)
    send_parts(1)
    load_right(0)
    to_sibling(0)
    to_chips(0)
    sent_parts(1)
    send_parts(2)
    load_right(1)
    to_sibling(1)
    to_chips(1)
    to_line(0)
    sent_parts(2)
    send_parts(3)
    load_right(2)
    to_sibling(2)
    to_chips(2)
    to_line(1)
    settle(0)
    memory_gradient()
    sent_parts(3)
    load_right(3)
    to_sibling(3)
    to_chips(3)
    to_line(2)
    settle(1)
    query_gradient()
    hidden_gradient()
    send_gains()
    to_line(3)
    settle(2)
    settle(3)
    sum_gains()
    pltpu.make_async_copy(grad_attn_in, grad_hidden, panel_sem.at[0]).wait()
    for step in range(chips):
        core_copy(3, step).wait_send()
    for m in (2, 3):
        for step in range(1, chips):
            chip_copy(m, step).wait_send()
    for m in range(count):
        for step in range(1, groups):
            line_copy(m, step).wait_send()
        store_grad(m).wait()


def reduce_call(dp_count, groups, piece, width, here):
    chips = dp_count // 2
    share = width // groups
    panel = groups * here
    hbm = pl.BlockSpec(memory_space=pl.ANY)
    vmem = pl.BlockSpec(memory_space=pltpu.VMEM)
    part = jax.ShapeDtypeStruct((groups, piece, share), BF16)
    grad = jax.ShapeDtypeStruct((here, width), F32)
    tokens = jax.ShapeDtypeStruct((piece, width), F32)
    some = min(64, piece)
    devices = dp_count * groups
    dma = pltpu.SemaphoreType.DMA
    others = max(chips - 1, 1)
    return pl.pallas_call(
        functools.partial(reduce_kernel, dp_count, groups, here),
        in_specs=[vmem] * 5 + [hbm] * 9,
        out_specs=[hbm] * 9 + [vmem],
        out_shape=(part, part, part, grad, grad, grad, grad, tokens, tokens, jax.ShapeDtypeStruct((8, 128), F32)),
        scratch_shapes=[
            pltpu.VMEM((2, groups, piece, share), BF16),
            pltpu.VMEM((chips, panel, width), BF16),
            pltpu.VMEM((2, chips, panel, width), BF16),
            pltpu.VMEM((2, others, panel, width), BF16),
            pltpu.VMEM((2, others, panel, width), BF16),
            pltpu.VMEM((2, panel, width), F32),
            pltpu.VMEM((4, groups - 1, here, width), BF16),
            pltpu.VMEM((4, groups - 1, here, width), BF16),
            pltpu.VMEM((4, here, width), F32),
            dma((4, groups - 1)), dma((4, groups - 1)), dma((4,)), dma((groups,)),
            dma((chips,)), dma((2, chips)),
            dma((2, others)), dma((2, others)),
            dma((4, groups - 1)), dma((4, groups - 1)), dma((4,)),
            pltpu.SemaphoreType.REGULAR, pltpu.SemaphoreType.REGULAR((others,)),
            pltpu.VMEM((2, 2, panel, width), BF16),
            pltpu.VMEM((2, piece, panel), F32),
            pltpu.VMEM((piece, width), F32),
            pltpu.VMEM((2, some, width), F32),
            pltpu.VMEM((2, some, width), BF16),
            pltpu.VMEM((8, width), F32),
            pltpu.VMEM((devices, 8, 128), F32),
            pltpu.VMEM((devices, 8, 128), F32),
            dma((2, 2)), dma((2,)), dma((2,)), dma((2,)), dma, dma,
        ],
        compiler_params=pltpu.CompilerParams(
            collective_id=2, has_side_effects=True, vmem_limit_bytes=63 * 1024 * 1024
        ),
        cost_estimate=pl.CostEstimate(
            flops=128 * piece * width * width, transcendentals=0, bytes_accessed=16 * width * width
        ),
        name="weight_gradients",
    )


def middle_kernel(
    dp_count, groups,
    gain_rows, hidden, context_heads, grad_own, out_rows, gate_rows, up_rows, down_rows, all_grad,
    context, gain_term, mid_out, grad_mid, grad_branch, grad_heads, branch, grad_down, grad_gate, grad_up,
    all_ffn, acts, grad_gates, grad_ups, core_in, chip_in, term_in,
    gate_w, up_w, down_w, out_w, mid, ffn_in, own_total, term_buf,
    col_send, col_recv, col_own, weight_sem, out_sem, mid_sem, chip_send, chip_recv, core_send, core_recv, own_sem,
    x_sem, dy_sem, act_sem, sum_send, sum_recv, load_sem, far_send, far_recv, branch_sem, left_sem, right_sem,
    term_send, term_recv, rows_sem, gm_sem, gb_sem, head_send, head_recv, head_own,
):
    place = Place(dp_count, groups)
    chips, seq, core = place.chips, place.seq, place.core
    piece, width = hidden.shape
    share = width // groups
    unit_rows = gate_rows.shape[0]
    padded = gate_w.shape[0]
    wide = (gate_rows, up_rows, down_rows)
    kept = (gate_w, up_w, down_w)

    def weight_copy(i):
        return pltpu.make_async_copy(wide[i], kept[i].at[pl.ds(0, unit_rows), :], weight_sem.at[i])

    def group_columns(group):
        return pl.ds(pl.multiple_of(group * share, share), share)

    def out_copy(group, slot):
        rows = pl.ds(pl.multiple_of(group * share, share), share)
        return pltpu.make_async_copy(out_rows.at[rows, :], out_w.at[slot], out_sem.at[slot])

    def collect(step):
        other = place.line_at(step)
        return remote(
            context_heads.at[other], context.at[:, group_columns(seq)], col_send.at[step - 1], col_recv.at[step - 1],
            place.line_device(other),
        )

    def came_from(step):
        return lax.rem(seq + groups - step, groups)

    place.barrier()
    for step in range(1, groups):
        collect(step).start()
    own_columns = pltpu.make_async_copy(context_heads.at[seq], context.at[:, group_columns(seq)], col_own)
    own_columns.start()
    out_copy(seq, 0).start()
    hidden_copy = pltpu.make_async_copy(hidden, ffn_in, own_sem)
    hidden_copy.start()
    for i in range(3):
        weight_copy(i).start()
        if padded > unit_rows:
            kept[i][unit_rows:, :] = jnp.zeros((padded - unit_rows, width), BF16)

    for step in range(groups):
        slot = step % 2
        group = came_from(step)
        if step + 1 < groups:
            out_copy(came_from(step + 1), 1 - slot).start()
        if step == 0:
            own_columns.wait()
        else:
            columns = context.at[:, group_columns(group)]
            remote(columns, columns, col_send.at[step - 1], col_recv.at[step - 1], place.sibling).wait_recv()
        out_copy(group, slot).wait()
        left = context[:, group_columns(group)]
        if step == 0:
            hidden_copy.wait()

        def project(part, _, left=left, slot=slot, step=step):
            columns = pl.ds(pl.multiple_of(part * share, share), share)
            value = mxu(left, out_w[slot, :, columns], NN)
            if step == 0:
                mid[:, columns] = ffn_in[:, columns].astype(F32) + value
            else:
                mid[:, columns] += value
            return 0

        lax.fori_loop(0, groups, project, 0)

    some = min(64, piece)
    batches = piece // some

    def batch(index):
        return pl.ds(pl.multiple_of(index * some, some), some)

    def normalize(index, _):
        rows = batch(index)
        x = mid[rows, :]
        rstd = lax.rsqrt(jnp.mean(x * x, axis=-1, keepdims=True) + EPSILON)
        ffn_in[rows, :] = (x * rstd * gain_rows[1:2, :]).astype(BF16)
        return 0

    lax.fori_loop(0, batches, normalize, 0)
    mid_copy = pltpu.make_async_copy(mid, mid_out, mid_sem)
    mid_copy.start()

    def to_chip(step):
        return remote(
            ffn_in, all_ffn.at[place.dp], chip_send.at[step - 1], chip_recv.at[step - 1],
            place.chip_device(place.chip_at(step)),
        )

    def to_sibling(step):
        dp = 2 * place.chip_at(step) + core
        return remote(all_ffn.at[dp], all_ffn.at[dp], core_send.at[step], core_recv.at[step], place.sibling)

    own_ffn = pltpu.make_async_copy(ffn_in, all_ffn.at[place.dp], own_sem)
    own_ffn.start()
    for step in range(1, chips):
        to_chip(step).start()
    own_ffn.wait()
    to_sibling(0).start()
    for i in range(3):
        weight_copy(i).wait()

    pieces = 2 * chips
    stored = (acts, grad_gates, grad_ups)

    def piece_of(u, own_first):
        step, which = u // 2, u % 2
        mine = 1 - which if own_first else which
        return step, which, 2 * place.chip_at(step) + mine * core + (1 - mine) * (1 - core)

    def hidden_units(x_buf, dy_buf, act_buf):
        def x_copy(u):
            dp = piece_of(u, True)[2]
            return pltpu.make_async_copy(all_ffn.at[dp], x_buf, x_sem)

        def dy_copy(u):
            dp = piece_of(u, True)[2]
            return pltpu.make_async_copy(all_grad.at[dp], dy_buf.at[u % 2], dy_sem.at[u % 2])

        def act_copy(u, i):
            dp = piece_of(u, True)[2]
            return pltpu.make_async_copy(act_buf.at[u % 2, i], stored[i].at[dp], act_sem.at[u % 2, i])

        dy_copy(0).start()

        def one(u, _):
            step, which, dp = piece_of(u, True)
            slot = u % 2

            @pl.when((which == 0) & (step > 0))
            def _():
                to_chip(step).wait_recv()
                to_sibling(step).start()

            @pl.when(which == 1)
            def _():
                to_sibling(step).wait_recv()

            x_copy(u).start()

            @pl.when(u + 1 < pieces)
            def _():
                dy_copy(u + 1).start()

            @pl.when(u >= 2)
            def _():
                for i in range(3):
                    act_copy(u - 2, i).wait()

            dy_copy(u).wait()
            grad_act = mxu(dy_buf[slot], down_w[...], NT)
            x_copy(u).wait()
            gate = mxu(x_buf[...], gate_w[...], NT)
            up = mxu(x_buf[...], up_w[...], NT)
            sig = 1.0 / (1.0 + jnp.exp(-gate))
            act_buf[slot, 0] = (gate * sig * up).astype(BF16)
            act_buf[slot, 1] = (grad_act * up * sig * (1.0 + gate * (1.0 - sig))).astype(BF16)
            act_buf[slot, 2] = (grad_act * gate * sig).astype(BF16)
            for i in range(3):
                act_copy(u, i).start()
            return 0

        lax.fori_loop(0, pieces, one, 0)
        for u in range(max(pieces - 2, 0), pieces):
            for i in range(3):
                act_copy(u, i).wait()

    pl.run_scoped(
        hidden_units,
        pltpu.VMEM((piece, width), BF16), pltpu.VMEM((2, piece, width), BF16), pltpu.VMEM((2, 3, piece, padded), BF16),
    )

    block = unit_rows // groups

    def term_copy(i, step):
        other = place.line_at(step)
        return remote(
            term_buf.at[i, pl.ds(other * block, block), :], term_in.at[i, step - 1], term_send.at[i, step - 1],
            term_recv.at[i, step - 1], place.line_device(other),
        )

    def weight_terms(left_buf, acc):
        for i, (lefts, rights) in enumerate(((acts, all_grad), (grad_gates, all_ffn), (grad_ups, all_ffn))):

            def copies(dp, slot, lefts=lefts, rights=rights):
                return (
                    pltpu.make_async_copy(lefts.at[dp], left_buf.at[slot], left_sem.at[slot]),
                    pltpu.make_async_copy(rights.at[dp], out_w.at[slot], right_sem.at[slot]),
                )

            for copy in copies(0, 0):
                copy.start()

            def one(dp, _, copies=copies):
                slot = dp % 2

                @pl.when(dp + 1 < dp_count)
                def _():
                    for copy in copies(dp + 1, 1 - slot):
                        copy.start()

                for copy in copies(dp, slot):
                    copy.wait()
                left = left_buf[slot].T

                def part_of(part, _):
                    columns = group_columns(part)
                    value = jnp.dot(left, out_w[slot, :, columns], preferred_element_type=F32)

                    @pl.when(dp == 0)
                    def _():
                        acc[:, columns] = value

                    @pl.when(dp > 0)
                    def _():
                        acc[:, columns] += value

                    return 0

                lax.fori_loop(0, groups, part_of, 0)
                return 0

            lax.fori_loop(0, dp_count, one, 0)
            term_buf[i] = acc[0:unit_rows, :].astype(BF16)
            for step in range(1, groups):
                term_copy(i, step).start()

    pl.run_scoped(weight_terms, pltpu.VMEM((2, piece, padded), BF16), pltpu.VMEM((padded, width), F32))

    def sum_copy(core_out, step):
        return remote(core_out, core_in.at[step], sum_send, sum_recv.at[step], place.sibling)

    def far_copy(chip_out, step):
        return remote(
            chip_out.at[step % 2], chip_in.at[step - 1], far_send.at[step % 2], far_recv.at[step - 1],
            place.chip_device(place.chip_at(step)),
        )

    def back_to_input(act_buf, core_out, chip_out, load_buf, branch_buf):
        def place_of(u):
            _, which, dp = piece_of(pieces - 2 + u - 4 * (u // 2), False)
            return chips - 1 - u // 2, which, dp

        def act_copy(u, i):
            dp = place_of(u)[2]
            return pltpu.make_async_copy(stored[i].at[dp], act_buf.at[u % 2, i], act_sem.at[u % 2, i])

        def branch_copy(u):
            dp = place_of(u)[2]
            return pltpu.make_async_copy(branch_buf.at[u % 2], branch.at[dp], branch_sem.at[u % 2])

        def load_copy(step):
            return pltpu.make_async_copy(core_in.at[step], load_buf, load_sem)

        for i in range(3):
            act_copy(0, i).start()

        def one(u, _):
            step, which, dp = place_of(u)
            slot = u % 2

            @pl.when(u + 1 < pieces)
            def _():
                for i in range(3):
                    act_copy(u + 1, i).start()

            for i in range(3):
                act_copy(u, i).wait()

            @pl.when(u >= 2)
            def _():
                branch_copy(u - 2).wait()

            def branch_of(part, _):
                columns = group_columns(part)
                branch_buf[slot, :, columns] = mxu(act_buf[slot, 0], down_w[:, columns], NN).astype(BF16)
                return 0

            @pl.when((which == 0) & (u >= 2))
            def _():
                sum_copy(core_out, step + 1).wait_send()

            @pl.when(which == 1)
            def _():
                lax.fori_loop(0, groups, branch_of, 0)
                sum_copy(core_out, step).wait_recv()
                load_copy(step).start()

                @pl.when((step > 0) & (step < chips - 2))
                def _():
                    far_copy(chip_out, step + 2).wait_send()

                load_copy(step).wait()

            def columns_of(part, _):
                columns = group_columns(part)
                value = mxu(act_buf[slot, 1], gate_w[:, columns], NN) + mxu(act_buf[slot, 2], up_w[:, columns], NN)

                @pl.when(which == 0)
                def _():
                    core_out[:, columns] = value.astype(BF16)

                @pl.when((which == 1) & (step > 0))
                def _():
                    chip_out[step % 2, :, columns] = (value + load_buf[:, columns].astype(F32)).astype(BF16)

                @pl.when((which == 1) & (step == 0))
                def _():
                    own_total[:, columns] = value + load_buf[:, columns].astype(F32)

                return 0

            lax.fori_loop(0, groups, columns_of, 0)

            @pl.when(which == 0)
            def _():
                sum_copy(core_out, step).start()
                lax.fori_loop(0, groups, branch_of, 0)

            @pl.when((which == 1) & (step > 0))
            def _():
                far_copy(chip_out, step).start()

            branch_copy(u).start()
            return 0

        lax.fori_loop(0, pieces, one, 0)
        for u in range(max(pieces - 2, 0), pieces):
            branch_copy(u).wait()
        sum_copy(core_out, 0).wait_send()
        for step in range(1, min(chips, 3)):
            far_copy(chip_out, step).wait_send()

    pl.run_scoped(
        back_to_input,
        pltpu.VMEM((2, 3, piece, padded), BF16), pltpu.VMEM((piece, width), BF16), pltpu.VMEM((2, piece, width), BF16),
        pltpu.VMEM((piece, width), BF16), pltpu.VMEM((2, piece, width), BF16),
    )

    for step in range(1, chips):
        landed = chip_in.at[step - 1]
        remote(landed, landed, far_send.at[0], far_recv.at[step - 1], place.sibling).wait_recv()
    for step in range(1, chips):
        to_chip(step).wait_send()
    mid_copy.wait()
    gain_term[...] = jnp.zeros_like(gain_term)

    def norm_and_heads(rows_buf, mid_buf, heads_buf, sum_buf):
        def rows_copy(index, step, slot):
            source = grad_own.at[batch(index), :] if step == 0 else chip_in.at[step - 1, batch(index), :]
            return pltpu.make_async_copy(source, rows_buf.at[slot, step], rows_sem.at[slot, step])

        def grad_mid_copy(index, slot):
            return pltpu.make_async_copy(mid_buf.at[slot], grad_mid.at[batch(index), :], gm_sem.at[slot])

        for step in range(chips):
            rows_copy(0, step, 0).start()

        def norm_back(index, _):
            slot = index % 2

            @pl.when(index + 1 < batches)
            def _():
                for step in range(chips):
                    rows_copy(index + 1, step, 1 - slot).start()

            for step in range(chips):
                rows_copy(index, step, slot).wait()

            @pl.when(index >= 2)
            def _():
                grad_mid_copy(index - 2, slot).wait()

            rows = batch(index)
            grad = own_total[rows, :]
            for step in range(1, chips):
                grad = grad + rows_buf[slot, step].astype(F32)
            x = mid[rows, :]
            rstd = lax.rsqrt(jnp.mean(x * x, axis=-1, keepdims=True) + EPSILON)
            normed = x * rstd
            gain_term[0:1, :] += jnp.sum(normed * grad, axis=0, keepdims=True)
            scaled = grad * gain_rows[1:2, :]
            shift = jnp.mean(scaled * normed, axis=-1, keepdims=True)
            total = rows_buf[slot, 0].astype(F32) + rstd * (scaled - normed * shift)
            mid_buf[slot] = total
            ffn_in[rows, :] = total.astype(BF16)
            grad_mid_copy(index, slot).start()
            return 0

        lax.fori_loop(0, batches, norm_back, 0)
        grad_branch_copy = pltpu.make_async_copy(ffn_in, grad_branch, gb_sem)
        grad_branch_copy.start()
        for index in range(max(batches - 2, 0), batches):
            grad_mid_copy(index, index % 2).wait()

        def head_copy(step):
            other = place.line_at(step)
            return remote(
                heads_buf.at[other], grad_heads.at[seq], head_send.at[step - 1], head_recv.at[step - 1],
                place.line_device(other),
            )

        own_heads = pltpu.make_async_copy(heads_buf.at[seq], grad_heads.at[seq], head_own)
        order = tuple(range(1, groups)) + (0,)
        out_copy(place.line_at(order[0]), 0).start()
        for at, step in enumerate(order):
            group = place.line_at(step)
            if at + 1 < groups:
                out_copy(place.line_at(order[at + 1]), (at + 1) % 2).start()
            out_copy(group, at % 2).wait()
            heads_buf[group] = mxu(ffn_in[...], out_w[at % 2], NT).astype(BF16)
            if step > 0:
                head_copy(step).start()
            else:
                own_heads.start()

        for i, target in enumerate((grad_down, grad_gate, grad_up)):
            for step in range(1, groups):
                term_copy(i, step).wait()

                def sum_load(step=step, i=i):
                    return pltpu.make_async_copy(term_in.at[i, step - 1], sum_buf.at[step - 1], rows_sem.at[0, 0])

                sum_load().start()
                sum_load().wait()
            total = term_buf[i, pl.ds(pl.multiple_of(seq * block, block), block), :].astype(F32)
            for step in range(1, groups):
                total = total + sum_buf[step - 1].astype(F32)
            mid[0:block, :] = total
            store = pltpu.make_async_copy(mid.at[pl.ds(0, block), :], target, gm_sem.at[0])
            store.start()
            store.wait()
        grad_branch_copy.wait()
        own_heads.wait()
        for step in range(1, groups):
            head_copy(step).wait()

    pl.run_scoped(
        norm_and_heads,
        pltpu.VMEM((2, chips, some, width), BF16), pltpu.VMEM((2, some, width), F32),
        pltpu.VMEM((groups, piece, share), BF16), pltpu.VMEM((groups - 1, block, width), BF16),
    )
    for step in range(1, groups):
        collect(step).wait_send()
    for step in range(chips):
        to_sibling(step).wait_send()


def middle_call(dp_count, groups, piece, width, unit_rows):
    chips = dp_count // 2
    share = width // groups
    assert share == piece
    padded = -(-unit_rows // 128) * 128
    block = unit_rows // groups
    others = max(chips - 1, 1)
    hbm = pl.BlockSpec(memory_space=pl.ANY)
    vmem = pl.BlockSpec(memory_space=pltpu.VMEM)
    dma = pltpu.SemaphoreType.DMA
    shape = jax.ShapeDtypeStruct
    return pl.pallas_call(
        functools.partial(middle_kernel, dp_count, groups),
        in_specs=[vmem] + [hbm] * 8,
        out_specs=[vmem, vmem] + [hbm] * 15,
        out_shape=(
            shape((piece, width), BF16),
            shape((8, width), F32),
            shape((piece, width), F32),
            shape((piece, width), F32),
            shape((piece, width), BF16),
            shape((groups, piece, share), BF16),
            shape((dp_count, piece, width), BF16),
            shape((block, width), F32),
            shape((block, width), F32),
            shape((block, width), F32),
            shape((dp_count, piece, width), BF16),
            shape((dp_count, piece, padded), BF16),
            shape((dp_count, piece, padded), BF16),
            shape((dp_count, piece, padded), BF16),
            shape((chips, piece, width), BF16),
            shape((others, piece, width), BF16),
            shape((3, groups - 1, block, width), BF16),
        ),
        scratch_shapes=[
            pltpu.VMEM((padded, width), BF16), pltpu.VMEM((padded, width), BF16), pltpu.VMEM((padded, width), BF16),
            pltpu.VMEM((2, share, width), BF16),
            pltpu.VMEM((piece, width), F32),
            pltpu.VMEM((piece, width), BF16),
            pltpu.VMEM((piece, width), F32),
            pltpu.VMEM((3, unit_rows, width), BF16),
            dma((groups - 1,)), dma((groups - 1,)), dma, dma((3,)), dma((2,)), dma,
            dma((others,)), dma((others,)), dma((chips,)), dma((chips,)), dma,
            dma, dma((2,)), dma((2, 3)),
            dma, dma((chips,)), dma, dma((2,)), dma((others,)), dma((2,)),
            dma((2,)), dma((2,)), dma((3, groups - 1)), dma((3, groups - 1)),
            dma((2, chips)), dma((2,)), dma,
            dma((groups - 1,)), dma((groups - 1,)), dma,
        ],
        compiler_params=pltpu.CompilerParams(
            collective_id=5, has_side_effects=True, vmem_limit_bytes=63 * 1024 * 1024
        ),
        cost_estimate=pl.CostEstimate(
            flops=128 * piece * width * width, transcendentals=0, bytes_accessed=64 * width * width
        ),
        name="feed_forward",
    )


def shards(
    hidden_in, memory, segments, gain_attn, w_query, w_key, w_value, w_out, gain_ffn, w_gate, w_up, w_down, cotangent
):
    seqs, piece, width = hidden_in.shape
    groups = lax.axis_size("seq")
    dp_count = lax.axis_size("dp")
    assert seqs == 1
    length = piece * groups
    share = width // groups
    heads = share // HEAD_DIM
    here = w_query.shape[0]
    block = min(512, length)
    tokens = hidden_in.reshape(piece, width)
    mem = memory.reshape(piece, width)
    grad_out = cotangent.reshape(piece, width)

    attend_forward, attend_backward = attention_calls(length, heads, block)
    start, low, high = document_bounds(segments[0], block)
    flat = (length, share)
    split = (groups, piece, share)

    units = w_gate.shape[0]
    padded = -(-units // 16) * 16
    own_units = [jnp.pad(weight, ((0, padded - units), (0, 0))) for weight in (w_gate, w_up, w_down)]
    (
        attn_in, gain_rows, key, value, query, _, key_rows, value_rows, query_rows, out_rows,
        gate_rows, up_rows, down_rows, dy,
    ) = project_call(dp_count, groups, piece, width, here, padded, 1)(
        tokens, mem, gain_tile(gain_attn, gain_ffn), w_key, w_value, w_query, w_out, *own_units, grad_out
    )
    gate_rows, up_rows, down_rows = [
        rows.reshape(groups * padded, width) for rows in (gate_rows, up_rows, down_rows)
    ]
    key, value, query = [part.reshape(flat) for part in (key, value, query)]
    key_rows, value_rows, query_rows, out_rows = [
        rows.reshape(width, width) for rows in (key_rows, value_rows, query_rows, out_rows)
    ]
    context_heads, lse = attend_forward(low, start, query, key, value)
    (
        context, gain_term, mid, grad_mid, grad_branch, grad_context_heads, branch, grad_w_down, grad_w_gate, grad_w_up, *_
    ) = middle_call(dp_count, groups, piece, width, groups * padded)(
        gain_rows, tokens, context_heads.reshape(split), grad_out, out_rows, gate_rows, up_rows, down_rows,
        dy.reshape(dp_count, piece, width),
    )
    branch = lax.psum_scatter(branch.reshape(dp_count * piece, width), "dp", scatter_dimension=0, tiled=True)
    grad_context_heads = grad_context_heads.reshape(flat)
    dq, dk, dv = attend_backward(high, start, query, key, value, context_heads, grad_context_heads, lse)

    _, _, _, grad_w_out, grad_w_value, grad_w_key, grad_w_query, grad_memory, grad_hidden, gains = reduce_call(
        dp_count, groups, piece, width, here
    )(
        context, mem, attn_in, gain_rows, gain_term, grad_branch, dv.reshape(split), dk.reshape(split),
        dq.reshape(split), value_rows, key_rows, query_rows, tokens, grad_mid,
    )
    gains, branch, mid = lax.optimization_barrier((gains, branch, mid))
    grad_w_down, grad_w_gate, grad_w_up = [grad[:units] for grad in (grad_w_down, grad_w_gate, grad_w_up)]
    layer_out = (mid + branch.astype(F32)).astype(BF16)
    grad_gain_attn, grad_gain_ffn = gains[0, :here], gains[1, :here]
    cube = (seqs, piece, width)
    return (
        layer_out.reshape(cube),
        grad_hidden.reshape(cube),
        grad_memory.reshape(cube),
        grad_gain_attn,
        grad_w_query,
        grad_w_key,
        grad_w_value,
        grad_w_out,
        grad_gain_ffn,
        grad_w_gate,
        grad_w_up,
        grad_w_down,
    )


def solution(mesh):
    tokens = P("dp", "seq", None)
    rows = P(ALL, None)
    gain = P(ALL)
    in_specs = (tokens, tokens, P("dp", None), gain, rows, rows, rows, rows, gain, rows, rows, rows, tokens)
    out_specs = (tokens, tokens, tokens, gain, rows, rows, rows, rows, gain, rows, rows, rows)
    return jax.shard_map(shards, mesh=mesh, in_specs=in_specs, out_specs=out_specs, check_vma=False)
```

```python
import functools
import math

import jax
import jax.numpy as jnp
from jax import lax
from jax.experimental import pallas as pl
from jax.experimental.pallas import tpu as pltpu
from jax.sharding import PartitionSpec as P

HEAD_DIM = 128
DOCS = 4
EPSILON = 1e-06
MASKED = -1e30
ALL = ("dp", "seq")
F32 = jnp.float32
BF16 = jnp.bfloat16
EXP2_SCALE = HEAD_DIM ** (-0.5) * math.log2(math.e)
NT = (((1,), (1,)), ((), ()))
TN = (((0,), (0,)), ((), ()))
NN = (((1,), (0,)), ((), ()))
BY_MESH = pl.DeviceIdType.MESH


def mxu(left, right, dims):
    return lax.dot_general(left, right, dims, preferred_element_type=F32)


def rms_scale(values):
    return lax.rsqrt(jnp.mean(values * values, axis=-1, keepdims=True) + EPSILON)


def norm_back(grad_normed, normed, rstd, gain):
    scaled = grad_normed * gain
    return rstd * (scaled - normed * jnp.mean(scaled * normed, axis=-1, keepdims=True))


def forward_kernel(block, low_ref, start_ref, q_ref, k_ref, v_ref, out_ref, lse_ref):
    length = q_ref.shape[0]

    def one_query_block(qb, _):
        q0 = pl.multiple_of(qb * block, block)
        rows = pl.ds(q0, block)
        query = q_ref[rows, :]
        start = start_ref[:, rows]
        query_pos = q0 + lax.broadcasted_iota(jnp.int32, (block, block), 1)

        def one_key_block(kb, carry):
            top, total, acc = carry
            k0 = pl.multiple_of(kb * block, block)
            keys = pl.ds(k0, block)
            score = mxu(k_ref[keys, :], query, NT)
            key_pos = k0 + lax.broadcasted_iota(jnp.int32, (block, block), 0)
            score = jnp.where((key_pos >= start) & (key_pos <= query_pos), score, MASKED)
            new_top = jnp.maximum(top, jnp.max(score, axis=0, keepdims=True))
            shrink = jnp.exp2((top - new_top) * EXP2_SCALE)
            raised = jnp.exp2((score - new_top) * EXP2_SCALE)
            total = total * shrink + jnp.sum(raised, axis=0, keepdims=True)
            acc = acc * shrink + mxu(v_ref[keys, :], raised.astype(BF16), TN)
            return new_top, total, acc

        top, total, acc = lax.fori_loop(
            low_ref[qb],
            qb + 1,
            one_key_block,
            (
                jnp.full((1, block), MASKED, F32),
                jnp.zeros((1, block), F32),
                jnp.zeros((HEAD_DIM, block), F32),
            ),
        )
        out_ref[rows, :] = (acc / total).T.astype(BF16)
        lse_ref[0, :, rows] = top * EXP2_SCALE + jnp.log2(total)
        return 0

    lax.fori_loop(0, length // block, one_query_block, 0)


def backward_kernel(
    block, high_ref, start_ref, q_ref, k_ref, v_ref, ctx_ref, grad_ref, lse_ref,
    dq_ref, dk_ref, dv_ref, dq_acc, delta_acc,
):
    length = q_ref.shape[0]
    blocks = length // block
    scale = HEAD_DIM ** (-0.5)
    dq_acc[...] = jnp.zeros_like(dq_acc)

    def one_delta(qb, _):
        rows = pl.ds(pl.multiple_of(qb * block, block), block)
        both = ctx_ref[rows, :].astype(F32) * grad_ref[rows, :].astype(F32)
        delta_acc[:, rows] = jnp.sum(both.T, axis=0, keepdims=True)
        return 0

    lax.fori_loop(0, blocks, one_delta, 0)

    def one_key_block(kb, _):
        k0 = pl.multiple_of(kb * block, block)
        keys = pl.ds(k0, block)
        key = k_ref[keys, :]
        value = v_ref[keys, :]
        key_pos = k0 + lax.broadcasted_iota(jnp.int32, (block, block), 0)

        def one_query_block(qb, carry):
            dk, dv = carry
            q0 = pl.multiple_of(qb * block, block)
            rows = pl.ds(q0, block)
            query = q_ref[rows, :]
            grad = grad_ref[rows, :]
            start = start_ref[:, rows]
            query_pos = q0 + lax.broadcasted_iota(jnp.int32, (block, block), 1)
            score = mxu(key, query, NT)
            prob = jnp.exp2(score * EXP2_SCALE - lse_ref[0, :, rows])
            prob = jnp.where((key_pos >= start) & (key_pos <= query_pos), prob, 0.0)
            grad_prob = mxu(value, grad, NT)
            grad_score = (prob * (grad_prob - delta_acc[:, rows])).astype(BF16)
            dv = dv + mxu(prob.astype(BF16), grad, NN)
            dk = dk + mxu(grad_score, query, NN)
            dq_acc[rows, :] += mxu(grad_score, key, TN)
            return dk, dv

        zeros = jnp.zeros((block, HEAD_DIM), F32)
        dk, dv = lax.fori_loop(kb, high_ref[kb], one_query_block, (zeros, zeros))
        dk_ref[keys, :] = (dk * scale).astype(BF16)
        dv_ref[keys, :] = dv.astype(BF16)
        return 0

    lax.fori_loop(0, blocks, one_key_block, 0)
    dq_ref[...] = (dq_acc[...] * scale).astype(BF16)


def attention_calls(length, heads, block):
    column = pl.BlockSpec((length, HEAD_DIM), lambda h, *_: (0, h))
    row = pl.BlockSpec((1, length), lambda h, *_: (0, 0))
    stat = pl.BlockSpec((1, 1, length), lambda h, *_: (h, 0, 0))
    flat = jax.ShapeDtypeStruct((length, heads * HEAD_DIM), BF16)
    pairs = heads * length * length // 4
    forward = pl.pallas_call(
        functools.partial(forward_kernel, block),
        grid_spec=pltpu.PrefetchScalarGridSpec(
            num_scalar_prefetch=1,
            grid=(heads,),
            in_specs=[row, column, column, column],
            out_specs=[column, stat],
        ),
        out_shape=(flat, jax.ShapeDtypeStruct((heads, 1, length), F32)),
        cost_estimate=pl.CostEstimate(
            flops=64 * pairs * HEAD_DIM, transcendentals=pairs, bytes_accessed=8 * length * heads * HEAD_DIM
        ),
        name="attend_forward",
    )
    backward = pl.pallas_call(
        functools.partial(backward_kernel, block),
        grid_spec=pltpu.PrefetchScalarGridSpec(
            num_scalar_prefetch=1,
            grid=(heads,),
            in_specs=[row, column, column, column, column, column, stat],
            out_specs=[column, column, column],
            scratch_shapes=[pltpu.VMEM((length, HEAD_DIM), F32), pltpu.VMEM((1, length), F32)],
        ),
        out_shape=(flat, flat, flat),
        cost_estimate=pl.CostEstimate(
            flops=96 * pairs * HEAD_DIM, transcendentals=pairs, bytes_accessed=16 * length * heads * HEAD_DIM
        ),
        name="attend_backward",
    )
    return forward, backward


def document_bounds(segment_ids, block):
    first = jnp.zeros_like(segment_ids)
    last = jnp.zeros_like(segment_ids)
    for number in range(DOCS):
        below = jnp.sum((segment_ids < number).astype(jnp.int32))
        upto = jnp.sum((segment_ids <= number).astype(jnp.int32))
        first = jnp.where(segment_ids == number, below, first)
        last = jnp.where(segment_ids == number, upto - 1, last)
    low = first[::block] // block
    high = last[block - 1 :: block] // block + 1
    return first[None, :], low, high


def remote(src, dst, send, recv, device):
    return pltpu.make_async_remote_copy(
        src_ref=src, dst_ref=dst, send_sem=send, recv_sem=recv, device_id=device, device_id_type=BY_MESH
    )


class Place:
    def __init__(self, dp_count, groups):
        self.groups = groups
        self.chips = dp_count // 2
        self.dp = lax.axis_index("dp")
        self.seq = lax.axis_index("seq")
        self.core = lax.rem(self.dp, 2)
        self.chip = self.dp // 2
        self.sibling = {"dp": self.dp + 1 - 2 * self.core, "seq": self.seq}

    def chip_at(self, step):
        chip, bit = self.chip, 1
        while bit < self.chips:
            chip = chip + (step // bit % 2) * bit * (1 - 2 * lax.rem(self.chip // bit, 2))
            bit *= 2
        return chip

    def chip_device(self, chip):
        return {"dp": 2 * chip + self.core, "seq": self.seq}

    def line_at(self, step):
        return lax.rem(self.seq + step, self.groups)

    def line_device(self, seq):
        return {"dp": self.dp, "seq": seq}

    def barrier(self):
        everyone = pltpu.get_barrier_semaphore()
        for step in range(1, self.groups):
            pl.semaphore_signal(everyone, inc=1, device_id=self.line_device(self.line_at(step)), device_id_type=BY_MESH)
        for step in range(1, self.chips):
            pl.semaphore_signal(everyone, inc=1, device_id=self.chip_device(self.chip_at(step)), device_id_type=BY_MESH)
        pl.semaphore_signal(everyone, inc=1, device_id=self.sibling, device_id_type=BY_MESH)
        pl.semaphore_wait(everyone, self.groups + self.chips - 1)


def project_kernel(
    dp_count, groups, hidden, memory, gains, w_key, w_value, w_query, w_out, w_gate, w_up, w_down, grad,
    attn_in, gain_rows, key, value, query, all_gains, all_key, all_value, all_query, all_out,
    all_gate, all_up, all_down, all_grad,
    weight, parts, line_send, line_recv, chip_send, chip_recv, core_send, core_recv,
    own_sem, load_sem, part_send, part_recv, part_own,
    dy_own, dy_chip_send, dy_chip_recv, dy_core_send, dy_core_recv,
):
    place = Place(dp_count, groups)
    chips, seq = place.chips, place.seq
    shards = (gains, w_key, w_value, w_query, w_out, w_gate, w_up, w_down)
    wholes = (all_gains, all_key, all_value, all_query, all_out, all_gate, all_up, all_down)
    count = 5
    whole_own = place.dp * groups + seq

    def own_block(m):
        return whole_own if m < count else seq

    above, below = seq < groups - 1, seq > 0
    up, down = place.line_device(lax.rem(seq + 1, groups)), place.line_device(lax.rem(seq + groups - 1, groups))

    def line(m, dp):
        return wholes[m].at[pl.ds(dp * groups, groups)]

    def along(m, src, block, distance, upward):
        slot = 0 if upward else 1
        return remote(
            src, wholes[m].at[block], line_send.at[m, slot, distance - 1], line_recv.at[m, slot, distance - 1],
            up if upward else down,
        )

    def to_chip(m, src, block, step):
        return remote(
            src, wholes[m].at[block], chip_send.at[m, step - 1], chip_recv.at[m, step - 1],
            place.chip_device(place.chip_at(step)),
        )

    def to_sibling(m, src, dst, step):
        return remote(src, dst, core_send.at[m, step], core_recv.at[m, step], place.sibling)

    def spread(m, src, block):
        for step in range(1, chips):
            to_chip(m, src, block, step).start()
        to_sibling(m, src, wholes[m].at[block], 0).start()

    def own_copy(m):
        return pltpu.make_async_copy(shards[m], wholes[m].at[own_block(m)], own_sem.at[m])

    def start_own(m):
        own = own_block(m)
        own_copy(m).start()

        @pl.when(above)
        def _():
            along(m, shards[m], own, 1, True).start()

        @pl.when(below)
        def _():
            along(m, shards[m], own, 1, False).start()

        if m < count:
            spread(m, shards[m], own)

    def serve_line(m):
        for distance in range(1, groups):
            for upward in (True, False):
                block = own_block(m) - distance if upward else own_block(m) + distance
                there = seq >= distance if upward else seq < groups - distance
                onward = above if upward else below

                @pl.when(there)
                def _():
                    landed = wholes[m].at[block]
                    along(m, landed, block, distance, upward).wait_recv()

                    @pl.when(onward)
                    def _():
                        along(m, landed, block, distance + 1, upward).start()

                    if m < count:
                        spread(m, landed, block)

    chunks = all_grad.shape[0]
    chunk_rows = grad.shape[0] // chunks

    def grad_rows(chunk):
        return grad.at[pl.ds(chunk * chunk_rows, chunk_rows), :]

    def grad_own(chunk):
        return pltpu.make_async_copy(grad_rows(chunk), all_grad.at[chunk, place.dp], dy_own.at[chunk])

    def grad_to_chip(chunk, step):
        return remote(
            grad_rows(chunk), all_grad.at[chunk, place.dp], dy_chip_send.at[chunk, step - 1],
            dy_chip_recv.at[chunk, step - 1], place.chip_device(place.chip_at(step)),
        )

    def grad_to_sibling(chunk, step):
        dp = 2 * place.chip_at(step) + place.core
        src = all_grad.at[chunk, dp] if step > 0 else grad_rows(chunk)
        return remote(
            src, all_grad.at[chunk, dp], dy_core_send.at[chunk, step], dy_core_recv.at[chunk, step], place.sibling
        )

    def start_grad(chunk):
        grad_own(chunk).start()
        for step in range(1, chips):
            grad_to_chip(chunk, step).start()
        grad_to_sibling(chunk, 0).start()

    def serve_grad(chunk):
        for step in range(1, chips):
            grad_to_chip(chunk, step).wait_recv()
            grad_to_sibling(chunk, step).start()

    def finish_grad(chunk):
        grad_own(chunk).wait()
        for step in range(1, chips):
            grad_to_chip(chunk, step).wait_send()
        for step in range(chips):
            grad_to_sibling(chunk, step).wait()

    def serve_chips(m):
        for step in range(1, chips):
            dp = 2 * place.chip_at(step) + place.core
            remote(
                line(m, dp), line(m, dp), chip_send.at[m, step - 1], chip_recv.at[m, step - 1], place.sibling
            ).wait_recv()
            to_sibling(m, line(m, dp), line(m, dp), step).start()

    def finish(m):
        for step in range(chips):
            dp = 2 * place.chip_at(step) + 1 - place.core
            to_sibling(m, line(m, dp), line(m, dp), step).wait_recv()
        own_copy(m).wait()

    targets = (None, key, value, query, None)
    lefts = (None, memory, memory, attn_in, None)
    share = weight.shape[2] // groups

    def part_copy(m, step):
        other = place.line_at(step)
        return remote(
            parts.at[m - 1, other], targets[m].at[seq], part_send.at[m - 1, step - 1], part_recv.at[m - 1, step - 1],
            place.line_device(other),
        )

    def own_part(m):
        return pltpu.make_async_copy(parts.at[m - 1, seq], targets[m].at[seq], part_own.at[m - 1])

    def load(m):
        return pltpu.make_async_copy(wholes[m], weight, load_sem)

    def project(m):
        load(m).start()
        load(m).wait()
        rows = weight.shape[0] * weight.shape[1]
        left = lefts[m][...]

        def one(step, _):
            group = place.line_at(step)
            columns = pl.ds(pl.multiple_of(group * share, share), share)
            right = weight[:, :, columns].reshape(rows, share)
            parts[m - 1, group] = jnp.dot(left, right, preferred_element_type=F32).astype(BF16)

            @pl.when(step > 0)
            def _():
                remote(
                    parts.at[m - 1, group], targets[m].at[seq], part_send.at[m - 1, step - 1],
                    part_recv.at[m - 1, step - 1], place.line_device(group),
                ).start()

            return 0

        lax.fori_loop(1, groups, one, 0)
        one(0, 0)
        own_part(m).start()

    def normalize():
        here = 128 // (weight.shape[1])
        tiles = weight.shape[2] // 128
        for tile in range(tiles):
            total = all_gains_v[tile * here]
            for i in range(1, here):
                total = total + pltpu.roll(all_gains_v[tile * here + i], i * weight.shape[1], 1)
            gain_rows[:, tile * 128 : (tile + 1) * 128] = total
        step_rows = 128 if hidden.shape[0] % 128 == 0 else hidden.shape[0]

        def some(i, _):
            rows = pl.ds(pl.multiple_of(i * step_rows, step_rows), step_rows)
            x = hidden[rows, :].astype(F32)
            normed = x * lax.rsqrt(jnp.mean(x * x, axis=-1, keepdims=True) + EPSILON)
            attn_in[rows, :] = (normed * gain_rows[0:1, :]).astype(BF16)
            return 0

        lax.fori_loop(0, hidden.shape[0] // step_rows, some, 0)

    all_gains_v = all_gains
    place.barrier()
    start_own(0)
    start_own(1)
    serve_line(0)
    start_own(2)
    serve_line(1)
    start_own(3)
    serve_chips(0)
    serve_line(2)
    start_own(4)
    serve_chips(1)
    finish(0)
    normalize()
    serve_line(3)
    start_own(5)
    finish(1)
    project(1)
    serve_line(4)
    start_own(6)
    for chunk in range(chunks):
        start_grad(chunk)
    serve_chips(2)
    finish(2)
    project(2)
    serve_line(5)
    start_own(7)
    serve_chips(3)
    finish(3)
    project(3)
    serve_line(6)
    serve_chips(4)
    serve_line(7)
    for chunk in range(chunks):
        serve_grad(chunk)
    finish(4)
    for chunk in range(chunks):
        finish_grad(chunk)
    for m in range(count, len(shards)):
        own_copy(m).wait()
    for m in range(len(shards)):
        for distance in range(1, groups):
            for upward in (True, False):
                came = seq >= distance - 1 if upward else seq < groups - distance + 1
                onward = above if upward else below

                @pl.when(came & onward)
                def _():
                    along(m, wholes[m].at[own_block(m)], own_block(m), distance, upward).wait_send()

        if m >= count:
            continue
        mine = line(m, place.dp)
        for step in range(1, chips):
            remote(
                mine, mine, chip_send.at[m, step - 1], chip_recv.at[m, step - 1], place.sibling
            ).wait_send()
        for step in range(chips):
            to_sibling(m, mine, mine, step).wait_send()
    for m in (1, 2, 3):
        own_part(m).wait()
        for step in range(1, groups):
            part_copy(m, step).wait()


def project_call(dp_count, groups, piece, width, here, padded, chunks):
    chips = dp_count // 2
    blocks = dp_count * groups
    share = width // groups
    hbm = pl.BlockSpec(memory_space=pl.ANY)
    vmem = pl.BlockSpec(memory_space=pltpu.VMEM)
    heads = jax.ShapeDtypeStruct((groups, piece, share), BF16)
    whole = jax.ShapeDtypeStruct((blocks, here, width), BF16)
    units = jax.ShapeDtypeStruct((groups, padded, width), BF16)
    dma = pltpu.SemaphoreType.DMA
    others = max(chips - 1, 1)
    return pl.pallas_call(
        functools.partial(project_kernel, dp_count, groups),
        in_specs=[vmem, vmem] + [hbm] * 9,
        out_specs=[vmem, vmem, hbm, hbm, hbm, vmem] + [hbm] * 8,
        out_shape=(
            jax.ShapeDtypeStruct((piece, width), BF16),
            jax.ShapeDtypeStruct((8, width), F32),
            heads, heads, heads,
            jax.ShapeDtypeStruct((blocks, 8, 128), F32),
            whole, whole, whole, whole, units, units, units,
            jax.ShapeDtypeStruct((chunks, dp_count, piece // chunks, width), BF16),
        ),
        scratch_shapes=[
            pltpu.VMEM((blocks, here, width), BF16),
            pltpu.VMEM((3, groups, piece, share), BF16),
            dma((8, 2, groups)), dma((8, 2, groups)),
            dma((5, others)), dma((5, others)),
            dma((5, chips)), dma((5, chips)),
            dma((8,)), dma, dma((3, groups - 1)), dma((3, groups - 1)), dma((3,)),
            dma((chunks,)), dma((chunks, others)), dma((chunks, others)), dma((chunks, chips)), dma((chunks, chips)),
        ],
        compiler_params=pltpu.CompilerParams(
            collective_id=1, has_side_effects=True, vmem_limit_bytes=48 * 1024 * 1024
        ),
        cost_estimate=pl.CostEstimate(
            flops=128 * piece * width * width, transcendentals=0, bytes_accessed=16 * width * width
        ),
        name="gather_project",
    )


def gain_tile(gain_attn, gain_ffn):
    here = gain_attn.shape[0]
    both = jnp.stack((gain_attn, gain_ffn)).astype(F32)
    return jnp.pad(both, ((0, 6), (0, 128 - here)))


def reduce_kernel(
    dp_count, groups, here, context, memory, attn_in, gain_rows, gain_ffn_term, grad_branch, dv, dk, dq,
    all_value, all_key, all_query, hidden, grad_mid,
    out_v, out_k, out_q, grad_out, grad_value, grad_key, grad_query, grad_memory, grad_hidden, grad_gains,
    right, core_buf, core_in, chip_buf, chip_in, kept, line_buf, line_in, line_own,
    part_send, part_recv, part_own, load_sem, core_send, core_recv, chip_send, chip_recv,
    line_send, line_recv, store_sem, core_free, chip_free,
    weight, panel_out, grad_attn_in, mid_buf, hidden_buf, gain_term, gain_buf, gain_in,
    weight_sem, panel_sem, mid_sem, hidden_sem, gain_send, gain_recv,
):
    place = Place(dp_count, groups)
    chips, seq = place.chips, place.seq
    panel = groups * here
    share = right.shape[3]
    lefts = (context, memory, memory, attn_in)
    parts = (None, dv, dk, dq)
    wholes = (None, out_v, out_k, out_q)
    grads = (grad_out, grad_value, grad_key, grad_query)
    count = 4

    def part_copy(m, step):
        other = place.line_at(step)
        return remote(
            parts[m].at[other], wholes[m].at[seq], part_send.at[m, step - 1], part_recv.at[m, step - 1],
            place.line_device(other),
        )

    def own_part(m):
        return pltpu.make_async_copy(parts[m].at[seq], wholes[m].at[seq], part_own.at[m])

    def send_parts(m):
        own_part(m).start()
        for step in range(1, groups):
            part_copy(m, step).start()

    def sent_parts(m):
        for step in range(1, groups):
            part_copy(m, step).wait_send()

    def load_copy(m, group):
        source = grad_branch.at[:, pl.ds(group * share, share)] if m == 0 else wholes[m].at[group]
        return pltpu.make_async_copy(source, right.at[m % 2, group], load_sem.at[group])

    def load_right(m):
        if m > 0:
            own_part(m).wait()
            for step in range(1, groups):
                part_copy(m, step).wait_recv()
        for group in range(groups):
            load_copy(m, group).start()
        for group in range(groups):
            load_copy(m, group).wait()

    def product(m, dp, store):
        rows = pl.ds(pl.multiple_of(dp * panel, panel), panel)
        left = lefts[m][:, rows].T

        def one(group, _):
            columns = pl.ds(pl.multiple_of(group * share, share), share)
            store(columns, jnp.dot(left, right[m % 2, group], preferred_element_type=F32))
            return 0

        lax.fori_loop(0, groups, one, 0)

    def core_copy(m, step):
        return remote(
            core_buf.at[step], core_in.at[m % 2, step], core_send.at[step], core_recv.at[m % 2, step], place.sibling
        )

    def chip_copy(m, step):
        return remote(
            chip_buf.at[m % 2, step - 1], chip_in.at[m % 2, step - 1], chip_send.at[m % 2, step - 1],
            chip_recv.at[m % 2, step - 1], place.chip_device(place.chip_at(step)),
        )

    def line_copy(m, step):
        return remote(
            line_buf.at[m, step - 1], line_in.at[m, step - 1], line_send.at[m, step - 1], line_recv.at[m, step - 1],
            place.line_device(place.line_at(step)),
        )

    order = tuple(range(1, chips)) + (0,)

    def to_sibling(m):
        if m >= 2:
            pl.semaphore_wait(core_free, 1)
        for step in order:
            if m >= 1:
                core_copy(m - 1, step).wait_send()
            dp = 2 * place.chip_at(step) + 1 - place.core

            def store(columns, value, step=step):
                core_buf[step, :, columns] = value.astype(BF16)

            product(m, dp, store)
            core_copy(m, step).start()

    def to_chips(m):
        for step in order:
            dp = 2 * place.chip_at(step) + place.core
            core_copy(m, step).wait_recv()
            if step > 0:
                if m >= 2:
                    chip_copy(m - 2, step).wait_send()
                    pl.semaphore_wait(chip_free.at[step - 1], 1)

                def store(columns, value, step=step):
                    total = value + core_in[m % 2, step, :, columns].astype(F32)
                    chip_buf[m % 2, step - 1, :, columns] = total.astype(BF16)

            else:

                def store(columns, value):
                    kept[m % 2, :, columns] = value + core_in[m % 2, 0, :, columns].astype(F32)

            product(m, dp, store)
            if step > 0:
                chip_copy(m, step).start()
        if m + 2 < count:
            pl.semaphore_signal(core_free, inc=1, device_id=place.sibling, device_id_type=BY_MESH)

    def to_line(m):
        for step in range(1, chips):
            chip_copy(m, step).wait_recv()
        for step in tuple(range(1, groups)) + (0,):
            block = place.line_at(step)
            rows = pl.ds(pl.multiple_of(block * here, here), here)
            total = kept[m % 2, rows, :]
            for other in range(1, chips):
                total = total + chip_in[m % 2, other - 1, rows, :].astype(F32)
            if step > 0:
                line_buf[m, step - 1] = total.astype(BF16)
                line_copy(m, step).start()
            else:
                line_own[m] = total
        if m + 2 < count:
            for step in range(1, chips):
                partner = place.chip_at(step)
                pl.semaphore_signal(
                    chip_free.at[step - 1], inc=1, device_id=place.chip_device(partner), device_id_type=BY_MESH
                )

    def store_grad(m):
        return pltpu.make_async_copy(line_own.at[m], grads[m], store_sem.at[m])

    def settle(m):
        total = line_own[m]
        for step in range(1, groups):
            line_copy(m, step).wait_recv()
            total = total + line_in[m, step - 1].astype(F32)
        line_own[m] = total
        store_grad(m).start()

    width = memory.shape[1]
    panels = width // panel
    piece = memory.shape[0]

    def weight_copy(slot, which, source, index):
        rows = pl.ds(pl.multiple_of(index * panel, panel), panel)
        return pltpu.make_async_copy(source.at[rows, :], weight.at[slot, which], weight_sem.at[slot, which])

    def panel_copy(slot, index):
        columns = pl.ds(pl.multiple_of(index * panel, panel), panel)
        return pltpu.make_async_copy(panel_out.at[slot], grad_memory.at[:, columns], panel_sem.at[slot])

    def back(slot, which, m):
        total = jnp.zeros((piece, panel), F32)
        for group in range(groups):
            columns = slice(group * share, (group + 1) * share)
            total = total + lax.dot_general(
                right[m % 2, group], weight[slot, which, :, columns], NT, preferred_element_type=F32
            )
        return total

    def memory_gradient():
        weight_copy(0, 0, all_value, 0).start()
        weight_copy(0, 1, all_key, 0).start()

        def one(index, _):
            slot = lax.rem(index, 2)

            @pl.when(index + 1 < panels)
            def _():
                weight_copy(1 - slot, 0, all_value, index + 1).start()
                weight_copy(1 - slot, 1, all_key, index + 1).start()

            weight_copy(slot, 0, all_value, index).wait()
            weight_copy(slot, 1, all_key, index).wait()

            @pl.when(index >= 2)
            def _():
                panel_copy(slot, index - 2).wait()

            panel_out[slot] = back(slot, 0, 1) + back(slot, 1, 2)
            panel_copy(slot, index).start()
            return 0

        lax.fori_loop(0, panels, one, 0)
        for index in range(max(panels - 2, 0), panels):
            panel_copy(index % 2, index).wait()

    def query_gradient():
        weight_copy(0, 0, all_query, 0).start()

        def one(index, _):
            slot = lax.rem(index, 2)

            @pl.when(index + 1 < panels)
            def _():
                weight_copy(1 - slot, 0, all_query, index + 1).start()

            weight_copy(slot, 0, all_query, index).wait()
            columns = pl.ds(pl.multiple_of(index * panel, panel), panel)
            grad_attn_in[:, columns] = back(slot, 0, 3)
            return 0

        lax.fori_loop(0, panels, one, 0)

    some = mid_buf.shape[1]
    batches = piece // some

    def batch_rows(index):
        return pl.ds(pl.multiple_of(index * some, some), some)

    def mid_copy(slot, index):
        return pltpu.make_async_copy(grad_mid.at[batch_rows(index), :], mid_buf.at[slot], mid_sem.at[slot])

    def hidden_copy(slot, index):
        return pltpu.make_async_copy(hidden.at[batch_rows(index), :], hidden_buf.at[slot], hidden_sem.at[slot])

    def hidden_store(index):
        rows = batch_rows(index)
        return pltpu.make_async_copy(grad_attn_in.at[rows, :], grad_hidden.at[rows, :], panel_sem.at[0])

    def hidden_gradient():
        gain_term[...] = jnp.zeros_like(gain_term)
        mid_copy(0, 0).start()
        hidden_copy(0, 0).start()

        def one(index, _):
            slot = lax.rem(index, 2)

            @pl.when(index + 1 < batches)
            def _():
                mid_copy(1 - slot, index + 1).start()
                hidden_copy(1 - slot, index + 1).start()

            mid_copy(slot, index).wait()
            hidden_copy(slot, index).wait()
            rows = batch_rows(index)
            x = hidden_buf[slot].astype(F32)
            rstd = lax.rsqrt(jnp.mean(x * x, axis=-1, keepdims=True) + EPSILON)
            normed = x * rstd
            grad = grad_attn_in[rows, :]
            gain_term[0:1, :] += jnp.sum(normed * grad, axis=0, keepdims=True)
            scaled = grad * gain_rows[0:1, :]
            shift = jnp.mean(scaled * normed, axis=-1, keepdims=True)
            grad_attn_in[rows, :] = mid_buf[slot] + rstd * (scaled - normed * shift)
            hidden_store(index).start()
            return 0

        lax.fori_loop(0, batches, one, 0)

    devices = dp_count * groups
    me = place.dp * groups + seq

    def gain_copy(step):
        owner = lax.rem(me + step, devices)
        return remote(
            gain_buf.at[owner], gain_in.at[step], gain_send, gain_recv, {"dp": owner // groups, "seq": owner % groups}
        )

    def send_gains():
        gain_term[1:2, :] = gain_ffn_term[0:1, :]
        per = 128 // here
        for owner in range(devices):
            tile = gain_term[:, owner // per * 128 : (owner // per + 1) * 128]
            shift = owner % per * here
            gain_buf[owner] = pltpu.roll(tile, 128 - shift, 1) if shift else tile

        def one(step, _):
            gain_copy(step).start()
            return 0

        lax.fori_loop(1, devices, one, 0)

    def sum_gains():
        remote(
            gain_buf.at[pl.ds(0, devices - 1)], gain_in.at[pl.ds(1, devices - 1)], gain_send, gain_recv, place.sibling
        ).wait()
        total = gain_buf[me]
        for step in range(1, devices):
            total = total + gain_in[step]
        grad_gains[...] = total

    everyone = pltpu.get_barrier_semaphore()

    def greet(step, _):
        other = lax.rem(me + step, devices)
        pl.semaphore_signal(
            everyone, inc=1, device_id={"dp": other // groups, "seq": other % groups}, device_id_type=BY_MESH
        )
        return 0

    lax.fori_loop(1, devices, greet, 0)
    pl.semaphore_wait(everyone, devices - 1)
    send_parts(1)
    load_right(0)
    to_sibling(0)
    to_chips(0)
    sent_parts(1)
    send_parts(2)
    load_right(1)
    to_sibling(1)
    to_chips(1)
    to_line(0)
    sent_parts(2)
    send_parts(3)
    load_right(2)
    to_sibling(2)
    to_chips(2)
    to_line(1)
    settle(0)
    memory_gradient()
    sent_parts(3)
    load_right(3)
    to_sibling(3)
    to_chips(3)
    to_line(2)
    settle(1)
    query_gradient()
    hidden_gradient()
    send_gains()
    to_line(3)
    settle(2)
    settle(3)
    sum_gains()
    pltpu.make_async_copy(grad_attn_in, grad_hidden, panel_sem.at[0]).wait()
    for step in range(chips):
        core_copy(3, step).wait_send()
    for m in (2, 3):
        for step in range(1, chips):
            chip_copy(m, step).wait_send()
    for m in range(count):
        for step in range(1, groups):
            line_copy(m, step).wait_send()
        store_grad(m).wait()


def reduce_call(dp_count, groups, piece, width, here):
    chips = dp_count // 2
    share = width // groups
    panel = groups * here
    hbm = pl.BlockSpec(memory_space=pl.ANY)
    vmem = pl.BlockSpec(memory_space=pltpu.VMEM)
    part = jax.ShapeDtypeStruct((groups, piece, share), BF16)
    grad = jax.ShapeDtypeStruct((here, width), F32)
    tokens = jax.ShapeDtypeStruct((piece, width), F32)
    some = min(64, piece)
    devices = dp_count * groups
    dma = pltpu.SemaphoreType.DMA
    others = max(chips - 1, 1)
    return pl.pallas_call(
        functools.partial(reduce_kernel, dp_count, groups, here),
        in_specs=[vmem] * 5 + [hbm] * 9,
        out_specs=[hbm] * 9 + [vmem],
        out_shape=(part, part, part, grad, grad, grad, grad, tokens, tokens, jax.ShapeDtypeStruct((8, 128), F32)),
        scratch_shapes=[
            pltpu.VMEM((2, groups, piece, share), BF16),
            pltpu.VMEM((chips, panel, width), BF16),
            pltpu.VMEM((2, chips, panel, width), BF16),
            pltpu.VMEM((2, others, panel, width), BF16),
            pltpu.VMEM((2, others, panel, width), BF16),
            pltpu.VMEM((2, panel, width), F32),
            pltpu.VMEM((4, groups - 1, here, width), BF16),
            pltpu.VMEM((4, groups - 1, here, width), BF16),
            pltpu.VMEM((4, here, width), F32),
            dma((4, groups - 1)), dma((4, groups - 1)), dma((4,)), dma((groups,)),
            dma((chips,)), dma((2, chips)),
            dma((2, others)), dma((2, others)),
            dma((4, groups - 1)), dma((4, groups - 1)), dma((4,)),
            pltpu.SemaphoreType.REGULAR, pltpu.SemaphoreType.REGULAR((others,)),
            pltpu.VMEM((2, 2, panel, width), BF16),
            pltpu.VMEM((2, piece, panel), F32),
            pltpu.VMEM((piece, width), F32),
            pltpu.VMEM((2, some, width), F32),
            pltpu.VMEM((2, some, width), BF16),
            pltpu.VMEM((8, width), F32),
            pltpu.VMEM((devices, 8, 128), F32),
            pltpu.VMEM((devices, 8, 128), F32),
            dma((2, 2)), dma((2,)), dma((2,)), dma((2,)), dma, dma,
        ],
        compiler_params=pltpu.CompilerParams(
            collective_id=2, has_side_effects=True, vmem_limit_bytes=63 * 1024 * 1024
        ),
        cost_estimate=pl.CostEstimate(
            flops=128 * piece * width * width, transcendentals=0, bytes_accessed=16 * width * width
        ),
        name="weight_gradients",
    )


def middle_kernel(
    dp_count, groups,
    gain_rows, hidden, context_heads, grad_own, out_rows, gate_rows, up_rows, down_rows, all_grad,
    context, gain_term, mid_out, grad_mid, grad_branch, grad_heads, branch, grad_down, grad_gate, grad_up,
    all_ffn, grad_acts, acts, grad_gates, grad_ups, core_in, chip_in, term_in,
    gate_w, up_w, down_w, out_w, mid, ffn_in, own_total, chip_out, term_buf,
    col_send, col_recv, col_own, weight_sem, out_sem, mid_sem, chip_send, chip_recv, core_send, core_recv, own_sem,
    x_sem, dy_sem, act_sem, sum_send, sum_recv, load_sem, far_send, far_recv, left_sem, right_sem, branch_sem,
    term_send, term_recv, rows_sem, gm_sem, gb_sem, head_send, head_recv, head_own,
):
    place = Place(dp_count, groups)
    chips, seq, core = place.chips, place.seq, place.core
    piece, width = hidden.shape
    share = width // groups
    unit_rows = gate_rows.shape[0]
    padded = gate_w.shape[0]
    wide = (gate_rows, up_rows, down_rows)
    kept = (gate_w, up_w, down_w)

    def weight_copy(i):
        return pltpu.make_async_copy(wide[i], kept[i].at[pl.ds(0, unit_rows), :], weight_sem.at[i])

    def group_columns(group):
        return pl.ds(pl.multiple_of(group * share, share), share)

    def out_copy(group, slot):
        rows = pl.ds(pl.multiple_of(group * share, share), share)
        return pltpu.make_async_copy(out_rows.at[rows, :], out_w.at[slot], out_sem.at[slot])

    def collect(step):
        other = place.line_at(step)
        return remote(
            context_heads.at[other], context.at[:, group_columns(seq)], col_send.at[step - 1], col_recv.at[step - 1],
            place.line_device(other),
        )

    def came_from(step):
        return lax.rem(seq + groups - step, groups)

    place.barrier()
    for step in range(1, groups):
        collect(step).start()
    own_columns = pltpu.make_async_copy(context_heads.at[seq], context.at[:, group_columns(seq)], col_own)
    own_columns.start()
    out_copy(seq, 0).start()
    hidden_copy = pltpu.make_async_copy(hidden, ffn_in, own_sem)
    hidden_copy.start()
    for i in range(3):
        weight_copy(i).start()
        if padded > unit_rows:
            kept[i][unit_rows:, :] = jnp.zeros((padded - unit_rows, width), BF16)

    def act_gradients(dy_buf, out_buf):
        def dy_copy(dp, slot):
            return pltpu.make_async_copy(all_grad.at[dp], dy_buf.at[slot], dy_sem.at[slot])

        def store(dp, slot):
            return pltpu.make_async_copy(out_buf.at[slot], grad_acts.at[dp], act_sem.at[slot, 0])

        dy_copy(0, 0).start()
        weight_copy(2).wait()

        def one(dp, _):
            slot = dp % 2

            @pl.when(dp + 1 < dp_count)
            def _():
                dy_copy(dp + 1, 1 - slot).start()

            dy_copy(dp, slot).wait()

            @pl.when(dp >= 2)
            def _():
                store(dp - 2, slot).wait()

            out_buf[slot] = mxu(dy_buf[slot], down_w[...], NT)
            store(dp, slot).start()
            return 0

        lax.fori_loop(0, dp_count, one, 0)
        for dp in range(dp_count - 2, dp_count):
            store(dp, dp % 2).wait()

    pl.run_scoped(act_gradients, pltpu.VMEM((2, piece, width), BF16), pltpu.VMEM((2, piece, padded), F32))

    for step in range(groups):
        slot = step % 2
        group = came_from(step)
        if step + 1 < groups:
            out_copy(came_from(step + 1), 1 - slot).start()
        if step == 0:
            own_columns.wait()
        else:
            columns = context.at[:, group_columns(group)]
            remote(columns, columns, col_send.at[step - 1], col_recv.at[step - 1], place.sibling).wait_recv()
        out_copy(group, slot).wait()
        left = context[:, group_columns(group)]
        if step == 0:
            hidden_copy.wait()

        def project(part, _, left=left, slot=slot, step=step):
            columns = pl.ds(pl.multiple_of(part * share, share), share)
            value = mxu(left, out_w[slot, :, columns], NN)
            if step == 0:
                mid[:, columns] = ffn_in[:, columns].astype(F32) + value
            else:
                mid[:, columns] += value
            return 0

        lax.fori_loop(0, groups, project, 0)

    some = min(64, piece)
    batches = piece // some

    def batch(index):
        return pl.ds(pl.multiple_of(index * some, some), some)

    def normalize(index, _):
        rows = batch(index)
        x = mid[rows, :]
        rstd = lax.rsqrt(jnp.mean(x * x, axis=-1, keepdims=True) + EPSILON)
        ffn_in[rows, :] = (x * rstd * gain_rows[1:2, :]).astype(BF16)
        return 0

    lax.fori_loop(0, batches, normalize, 0)
    mid_copy = pltpu.make_async_copy(mid, mid_out, mid_sem)
    mid_copy.start()

    def to_chip(step):
        return remote(
            ffn_in, all_ffn.at[place.dp], chip_send.at[step - 1], chip_recv.at[step - 1],
            place.chip_device(place.chip_at(step)),
        )

    def to_sibling(step):
        dp = 2 * place.chip_at(step) + core
        return remote(all_ffn.at[dp], all_ffn.at[dp], core_send.at[step], core_recv.at[step], place.sibling)

    own_ffn = pltpu.make_async_copy(ffn_in, all_ffn.at[place.dp], own_sem)
    own_ffn.start()
    square = chips == 4
    for step in range(1, 3 if square else chips):
        to_chip(step).start()
    own_ffn.wait()
    to_sibling(0).start()
    for i in range(2):
        weight_copy(i).wait()

    def hand_on(step):
        half = piece // 2
        dp = 2 * place.chip_at(step) + core
        rows = all_ffn.at[dp, pl.ds((step - 1) * half, half), :]
        return remote(rows, rows, chip_send.at[2], chip_recv.at[2], place.chip_device(place.chip_at(3 - step)))

    pieces = 2 * chips
    stored = (acts, grad_gates, grad_ups)

    def piece_of(u, own_first):
        step, which = u // 2, u % 2
        mine = 1 - which if own_first else which
        return step, which, 2 * place.chip_at(step) + mine * core + (1 - mine) * (1 - core)

    def hidden_units(x_buf, da_buf, act_buf):
        def x_copy(u):
            dp = piece_of(u, True)[2]
            return pltpu.make_async_copy(all_ffn.at[dp], x_buf.at[u % 2], x_sem.at[u % 2])

        def da_copy(u):
            dp = piece_of(u, True)[2]
            return pltpu.make_async_copy(grad_acts.at[dp], da_buf.at[u % 2], dy_sem.at[u % 2])

        def act_copy(u, i):
            dp = piece_of(u, True)[2]
            return pltpu.make_async_copy(act_buf.at[u % 2, i], stored[i].at[dp], act_sem.at[u % 2, i])

        def fetch(u):
            step, which, _ = piece_of(u, True)
            if square:

                @pl.when(u == 2)
                def _():
                    for near in (1, 2):
                        to_chip(near).wait_recv()
                        to_sibling(near).start()
                        hand_on(near).start()

                @pl.when(u == 6)
                def _():
                    to_chip(3).wait_recv()
                    to_sibling(3).start()

            else:

                @pl.when((which == 0) & (step > 0))
                def _():
                    to_chip(step).wait_recv()
                    to_sibling(step).start()

            @pl.when(which == 1)
            def _():
                to_sibling(step).wait_recv()

            x_copy(u).start()

        da_copy(0).start()

        def one(u, _):
            slot = u % 2
            ahead = u % 2 == 1
            if square:
                ahead = ahead | (u == 4)
            next_ahead = (u + 1 < pieces) & (u % 2 == 0)
            if square:
                next_ahead = next_ahead | (u == 3)

            @pl.when(jnp.logical_not(ahead))
            def _():
                fetch(u)

            @pl.when(next_ahead)
            def _():
                fetch(u + 1)

            @pl.when(u + 1 < pieces)
            def _():
                da_copy(u + 1).start()

            @pl.when(u >= 2)
            def _():
                for i in range(3):
                    act_copy(u - 2, i).wait()

            x_copy(u).wait()
            gate = mxu(x_buf[slot], gate_w[...], NT)
            up = mxu(x_buf[slot], up_w[...], NT)
            sig = 1.0 / (1.0 + jnp.exp(-gate))
            da_copy(u).wait()
            grad_act = da_buf[slot]
            act_buf[slot, 0] = (gate * sig * up).astype(BF16)
            act_buf[slot, 1] = (grad_act * up * sig * (1.0 + gate * (1.0 - sig))).astype(BF16)
            act_buf[slot, 2] = (grad_act * gate * sig).astype(BF16)
            for i in range(3):
                act_copy(u, i).start()
            return 0

        lax.fori_loop(0, pieces, one, 0)
        for u in range(max(pieces - 2, 0), pieces):
            for i in range(3):
                act_copy(u, i).wait()

    pl.run_scoped(
        hidden_units,
        pltpu.VMEM((2, piece, width), BF16), pltpu.VMEM((2, piece, padded), F32),
        pltpu.VMEM((2, 3, piece, padded), BF16),
    )

    def far_copy(step):
        return remote(
            chip_out.at[step - 1], chip_in.at[step - 1], far_send.at[step - 1],
            far_recv.at[step - 1], place.chip_device(place.chip_at(step)),
        )

    def input_sum(act_buf, core_out, load_buf):
        sources, rights, own = (grad_gates, grad_ups), (gate_w, up_w), own_total
        used = len(sources)

        def place_of(u):
            _, which, dp = piece_of(pieces - 2 + u - 4 * (u // 2), False)
            return chips - 1 - u // 2, which, dp

        def act_copy(u, i):
            dp = place_of(u)[2]
            return pltpu.make_async_copy(sources[i].at[dp], act_buf.at[u % 2, i], act_sem.at[u % 2, i])

        def sum_copy(step):
            return remote(
                core_out, core_in.at[step], sum_send, sum_recv.at[step], place.sibling
            )

        def load_copy(step):
            return pltpu.make_async_copy(core_in.at[step], load_buf, load_sem)

        for i in range(used):
            act_copy(0, i).start()

        def one(u, _):
            step, which, dp = place_of(u)
            slot = u % 2

            @pl.when(u + 1 < pieces)
            def _():
                for i in range(used):
                    act_copy(u + 1, i).start()

            for i in range(used):
                act_copy(u, i).wait()

            @pl.when((which == 0) & (u >= 2))
            def _():
                sum_copy(step + 1).wait_send()

            @pl.when(which == 1)
            def _():
                sum_copy(step).wait_recv()
                load_copy(step).start()
                load_copy(step).wait()

            def columns_of(part, _):
                columns = group_columns(part)
                value = mxu(act_buf[slot, 0], rights[0][:, columns], NN)
                for i in range(1, used):
                    value = value + mxu(act_buf[slot, i], rights[i][:, columns], NN)

                @pl.when(which == 0)
                def _():
                    core_out[:, columns] = value.astype(BF16)

                @pl.when((which == 1) & (step > 0))
                def _():
                    chip_out[step - 1, :, columns] = (value + load_buf[:, columns].astype(F32)).astype(BF16)

                @pl.when((which == 1) & (step == 0))
                def _():
                    own[:, columns] = value + load_buf[:, columns].astype(F32)

                return 0

            lax.fori_loop(0, groups, columns_of, 0)

            @pl.when(which == 0)
            def _():
                sum_copy(step).start()

            @pl.when((which == 1) & (step > 0))
            def _():
                far_copy(step).start()

            return 0

        lax.fori_loop(0, pieces, one, 0)
        sum_copy(0).wait_send()

    block = unit_rows // groups

    paired = groups == 4
    side = seq // 2
    inner = (seq == 1) | (seq == 2)
    partner = seq + 1 - 2 * (seq % 2)

    def across(j):
        return 2 * (1 - side) + j

    def term_rows(i, owner):
        return term_buf.at[i, pl.ds(pl.multiple_of(owner * block, block), block), :]

    def term_copy(i, step):
        other = place.line_at(step)
        return remote(
            term_rows(i, other), term_in.at[i, step - 1], term_send.at[i, step - 1], term_recv.at[i, step - 1],
            place.line_device(other),
        )

    def near_copy(i):
        return remote(
            term_rows(i, partner), term_in.at[i, 0], term_send.at[i, 0], term_recv.at[i, 0], place.line_device(partner)
        )

    def relay_copy(i, j):
        return remote(
            term_rows(i, across(j)), term_in.at[i, 2 + j], term_send.at[i, 1 + j], term_recv.at[i, 2 + j],
            place.line_device(partner),
        )

    def across_copy(i, j):
        return remote(
            term_rows(i, across(j)), term_in.at[i, 1], term_send.at[i, 1 + j], term_recv.at[i, 1],
            place.line_device(across(j)),
        )

    def send_term(i):
        if paired:
            near_copy(i).start()

            @pl.when(jnp.logical_not(inner))
            def _():
                for j in range(2):
                    relay_copy(i, j).start()

        else:
            for step in range(1, groups):
                term_copy(i, step).start()

    def relay_term(i, buf):
        if not paired:
            return

        @pl.when(inner)
        def _():
            for j in range(2):
                relay_copy(i, j).wait_recv()
                load = pltpu.make_async_copy(term_in.at[i, 2 + j], buf, left_sem.at[0])
                load.start()
                load.wait()
                rows = pl.ds(pl.multiple_of(across(j) * block, block), block)
                term_buf[i, rows, :] = (term_buf[i, rows, :].astype(F32) + buf[...].astype(F32)).astype(BF16)
                across_copy(i, j).start()

    def arrived_terms(i):
        if not paired:
            for step in range(1, groups):
                term_copy(i, step).wait()
            return range(groups - 1)
        near_copy(i).wait()
        across_copy(i, 0).wait_recv()
        for j in range(2):
            across_copy(i, j).wait_send()
        return range(2)

    def weight_terms(left_buf, acc):
        for i, (lefts, rights) in enumerate(((acts, all_grad), (grad_gates, all_ffn), (grad_ups, all_ffn))):

            def copies(dp, slot, lefts=lefts, rights=rights):
                return (
                    pltpu.make_async_copy(lefts.at[dp], left_buf.at[slot], left_sem.at[slot]),
                    pltpu.make_async_copy(rights.at[dp], out_w.at[slot], right_sem.at[slot]),
                )

            for copy in copies(0, 0):
                copy.start()

            def one(dp, _, copies=copies):
                slot = dp % 2

                @pl.when(dp + 1 < dp_count)
                def _():
                    for copy in copies(dp + 1, 1 - slot):
                        copy.start()

                for copy in copies(dp, slot):
                    copy.wait()
                left = left_buf[slot].T


                @pl.when(dp == 0)
                def _():
                    acc[...] = jnp.zeros_like(acc)

                acc[...] += jnp.dot(left, out_w[slot], preferred_element_type=F32)
                return 0

            lax.fori_loop(0, dp_count, one, 0)
            term_buf[i] = acc[0:unit_rows, :].astype(BF16)
            send_term(i)

    pl.run_scoped(weight_terms, pltpu.VMEM((2, piece, padded), BF16), pltpu.VMEM((padded, width), F32))

    pl.run_scoped(
        input_sum,
        pltpu.VMEM((2, 2, piece, padded), BF16), pltpu.VMEM((piece, width), BF16), pltpu.VMEM((piece, width), BF16),
    )

    def branch_parts(relay_buf, act_buf, branch_buf):
        relay_term(0, relay_buf)

        def act_copy(dp, slot):
            return pltpu.make_async_copy(acts.at[dp], act_buf.at[slot], act_sem.at[slot, 0])

        def branch_copy(dp, slot):
            return pltpu.make_async_copy(branch_buf.at[slot], branch.at[dp], branch_sem.at[slot])

        act_copy(0, 0).start()

        def one(dp, _):
            slot = dp % 2

            @pl.when(dp + 1 < dp_count)
            def _():
                act_copy(dp + 1, 1 - slot).start()

            act_copy(dp, slot).wait()

            @pl.when(dp >= 2)
            def _():
                branch_copy(dp - 2, slot).wait()

            def part_of(part, _):
                columns = group_columns(part)
                branch_buf[slot, :, columns] = mxu(act_buf[slot], down_w[:, columns], NN).astype(BF16)
                return 0

            lax.fori_loop(0, groups, part_of, 0)
            branch_copy(dp, slot).start()
            return 0

        lax.fori_loop(0, dp_count, one, 0)
        for dp in range(dp_count - 2, dp_count):
            branch_copy(dp, dp % 2).wait()
        relay_term(1, relay_buf)

    pl.run_scoped(
        branch_parts,
        pltpu.VMEM((block, width), BF16), pltpu.VMEM((2, piece, padded), BF16), pltpu.VMEM((2, piece, width), BF16),
    )

    for step in range(1, chips):
        landed = chip_in.at[step - 1]
        remote(landed, landed, far_send.at[step - 1], far_recv.at[step - 1], place.sibling).wait_recv()
    for step in range(1, chips):
        to_chip(step).wait_send()
    mid_copy.wait()
    gain_term[...] = jnp.zeros_like(gain_term)

    def norm_and_heads(rows_buf, mid_buf, heads_buf, sum_buf):
        def rows_copy(index, step, slot):
            source = grad_own.at[batch(index), :] if step == 0 else chip_in.at[step - 1, batch(index), :]
            return pltpu.make_async_copy(source, rows_buf.at[slot, step], rows_sem.at[slot, step])

        def grad_mid_copy(index, slot):
            return pltpu.make_async_copy(mid_buf.at[slot], grad_mid.at[batch(index), :], gm_sem.at[slot])

        for step in range(chips):
            rows_copy(0, step, 0).start()

        def norm_back(index, _):
            slot = index % 2

            @pl.when(index + 1 < batches)
            def _():
                for step in range(chips):
                    rows_copy(index + 1, step, 1 - slot).start()

            for step in range(chips):
                rows_copy(index, step, slot).wait()

            @pl.when(index >= 2)
            def _():
                grad_mid_copy(index - 2, slot).wait()

            rows = batch(index)
            grad = own_total[rows, :]
            for step in range(1, chips):
                grad = grad + rows_buf[slot, step].astype(F32)
            x = mid[rows, :]
            rstd = lax.rsqrt(jnp.mean(x * x, axis=-1, keepdims=True) + EPSILON)
            normed = x * rstd
            gain_term[0:1, :] += jnp.sum(normed * grad, axis=0, keepdims=True)
            scaled = grad * gain_rows[1:2, :]
            shift = jnp.mean(scaled * normed, axis=-1, keepdims=True)
            total = rows_buf[slot, 0].astype(F32) + rstd * (scaled - normed * shift)
            mid_buf[slot] = total
            ffn_in[rows, :] = total.astype(BF16)
            grad_mid_copy(index, slot).start()
            return 0

        lax.fori_loop(0, batches, norm_back, 0)
        grad_branch_copy = pltpu.make_async_copy(ffn_in, grad_branch, gb_sem)
        grad_branch_copy.start()
        for index in range(max(batches - 2, 0), batches):
            grad_mid_copy(index, index % 2).wait()

        def head_copy(step):
            other = place.line_at(step)
            return remote(
                heads_buf.at[other], grad_heads.at[seq], head_send.at[step - 1], head_recv.at[step - 1],
                place.line_device(other),
            )

        own_heads = pltpu.make_async_copy(heads_buf.at[seq], grad_heads.at[seq], head_own)
        order = tuple(range(1, groups)) + (0,)
        out_copy(place.line_at(order[0]), 0).start()
        for at, step in enumerate(order):
            group = place.line_at(step)
            if at + 1 < groups:
                out_copy(place.line_at(order[at + 1]), (at + 1) % 2).start()
            out_copy(group, at % 2).wait()
            heads_buf[group] = mxu(ffn_in[...], out_w[at % 2], NT).astype(BF16)
            if step > 0:
                head_copy(step).start()
            else:
                own_heads.start()

        relay_term(2, sum_buf.at[0])

        for i, target in enumerate((grad_down, grad_gate, grad_up)):
            landed = arrived_terms(i)
            for j in landed:
                load = pltpu.make_async_copy(term_in.at[i, j], sum_buf.at[j], rows_sem.at[0, 0])
                load.start()
                load.wait()
            total = term_buf[i, pl.ds(pl.multiple_of(seq * block, block), block), :].astype(F32)
            for j in landed:
                total = total + sum_buf[j].astype(F32)
            mid[0:block, :] = total
            store = pltpu.make_async_copy(mid.at[pl.ds(0, block), :], target, gm_sem.at[0])
            store.start()
            store.wait()
        grad_branch_copy.wait()
        own_heads.wait()
        for step in range(1, groups):
            head_copy(step).wait()

    pl.run_scoped(
        norm_and_heads,
        pltpu.VMEM((2, chips, some, width), BF16), pltpu.VMEM((2, some, width), F32),
        pltpu.VMEM((groups, piece, share), BF16), pltpu.VMEM((groups - 1, block, width), BF16),
    )
    for step in range(1, groups):
        collect(step).wait_send()
    for step in range(chips):
        to_sibling(step).wait_send()
    for step in range(1, chips):
        far_copy(step).wait_send()


def middle_call(dp_count, groups, piece, width, unit_rows):
    chips = dp_count // 2
    share = width // groups
    assert share == piece
    padded = -(-unit_rows // 128) * 128
    block = unit_rows // groups
    others = max(chips - 1, 1)
    hbm = pl.BlockSpec(memory_space=pl.ANY)
    vmem = pl.BlockSpec(memory_space=pltpu.VMEM)
    dma = pltpu.SemaphoreType.DMA
    shape = jax.ShapeDtypeStruct
    return pl.pallas_call(
        functools.partial(middle_kernel, dp_count, groups),
        in_specs=[vmem] + [hbm] * 8,
        out_specs=[vmem, vmem] + [hbm] * 16,
        out_shape=(
            shape((piece, width), BF16),
            shape((8, width), F32),
            shape((piece, width), F32),
            shape((piece, width), F32),
            shape((piece, width), BF16),
            shape((groups, piece, share), BF16),
            shape((dp_count, piece, width), BF16),
            shape((block, width), F32),
            shape((block, width), F32),
            shape((block, width), F32),
            shape((dp_count, piece, width), BF16),
            shape((dp_count, piece, padded), F32),
            shape((dp_count, piece, padded), BF16),
            shape((dp_count, piece, padded), BF16),
            shape((dp_count, piece, padded), BF16),
            shape((chips, piece, width), BF16),
            shape((others, piece, width), BF16),
            shape((3, max(groups - 1, 4), block, width), BF16),
        ),
        scratch_shapes=[
            pltpu.VMEM((padded, width), BF16), pltpu.VMEM((padded, width), BF16), pltpu.VMEM((padded, width), BF16),
            pltpu.VMEM((2, share, width), BF16),
            pltpu.VMEM((piece, width), F32),
            pltpu.VMEM((piece, width), BF16),
            pltpu.VMEM((piece, width), F32),
            pltpu.VMEM((others, piece, width), BF16),
            pltpu.VMEM((3, unit_rows, width), BF16),
            dma((groups - 1,)), dma((groups - 1,)), dma, dma((3,)), dma((2,)), dma,
            dma((others,)), dma((others,)), dma((chips,)), dma((chips,)), dma,
            dma((2,)), dma((2,)), dma((2, 3)),
            dma, dma((chips,)), dma, dma((others,)), dma((others,)),
            dma((2,)), dma((2,)), dma((2,)), dma((3, max(groups - 1, 4))), dma((3, max(groups - 1, 4))),
            dma((2, chips)), dma((2,)), dma,
            dma((groups - 1,)), dma((groups - 1,)), dma,
        ],
        compiler_params=pltpu.CompilerParams(
            collective_id=5, has_side_effects=True, vmem_limit_bytes=63 * 1024 * 1024
        ),
        cost_estimate=pl.CostEstimate(
            flops=128 * piece * width * width, transcendentals=0, bytes_accessed=64 * width * width
        ),
        name="feed_forward",
    )


def shards(
    hidden_in, memory, segments, gain_attn, w_query, w_key, w_value, w_out, gain_ffn, w_gate, w_up, w_down, cotangent
):
    seqs, piece, width = hidden_in.shape
    groups = lax.axis_size("seq")
    dp_count = lax.axis_size("dp")
    assert seqs == 1
    length = piece * groups
    share = width // groups
    heads = share // HEAD_DIM
    here = w_query.shape[0]
    block = min(512, length)
    tokens = hidden_in.reshape(piece, width)
    mem = memory.reshape(piece, width)
    grad_out = cotangent.reshape(piece, width)

    attend_forward, attend_backward = attention_calls(length, heads, block)
    start, low, high = document_bounds(segments[0], block)
    flat = (length, share)
    split = (groups, piece, share)

    units = w_gate.shape[0]
    padded = -(-units // 16) * 16
    own_units = [jnp.pad(weight, ((0, padded - units), (0, 0))) for weight in (w_gate, w_up, w_down)]
    (
        attn_in, gain_rows, key, value, query, _, key_rows, value_rows, query_rows, out_rows,
        gate_rows, up_rows, down_rows, dy,
    ) = project_call(dp_count, groups, piece, width, here, padded, 1)(
        tokens, mem, gain_tile(gain_attn, gain_ffn), w_key, w_value, w_query, w_out, *own_units, grad_out
    )
    gate_rows, up_rows, down_rows = [
        rows.reshape(groups * padded, width) for rows in (gate_rows, up_rows, down_rows)
    ]
    key, value, query = [part.reshape(flat) for part in (key, value, query)]
    key_rows, value_rows, query_rows, out_rows = [
        rows.reshape(width, width) for rows in (key_rows, value_rows, query_rows, out_rows)
    ]
    context_heads, lse = attend_forward(low, start, query, key, value)
    (
        context, gain_term, mid, grad_mid, grad_branch, grad_context_heads, branch, grad_w_down, grad_w_gate, grad_w_up, *_
    ) = middle_call(dp_count, groups, piece, width, groups * padded)(
        gain_rows, tokens, context_heads.reshape(split), grad_out, out_rows, gate_rows, up_rows, down_rows,
        dy.reshape(dp_count, piece, width),
    )
    branch = lax.psum_scatter(branch.reshape(dp_count * piece, width), "dp", scatter_dimension=0, tiled=True)
    grad_context_heads = grad_context_heads.reshape(flat)
    dq, dk, dv = attend_backward(high, start, query, key, value, context_heads, grad_context_heads, lse)

    _, _, _, grad_w_out, grad_w_value, grad_w_key, grad_w_query, grad_memory, grad_hidden, gains = reduce_call(
        dp_count, groups, piece, width, here
    )(
        context, mem, attn_in, gain_rows, gain_term, grad_branch, dv.reshape(split), dk.reshape(split),
        dq.reshape(split), value_rows, key_rows, query_rows, tokens, grad_mid,
    )
    gains, branch, mid = lax.optimization_barrier((gains, branch, mid))
    grad_w_down, grad_w_gate, grad_w_up = [grad[:units] for grad in (grad_w_down, grad_w_gate, grad_w_up)]
    layer_out = (mid + branch.astype(F32)).astype(BF16)
    grad_gain_attn, grad_gain_ffn = gains[0, :here], gains[1, :here]
    cube = (seqs, piece, width)
    return (
        layer_out.reshape(cube),
        grad_hidden.reshape(cube),
        grad_memory.reshape(cube),
        grad_gain_attn,
        grad_w_query,
        grad_w_key,
        grad_w_value,
        grad_w_out,
        grad_gain_ffn,
        grad_w_gate,
        grad_w_up,
        grad_w_down,
    )


def solution(mesh):
    tokens = P("dp", "seq", None)
    rows = P(ALL, None)
    gain = P(ALL)
    in_specs = (tokens, tokens, P("dp", None), gain, rows, rows, rows, rows, gain, rows, rows, rows, tokens)
    out_specs = (tokens, tokens, tokens, gain, rows, rows, rows, rows, gain, rows, rows, rows)
    return jax.shard_map(shards, mesh=mesh, in_specs=in_specs, out_specs=out_specs, check_vma=False)
```

```python
import functools
import math

import jax
import jax.numpy as jnp
from jax import lax
from jax.experimental import pallas as pl
from jax.experimental.pallas import tpu as pltpu
from jax.sharding import PartitionSpec as P

HEAD_DIM = 128
DOCS = 4
EPSILON = 1e-06
MASKED = -1e30
ALL = ("dp", "seq")
F32 = jnp.float32
BF16 = jnp.bfloat16
EXP2_SCALE = HEAD_DIM ** (-0.5) * math.log2(math.e)
NT = (((1,), (1,)), ((), ()))
TN = (((0,), (0,)), ((), ()))
NN = (((1,), (0,)), ((), ()))
BY_MESH = pl.DeviceIdType.MESH


def mxu(left, right, dims):
    return lax.dot_general(left, right, dims, preferred_element_type=F32)


def rms_scale(values):
    return lax.rsqrt(jnp.mean(values * values, axis=-1, keepdims=True) + EPSILON)


def norm_back(grad_normed, normed, rstd, gain):
    scaled = grad_normed * gain
    return rstd * (scaled - normed * jnp.mean(scaled * normed, axis=-1, keepdims=True))


def forward_kernel(block, low_ref, start_ref, q_ref, k_ref, v_ref, out_ref, lse_ref):
    length = q_ref.shape[0]

    def one_query_block(qb, _):
        q0 = pl.multiple_of(qb * block, block)
        rows = pl.ds(q0, block)
        query = q_ref[rows, :]
        start = start_ref[:, rows]
        query_pos = q0 + lax.broadcasted_iota(jnp.int32, (block, block), 1)

        def one_key_block(kb, carry):
            top, total, acc = carry
            k0 = pl.multiple_of(kb * block, block)
            keys = pl.ds(k0, block)
            score = mxu(k_ref[keys, :], query, NT)
            key_pos = k0 + lax.broadcasted_iota(jnp.int32, (block, block), 0)
            score = jnp.where((key_pos >= start) & (key_pos <= query_pos), score, MASKED)
            new_top = jnp.maximum(top, jnp.max(score, axis=0, keepdims=True))
            shrink = jnp.exp2((top - new_top) * EXP2_SCALE)
            raised = jnp.exp2((score - new_top) * EXP2_SCALE)
            total = total * shrink + jnp.sum(raised, axis=0, keepdims=True)
            acc = acc * shrink + mxu(v_ref[keys, :], raised.astype(BF16), TN)
            return new_top, total, acc

        top, total, acc = lax.fori_loop(
            low_ref[qb],
            qb + 1,
            one_key_block,
            (
                jnp.full((1, block), MASKED, F32),
                jnp.zeros((1, block), F32),
                jnp.zeros((HEAD_DIM, block), F32),
            ),
        )
        out_ref[rows, :] = (acc / total).T.astype(BF16)
        lse_ref[0, :, rows] = top * EXP2_SCALE + jnp.log2(total)
        return 0

    lax.fori_loop(0, length // block, one_query_block, 0)


def backward_kernel(
    block, high_ref, start_ref, q_ref, k_ref, v_ref, ctx_ref, grad_ref, lse_ref,
    dq_ref, dk_ref, dv_ref, dq_acc, delta_acc,
):
    length = q_ref.shape[0]
    blocks = length // block
    scale = HEAD_DIM ** (-0.5)
    dq_acc[...] = jnp.zeros_like(dq_acc)

    def one_delta(qb, _):
        rows = pl.ds(pl.multiple_of(qb * block, block), block)
        both = ctx_ref[rows, :].astype(F32) * grad_ref[rows, :].astype(F32)
        delta_acc[:, rows] = jnp.sum(both.T, axis=0, keepdims=True)
        return 0

    lax.fori_loop(0, blocks, one_delta, 0)

    def one_key_block(kb, _):
        k0 = pl.multiple_of(kb * block, block)
        keys = pl.ds(k0, block)
        key = k_ref[keys, :]
        value = v_ref[keys, :]
        key_pos = k0 + lax.broadcasted_iota(jnp.int32, (block, block), 0)

        def one_query_block(qb, carry):
            dk, dv = carry
            q0 = pl.multiple_of(qb * block, block)
            rows = pl.ds(q0, block)
            query = q_ref[rows, :]
            grad = grad_ref[rows, :]
            start = start_ref[:, rows]
            query_pos = q0 + lax.broadcasted_iota(jnp.int32, (block, block), 1)
            score = mxu(key, query, NT)
            prob = jnp.exp2(score * EXP2_SCALE - lse_ref[0, :, rows])
            prob = jnp.where((key_pos >= start) & (key_pos <= query_pos), prob, 0.0)
            grad_prob = mxu(value, grad, NT)
            grad_score = (prob * (grad_prob - delta_acc[:, rows])).astype(BF16)
            dv = dv + mxu(prob.astype(BF16), grad, NN)
            dk = dk + mxu(grad_score, query, NN)
            dq_acc[rows, :] += mxu(grad_score, key, TN)
            return dk, dv

        zeros = jnp.zeros((block, HEAD_DIM), F32)
        dk, dv = lax.fori_loop(kb, high_ref[kb], one_query_block, (zeros, zeros))
        dk_ref[keys, :] = (dk * scale).astype(BF16)
        dv_ref[keys, :] = dv.astype(BF16)
        return 0

    lax.fori_loop(0, blocks, one_key_block, 0)
    dq_ref[...] = (dq_acc[...] * scale).astype(BF16)


def attention_calls(length, heads, block):
    column = pl.BlockSpec((length, HEAD_DIM), lambda h, *_: (0, h))
    row = pl.BlockSpec((1, length), lambda h, *_: (0, 0))
    stat = pl.BlockSpec((1, 1, length), lambda h, *_: (h, 0, 0))
    flat = jax.ShapeDtypeStruct((length, heads * HEAD_DIM), BF16)
    pairs = heads * length * length // 4
    forward = pl.pallas_call(
        functools.partial(forward_kernel, block),
        grid_spec=pltpu.PrefetchScalarGridSpec(
            num_scalar_prefetch=1,
            grid=(heads,),
            in_specs=[row, column, column, column],
            out_specs=[column, stat],
        ),
        out_shape=(flat, jax.ShapeDtypeStruct((heads, 1, length), F32)),
        cost_estimate=pl.CostEstimate(
            flops=64 * pairs * HEAD_DIM, transcendentals=pairs, bytes_accessed=8 * length * heads * HEAD_DIM
        ),
        name="attend_forward",
    )
    backward = pl.pallas_call(
        functools.partial(backward_kernel, block),
        grid_spec=pltpu.PrefetchScalarGridSpec(
            num_scalar_prefetch=1,
            grid=(heads,),
            in_specs=[row, column, column, column, column, column, stat],
            out_specs=[column, column, column],
            scratch_shapes=[pltpu.VMEM((length, HEAD_DIM), F32), pltpu.VMEM((1, length), F32)],
        ),
        out_shape=(flat, flat, flat),
        cost_estimate=pl.CostEstimate(
            flops=96 * pairs * HEAD_DIM, transcendentals=pairs, bytes_accessed=16 * length * heads * HEAD_DIM
        ),
        name="attend_backward",
    )
    return forward, backward


def document_bounds(segment_ids, block):
    first = jnp.zeros_like(segment_ids)
    last = jnp.zeros_like(segment_ids)
    for number in range(DOCS):
        below = jnp.sum((segment_ids < number).astype(jnp.int32))
        upto = jnp.sum((segment_ids <= number).astype(jnp.int32))
        first = jnp.where(segment_ids == number, below, first)
        last = jnp.where(segment_ids == number, upto - 1, last)
    low = first[::block] // block
    high = last[block - 1 :: block] // block + 1
    return first[None, :], low, high


def remote(src, dst, send, recv, device):
    return pltpu.make_async_remote_copy(
        src_ref=src, dst_ref=dst, send_sem=send, recv_sem=recv, device_id=device, device_id_type=BY_MESH
    )


class Place:
    def __init__(self, dp_count, groups):
        self.groups = groups
        self.chips = dp_count // 2
        self.dp = lax.axis_index("dp")
        self.seq = lax.axis_index("seq")
        self.core = lax.rem(self.dp, 2)
        self.chip = self.dp // 2
        self.sibling = {"dp": self.dp + 1 - 2 * self.core, "seq": self.seq}

    def chip_at(self, step):
        chip, bit = self.chip, 1
        while bit < self.chips:
            chip = chip + (step // bit % 2) * bit * (1 - 2 * lax.rem(self.chip // bit, 2))
            bit *= 2
        return chip

    def chip_device(self, chip):
        return {"dp": 2 * chip + self.core, "seq": self.seq}

    def line_at(self, step):
        return lax.rem(self.seq + step, self.groups)

    def line_device(self, seq):
        return {"dp": self.dp, "seq": seq}

    def barrier(self):
        everyone = pltpu.get_barrier_semaphore()
        for step in range(1, self.groups):
            pl.semaphore_signal(everyone, inc=1, device_id=self.line_device(self.line_at(step)), device_id_type=BY_MESH)
        for step in range(1, self.chips):
            pl.semaphore_signal(everyone, inc=1, device_id=self.chip_device(self.chip_at(step)), device_id_type=BY_MESH)
        pl.semaphore_signal(everyone, inc=1, device_id=self.sibling, device_id_type=BY_MESH)
        pl.semaphore_wait(everyone, self.groups + self.chips - 1)


def project_kernel(
    dp_count, groups, hidden, memory, gains, w_key, w_value, w_query, w_out, w_gate, w_up, w_down, grad,
    attn_in, gain_rows, key, value, query, all_gains, all_key, all_value, all_query, all_out,
    all_gate, all_up, all_down, all_grad,
    weight, parts, line_send, line_recv, chip_send, chip_recv, core_send, core_recv,
    own_sem, load_sem, part_send, part_recv, part_own,
    dy_own, dy_chip_send, dy_chip_recv, dy_core_send, dy_core_recv,
):
    place = Place(dp_count, groups)
    chips, seq = place.chips, place.seq
    shards = (gains, w_key, w_value, w_query, w_out, w_gate, w_up, w_down)
    wholes = (all_gains, all_key, all_value, all_query, all_out, all_gate, all_up, all_down)
    count = 5
    whole_own = place.dp * groups + seq

    def own_block(m):
        return whole_own if m < count else seq

    above, below = seq < groups - 1, seq > 0
    up, down = place.line_device(lax.rem(seq + 1, groups)), place.line_device(lax.rem(seq + groups - 1, groups))

    def line(m, dp):
        return wholes[m].at[pl.ds(dp * groups, groups)]

    def along(m, src, block, distance, upward):
        slot = 0 if upward else 1
        return remote(
            src, wholes[m].at[block], line_send.at[m, slot, distance - 1], line_recv.at[m, slot, distance - 1],
            up if upward else down,
        )

    def to_chip(m, src, block, step):
        return remote(
            src, wholes[m].at[block], chip_send.at[m, step - 1], chip_recv.at[m, step - 1],
            place.chip_device(place.chip_at(step)),
        )

    def to_sibling(m, src, dst, step):
        return remote(src, dst, core_send.at[m, step], core_recv.at[m, step], place.sibling)

    def spread(m, src, block):
        for step in range(1, chips):
            to_chip(m, src, block, step).start()
        to_sibling(m, src, wholes[m].at[block], 0).start()

    def own_copy(m):
        return pltpu.make_async_copy(shards[m], wholes[m].at[own_block(m)], own_sem.at[m])

    def start_own(m):
        own = own_block(m)
        own_copy(m).start()

        @pl.when(above)
        def _():
            along(m, shards[m], own, 1, True).start()

        @pl.when(below)
        def _():
            along(m, shards[m], own, 1, False).start()

        if m < count:
            spread(m, shards[m], own)

    def serve_line(m):
        for distance in range(1, groups):
            for upward in (True, False):
                block = own_block(m) - distance if upward else own_block(m) + distance
                there = seq >= distance if upward else seq < groups - distance
                onward = above if upward else below

                @pl.when(there)
                def _():
                    landed = wholes[m].at[block]
                    along(m, landed, block, distance, upward).wait_recv()

                    @pl.when(onward)
                    def _():
                        along(m, landed, block, distance + 1, upward).start()

                    if m < count:
                        spread(m, landed, block)

    chunks = all_grad.shape[0]
    chunk_rows = grad.shape[0] // chunks

    def grad_rows(chunk):
        return grad.at[pl.ds(chunk * chunk_rows, chunk_rows), :]

    def grad_own(chunk):
        return pltpu.make_async_copy(grad_rows(chunk), all_grad.at[chunk, place.dp], dy_own.at[chunk])

    def grad_to_chip(chunk, step):
        return remote(
            grad_rows(chunk), all_grad.at[chunk, place.dp], dy_chip_send.at[chunk, step - 1],
            dy_chip_recv.at[chunk, step - 1], place.chip_device(place.chip_at(step)),
        )

    def grad_to_sibling(chunk, step):
        dp = 2 * place.chip_at(step) + place.core
        src = all_grad.at[chunk, dp] if step > 0 else grad_rows(chunk)
        return remote(
            src, all_grad.at[chunk, dp], dy_core_send.at[chunk, step], dy_core_recv.at[chunk, step], place.sibling
        )

    def start_grad(chunk):
        grad_own(chunk).start()
        for step in range(1, chips):
            grad_to_chip(chunk, step).start()
        grad_to_sibling(chunk, 0).start()

    def serve_grad(chunk):
        for step in range(1, chips):
            grad_to_chip(chunk, step).wait_recv()
            grad_to_sibling(chunk, step).start()

    def finish_grad(chunk):
        grad_own(chunk).wait()
        for step in range(1, chips):
            grad_to_chip(chunk, step).wait_send()
        for step in range(chips):
            grad_to_sibling(chunk, step).wait()

    def serve_chips(m):
        for step in range(1, chips):
            dp = 2 * place.chip_at(step) + place.core
            remote(
                line(m, dp), line(m, dp), chip_send.at[m, step - 1], chip_recv.at[m, step - 1], place.sibling
            ).wait_recv()
            to_sibling(m, line(m, dp), line(m, dp), step).start()

    def finish(m):
        for step in range(chips):
            dp = 2 * place.chip_at(step) + 1 - place.core
            to_sibling(m, line(m, dp), line(m, dp), step).wait_recv()
        own_copy(m).wait()

    targets = (None, key, value, query, None)
    lefts = (None, memory, memory, attn_in, None)
    share = weight.shape[2] // groups

    def part_copy(m, step):
        other = place.line_at(step)
        return remote(
            parts.at[m - 1, other], targets[m].at[seq], part_send.at[m - 1, step - 1], part_recv.at[m - 1, step - 1],
            place.line_device(other),
        )

    def own_part(m):
        return pltpu.make_async_copy(parts.at[m - 1, seq], targets[m].at[seq], part_own.at[m - 1])

    def load(m):
        return pltpu.make_async_copy(wholes[m], weight, load_sem)

    def project(m):
        load(m).start()
        load(m).wait()
        rows = weight.shape[0] * weight.shape[1]
        left = lefts[m][...]

        def one(step, _):
            group = place.line_at(step)
            columns = pl.ds(pl.multiple_of(group * share, share), share)
            right = weight[:, :, columns].reshape(rows, share)
            parts[m - 1, group] = jnp.dot(left, right, preferred_element_type=F32).astype(BF16)

            @pl.when(step > 0)
            def _():
                remote(
                    parts.at[m - 1, group], targets[m].at[seq], part_send.at[m - 1, step - 1],
                    part_recv.at[m - 1, step - 1], place.line_device(group),
                ).start()

            return 0

        lax.fori_loop(1, groups, one, 0)
        one(0, 0)
        own_part(m).start()

    def normalize():
        here = 128 // (weight.shape[1])
        tiles = weight.shape[2] // 128
        for tile in range(tiles):
            total = all_gains_v[tile * here]
            for i in range(1, here):
                total = total + pltpu.roll(all_gains_v[tile * here + i], i * weight.shape[1], 1)
            gain_rows[:, tile * 128 : (tile + 1) * 128] = total
        step_rows = 128 if hidden.shape[0] % 128 == 0 else hidden.shape[0]

        def some(i, _):
            rows = pl.ds(pl.multiple_of(i * step_rows, step_rows), step_rows)
            x = hidden[rows, :].astype(F32)
            normed = x * lax.rsqrt(jnp.mean(x * x, axis=-1, keepdims=True) + EPSILON)
            attn_in[rows, :] = (normed * gain_rows[0:1, :]).astype(BF16)
            return 0

        lax.fori_loop(0, hidden.shape[0] // step_rows, some, 0)

    all_gains_v = all_gains
    place.barrier()
    start_own(0)
    start_own(1)
    serve_line(0)
    start_own(2)
    serve_line(1)
    start_own(3)
    serve_chips(0)
    serve_line(2)
    start_own(4)
    serve_chips(1)
    finish(0)
    normalize()
    serve_line(3)
    start_own(5)
    finish(1)
    project(1)
    serve_line(4)
    start_own(6)
    for chunk in range(chunks):
        start_grad(chunk)
    serve_chips(2)
    finish(2)
    project(2)
    serve_line(5)
    start_own(7)
    serve_chips(3)
    finish(3)
    project(3)
    serve_line(6)
    serve_chips(4)
    serve_line(7)
    for chunk in range(chunks):
        serve_grad(chunk)
    finish(4)
    for chunk in range(chunks):
        finish_grad(chunk)
    for m in range(count, len(shards)):
        own_copy(m).wait()
    for m in range(len(shards)):
        for distance in range(1, groups):
            for upward in (True, False):
                came = seq >= distance - 1 if upward else seq < groups - distance + 1
                onward = above if upward else below

                @pl.when(came & onward)
                def _():
                    along(m, wholes[m].at[own_block(m)], own_block(m), distance, upward).wait_send()

        if m >= count:
            continue
        mine = line(m, place.dp)
        for step in range(1, chips):
            remote(
                mine, mine, chip_send.at[m, step - 1], chip_recv.at[m, step - 1], place.sibling
            ).wait_send()
        for step in range(chips):
            to_sibling(m, mine, mine, step).wait_send()
    for m in (1, 2, 3):
        own_part(m).wait()
        for step in range(1, groups):
            part_copy(m, step).wait()


def project_call(dp_count, groups, piece, width, here, padded, chunks):
    chips = dp_count // 2
    blocks = dp_count * groups
    share = width // groups
    hbm = pl.BlockSpec(memory_space=pl.ANY)
    vmem = pl.BlockSpec(memory_space=pltpu.VMEM)
    heads = jax.ShapeDtypeStruct((groups, piece, share), BF16)
    whole = jax.ShapeDtypeStruct((blocks, here, width), BF16)
    units = jax.ShapeDtypeStruct((groups, padded, width), BF16)
    dma = pltpu.SemaphoreType.DMA
    others = max(chips - 1, 1)
    return pl.pallas_call(
        functools.partial(project_kernel, dp_count, groups),
        in_specs=[vmem, vmem] + [hbm] * 9,
        out_specs=[vmem, vmem, hbm, hbm, hbm, vmem] + [hbm] * 8,
        out_shape=(
            jax.ShapeDtypeStruct((piece, width), BF16),
            jax.ShapeDtypeStruct((8, width), F32),
            heads, heads, heads,
            jax.ShapeDtypeStruct((blocks, 8, 128), F32),
            whole, whole, whole, whole, units, units, units,
            jax.ShapeDtypeStruct((chunks, dp_count, piece // chunks, width), BF16),
        ),
        scratch_shapes=[
            pltpu.VMEM((blocks, here, width), BF16),
            pltpu.VMEM((3, groups, piece, share), BF16),
            dma((8, 2, groups)), dma((8, 2, groups)),
            dma((5, others)), dma((5, others)),
            dma((5, chips)), dma((5, chips)),
            dma((8,)), dma, dma((3, groups - 1)), dma((3, groups - 1)), dma((3,)),
            dma((chunks,)), dma((chunks, others)), dma((chunks, others)), dma((chunks, chips)), dma((chunks, chips)),
        ],
        compiler_params=pltpu.CompilerParams(
            collective_id=1, has_side_effects=True, vmem_limit_bytes=48 * 1024 * 1024
        ),
        cost_estimate=pl.CostEstimate(
            flops=128 * piece * width * width, transcendentals=0, bytes_accessed=16 * width * width
        ),
        name="gather_project",
    )


def gain_tile(gain_attn, gain_ffn):
    here = gain_attn.shape[0]
    both = jnp.stack((gain_attn, gain_ffn)).astype(F32)
    return jnp.pad(both, ((0, 6), (0, 128 - here)))


def reduce_kernel(
    dp_count, groups, here, context, memory, attn_in, gain_rows, gain_ffn_term, grad_branch, dv, dk, dq,
    all_value, all_key, all_query, hidden, grad_mid,
    grad_out, grad_value, grad_key, grad_query, grad_memory, grad_hidden, grad_gains,
    right, core_buf, core_in, chip_buf, chip_in, kept, line_buf, line_in, line_own,
    part_send, part_recv, part_own, load_sem, core_send, core_recv, chip_send, chip_recv,
    line_send, line_recv, store_sem, core_free, chip_free,
    weight, panel_out, grad_attn_in, mid_buf, hidden_buf, gain_term, gain_buf, gain_in,
    weight_sem, panel_sem, mid_sem, hidden_sem, gain_send, gain_recv,
):
    place = Place(dp_count, groups)
    chips, seq = place.chips, place.seq
    panel = groups * here
    share = right.shape[3]
    lefts = (context, memory, memory, attn_in)
    parts = (None, dv, dk, dq)
    grads = (grad_out, grad_value, grad_key, grad_query)
    half = share // 2
    count = 8

    def half_columns(job, group=0):
        return pl.ds(group * share + job % 2 * half, half)

    def part_copy(job, step):
        other = place.line_at(step)
        return remote(
            parts[job // 2].at[other, :, half_columns(job)], right.at[job // 2, seq, :, half_columns(job)],
            part_send.at[job, step - 1], part_recv.at[job, step - 1], place.line_device(other),
        )

    def own_part(job):
        return pltpu.make_async_copy(
            parts[job // 2].at[seq, :, half_columns(job)], right.at[job // 2, seq, :, half_columns(job)],
            part_own.at[job],
        )

    def send_parts(job):
        own_part(job).start()
        for step in range(1, groups):
            part_copy(job, step).start()

    def sent_parts(job):
        for step in range(1, groups):
            part_copy(job, step).wait_send()

    def arrived_parts(job):
        own_part(job).wait()
        for step in range(1, groups):
            part_copy(job, step).wait_recv()

    def branch_copy(group):
        return pltpu.make_async_copy(
            grad_branch.at[:, pl.ds(group * share, share)], right.at[0, group], load_sem.at[group]
        )

    def product(job, dp, store):
        rows = pl.ds(pl.multiple_of(dp * panel, panel), panel)
        left = lefts[job // 2][:, rows].T
        for group in range(groups):
            store(
                slice(group * half, (group + 1) * half),
                jnp.dot(left, right[job // 2, group, :, half_columns(job)], preferred_element_type=F32),
            )

    def core_copy(m, step):
        return remote(
            core_buf.at[step], core_in.at[m % 2, step], core_send.at[step], core_recv.at[m % 2, step], place.sibling
        )

    def chip_copy(m, step):
        return remote(
            chip_buf.at[m % 2, step - 1], chip_in.at[m % 2, step - 1], chip_send.at[m % 2, step - 1],
            chip_recv.at[m % 2, step - 1], place.chip_device(place.chip_at(step)),
        )

    def line_copy(m, step):
        return remote(
            line_buf.at[m, step - 1], line_in.at[m, step - 1], line_send.at[m, step - 1], line_recv.at[m, step - 1],
            place.line_device(place.line_at(step)),
        )

    paired = groups == 4
    inner = (seq == 1) | (seq == 2)
    mate = seq + 1 - 2 * (seq % 2)

    def across(j):
        return 2 * (1 - seq // 2) + j

    def near_copy(m):
        return remote(
            line_buf.at[m, 0], line_in.at[m, 0], line_send.at[m, 0], line_recv.at[m, 0], place.line_device(mate)
        )

    def relay_copy(m, j):
        return remote(
            line_buf.at[m, 1 + j], line_in.at[m, 2 + j], line_send.at[m, 1 + j], line_recv.at[m, 2 + j],
            place.line_device(mate),
        )

    def across_copy(m, j):
        return remote(
            line_buf.at[m, 1 + j], line_in.at[m, 1], line_send.at[m, 1 + j], line_recv.at[m, 1],
            place.line_device(across(j)),
        )

    order = tuple(range(1, chips)) + (0,)

    def to_sibling(m):
        if m >= 2:
            pl.semaphore_wait(core_free, 1)
        for step in order:
            if m >= 1:
                core_copy(m - 1, step).wait_send()
            dp = 2 * place.chip_at(step) + 1 - place.core

            def store(columns, value, step=step):
                core_buf[step, :, columns] = value.astype(BF16)

            product(m, dp, store)
            core_copy(m, step).start()

    def to_chips(m):
        for step in order:
            dp = 2 * place.chip_at(step) + place.core
            core_copy(m, step).wait_recv()
            if step > 0:
                if m >= 2:
                    chip_copy(m - 2, step).wait_send()
                    pl.semaphore_wait(chip_free.at[step - 1], 1)

                def store(columns, value, step=step):
                    total = value + core_in[m % 2, step, :, columns].astype(F32)
                    chip_buf[m % 2, step - 1, :, columns] = total.astype(BF16)

            else:

                def store(columns, value):
                    kept[m % 2, :, columns] = value + core_in[m % 2, 0, :, columns].astype(F32)

            product(m, dp, store)
            if step > 0:
                chip_copy(m, step).start()
        if m + 2 < count:
            pl.semaphore_signal(core_free, inc=1, device_id=place.sibling, device_id_type=BY_MESH)

    def sum_chips(m):
        for step in range(1, chips):
            chip_copy(m, step).wait_recv()

        def block_sum(block):
            rows = pl.ds(pl.multiple_of(block * here, here), here)
            total = kept[m % 2, rows, :]
            for other in range(1, chips):
                total = total + chip_in[m % 2, other - 1, rows, :].astype(F32)
            return total

        if paired:
            line_buf[m, 0] = block_sum(mate).astype(BF16)
            for j in range(2):
                line_buf[m, 1 + j] = block_sum(across(j)).astype(BF16)
        else:
            for step in range(1, groups):
                line_buf[m, step - 1] = block_sum(place.line_at(step)).astype(BF16)
        line_own[m] = block_sum(seq)
        if m + 2 < count:
            for step in range(1, chips):
                pl.semaphore_signal(
                    chip_free.at[step - 1], inc=1, device_id=place.chip_device(place.chip_at(step)),
                    device_id_type=BY_MESH,
                )

    def send_line(m):
        if paired:
            near_copy(m).start()

            @pl.when(jnp.logical_not(inner))
            def _():
                for j in range(2):
                    relay_copy(m, j).start()

        else:
            for step in range(1, groups):
                line_copy(m, step).start()

    def relay(m):
        if not paired:
            return

        @pl.when(inner)
        def _():
            for j in range(2):
                relay_copy(m, j).wait_recv()
                line_buf[m, 1 + j] = (line_buf[m, 1 + j].astype(F32) + line_in[m, 2 + j].astype(F32)).astype(BF16)
                across_copy(m, j).start()

    def store_grad(m, group):
        return pltpu.make_async_copy(
            line_own.at[m, :, pl.ds(group * half, half)], grads[m // 2].at[:, half_columns(m, group)],
            store_sem.at[m, group],
        )

    def settle(m):
        total = line_own[m]
        if paired:
            near_copy(m).wait_recv()
            across_copy(m, 0).wait_recv()
            total = total + line_in[m, 0].astype(F32) + line_in[m, 1].astype(F32)
        else:
            for step in range(1, groups):
                line_copy(m, step).wait_recv()
                total = total + line_in[m, step - 1].astype(F32)
        line_own[m] = total
        for group in range(groups):
            store_grad(m, group).start()

    width = memory.shape[1]
    panels = width // panel
    piece = memory.shape[0]

    def weight_copy(slot, which, source, index):
        rows = pl.ds(pl.multiple_of(index * panel, panel), panel)
        return pltpu.make_async_copy(source.at[rows, :], weight.at[slot, which], weight_sem.at[slot, which])

    def panel_copy(slot, index):
        columns = pl.ds(pl.multiple_of(index * panel, panel), panel)
        return pltpu.make_async_copy(panel_out.at[slot], grad_memory.at[:, columns], panel_sem.at[slot])

    def back(slot, which, m):
        total = jnp.zeros((piece, panel), F32)
        for group in range(groups):
            columns = slice(group * share, (group + 1) * share)
            total = total + lax.dot_general(
                right[m, group], weight[slot, which, :, columns], NT, preferred_element_type=F32
            )
        return total

    def memory_gradient():
        weight_copy(0, 0, all_value, 0).start()
        weight_copy(0, 1, all_key, 0).start()

        def one(index, _):
            slot = lax.rem(index, 2)

            @pl.when(index + 1 < panels)
            def _():
                weight_copy(1 - slot, 0, all_value, index + 1).start()
                weight_copy(1 - slot, 1, all_key, index + 1).start()

            weight_copy(slot, 0, all_value, index).wait()
            weight_copy(slot, 1, all_key, index).wait()

            @pl.when(index >= 2)
            def _():
                panel_copy(slot, index - 2).wait()

            panel_out[slot] = back(slot, 0, 1) + back(slot, 1, 2)
            panel_copy(slot, index).start()
            return 0

        lax.fori_loop(0, panels, one, 0)
        for index in range(max(panels - 2, 0), panels):
            panel_copy(index % 2, index).wait()

    def query_gradient():
        weight_copy(0, 0, all_query, 0).start()

        def one(index, _):
            slot = lax.rem(index, 2)

            @pl.when(index + 1 < panels)
            def _():
                weight_copy(1 - slot, 0, all_query, index + 1).start()

            weight_copy(slot, 0, all_query, index).wait()
            columns = pl.ds(pl.multiple_of(index * panel, panel), panel)
            grad_attn_in[:, columns] = back(slot, 0, 3)
            return 0

        lax.fori_loop(0, panels, one, 0)

    some = mid_buf.shape[1]
    batches = piece // some

    def batch_rows(index):
        return pl.ds(pl.multiple_of(index * some, some), some)

    def mid_copy(slot, index):
        return pltpu.make_async_copy(grad_mid.at[batch_rows(index), :], mid_buf.at[slot], mid_sem.at[slot])

    def hidden_copy(slot, index):
        return pltpu.make_async_copy(hidden.at[batch_rows(index), :], hidden_buf.at[slot], hidden_sem.at[slot])

    def hidden_store(index):
        rows = batch_rows(index)
        return pltpu.make_async_copy(grad_attn_in.at[rows, :], grad_hidden.at[rows, :], panel_sem.at[0])

    def hidden_gradient():
        gain_term[...] = jnp.zeros_like(gain_term)
        mid_copy(0, 0).start()
        hidden_copy(0, 0).start()

        def one(index, _):
            slot = lax.rem(index, 2)

            @pl.when(index + 1 < batches)
            def _():
                mid_copy(1 - slot, index + 1).start()
                hidden_copy(1 - slot, index + 1).start()

            mid_copy(slot, index).wait()
            hidden_copy(slot, index).wait()
            rows = batch_rows(index)
            x = hidden_buf[slot].astype(F32)
            rstd = lax.rsqrt(jnp.mean(x * x, axis=-1, keepdims=True) + EPSILON)
            normed = x * rstd
            grad = grad_attn_in[rows, :]
            gain_term[0:1, :] += jnp.sum(normed * grad, axis=0, keepdims=True)
            scaled = grad * gain_rows[0:1, :]
            shift = jnp.mean(scaled * normed, axis=-1, keepdims=True)
            grad_attn_in[rows, :] = mid_buf[slot] + rstd * (scaled - normed * shift)
            hidden_store(index).start()
            return 0

        lax.fori_loop(0, batches, one, 0)

    devices = dp_count * groups
    me = place.dp * groups + seq

    def gain_copy(step):
        owner = lax.rem(me + step, devices)
        return remote(
            gain_buf.at[owner], gain_in.at[step], gain_send, gain_recv, {"dp": owner // groups, "seq": owner % groups}
        )

    def send_gains():
        gain_term[1:2, :] = gain_ffn_term[0:1, :]
        per = 128 // here
        for owner in range(devices):
            tile = gain_term[:, owner // per * 128 : (owner // per + 1) * 128]
            shift = owner % per * here
            gain_buf[owner] = pltpu.roll(tile, 128 - shift, 1) if shift else tile

        def one(step, _):
            gain_copy(step).start()
            return 0

        lax.fori_loop(1, devices, one, 0)

    def sum_gains():
        remote(
            gain_buf.at[pl.ds(0, devices - 1)], gain_in.at[pl.ds(1, devices - 1)], gain_send, gain_recv, place.sibling
        ).wait()
        total = gain_buf[me]
        for step in range(1, devices):
            total = total + gain_in[step]
        grad_gains[...] = total

    everyone = pltpu.get_barrier_semaphore()

    def greet(step, _):
        other = lax.rem(me + step, devices)
        pl.semaphore_signal(
            everyone, inc=1, device_id={"dp": other // groups, "seq": other % groups}, device_id_type=BY_MESH
        )
        return 0

    lax.fori_loop(1, devices, greet, 0)
    pl.semaphore_wait(everyone, devices - 1)
    send_parts(2)
    send_parts(3)
    for group in range(groups):
        branch_copy(group).start()
    for group in range(groups):
        branch_copy(group).wait()
    for job in range(2):
        to_sibling(job)
        to_chips(job)
    for job in range(2, count):
        sent_parts(job)
        if job + 2 < count:
            send_parts(job + 2)
        if job == count - 1:
            for earlier in range(job - 2):
                send_line(earlier)
        arrived_parts(job)
        to_sibling(job)
        sum_chips(job - 2)
        if job == count - 1:
            send_line(job - 2)
        to_chips(job)
        if job == 5:
            memory_gradient()
    sum_chips(6)
    send_line(6)
    query_gradient()
    relay(0)
    relay(1)
    relay(2)
    hidden_gradient()
    relay(3)
    relay(4)
    relay(5)
    send_gains()
    sum_chips(7)
    send_line(7)
    for job in range(6):
        settle(job)
    relay(6)
    settle(6)
    relay(7)
    settle(7)
    sum_gains()
    pltpu.make_async_copy(grad_attn_in, grad_hidden, panel_sem.at[0]).wait()
    for step in range(chips):
        core_copy(count - 1, step).wait_send()
    for job in range(count):
        if job >= count - 2:
            for step in range(1, chips):
                chip_copy(job, step).wait_send()
        if paired:
            near_copy(job).wait_send()
            for j in range(2):
                across_copy(job, j).wait_send()
        else:
            for step in range(1, groups):
                line_copy(job, step).wait_send()
        for group in range(groups):
            store_grad(job, group).wait()


def reduce_call(dp_count, groups, piece, width, here):
    chips = dp_count // 2
    share = width // groups
    panel = groups * here
    hbm = pl.BlockSpec(memory_space=pl.ANY)
    vmem = pl.BlockSpec(memory_space=pltpu.VMEM)
    grad = jax.ShapeDtypeStruct((here, width), F32)
    tokens = jax.ShapeDtypeStruct((piece, width), F32)
    some = min(64, piece)
    devices = dp_count * groups
    dma = pltpu.SemaphoreType.DMA
    others = max(chips - 1, 1)
    return pl.pallas_call(
        functools.partial(reduce_kernel, dp_count, groups, here),
        in_specs=[vmem] * 5 + [hbm] * 9,
        out_specs=[hbm] * 6 + [vmem],
        out_shape=(grad, grad, grad, grad, tokens, tokens, jax.ShapeDtypeStruct((8, 128), F32)),
        scratch_shapes=[
            pltpu.VMEM((4, groups, piece, share), BF16),
            pltpu.VMEM((chips, panel, width // 2), BF16),
            pltpu.VMEM((2, chips, panel, width // 2), BF16),
            pltpu.VMEM((2, others, panel, width // 2), BF16),
            pltpu.VMEM((2, others, panel, width // 2), BF16),
            pltpu.VMEM((2, panel, width // 2), F32),
            pltpu.VMEM((8, max(groups - 1, 3), here, width // 2), BF16),
            pltpu.VMEM((8, max(groups - 1, 4), here, width // 2), BF16),
            pltpu.VMEM((8, here, width // 2), F32),
            dma((8, groups - 1)), dma((8, groups - 1)), dma((8,)), dma((groups,)),
            dma((chips,)), dma((2, chips)),
            dma((2, others)), dma((2, others)),
            dma((8, max(groups - 1, 3))), dma((8, max(groups - 1, 4))), dma((8, groups)),
            pltpu.SemaphoreType.REGULAR, pltpu.SemaphoreType.REGULAR((others,)),
            pltpu.VMEM((2, 2, panel, width), BF16),
            pltpu.VMEM((2, piece, panel), F32),
            pltpu.VMEM((piece, width), F32),
            pltpu.VMEM((2, some, width), F32),
            pltpu.VMEM((2, some, width), BF16),
            pltpu.VMEM((8, width), F32),
            pltpu.VMEM((devices, 8, 128), F32),
            pltpu.VMEM((devices, 8, 128), F32),
            dma((2, 2)), dma((2,)), dma((2,)), dma((2,)), dma, dma,
        ],
        compiler_params=pltpu.CompilerParams(
            collective_id=2, has_side_effects=True, vmem_limit_bytes=63 * 1024 * 1024
        ),
        cost_estimate=pl.CostEstimate(
            flops=128 * piece * width * width, transcendentals=0, bytes_accessed=16 * width * width
        ),
        name="weight_gradients",
    )


def middle_kernel(
    dp_count, groups,
    gain_rows, hidden, context_heads, grad_own, out_rows, gate_rows, up_rows, down_rows, all_grad,
    context, gain_term, layer_out, grad_mid, grad_branch, grad_heads, grad_down, grad_gate, grad_up,
    all_ffn, grad_acts, acts, grad_gates, grad_ups, core_in, chip_in, branch_core, branch_out, branch_in, term_in,
    gate_w, up_w, down_w, out_w, mid, ffn_in, own_total, chip_out, term_buf,
    col_send, col_recv, col_own, weight_sem, out_sem, chip_send, chip_recv, core_send, core_recv, own_sem,
    x_sem, dy_sem, act_sem, sum_send, sum_recv, load_sem, far_send, far_recv, left_sem, right_sem, branch_sem,
    part_send, part_recv, plane_send, plane_recv,
    term_send, term_recv, rows_sem, gm_sem, gb_sem, head_send, head_recv, head_own,
):
    place = Place(dp_count, groups)
    chips, seq, core = place.chips, place.seq, place.core
    piece, width = hidden.shape
    share = width // groups
    unit_rows = gate_rows.shape[0]
    padded = gate_w.shape[0]
    wide = (gate_rows, up_rows, down_rows)
    kept = (gate_w, up_w, down_w)

    def weight_copy(i):
        return pltpu.make_async_copy(wide[i], kept[i].at[pl.ds(0, unit_rows), :], weight_sem.at[i])

    def group_columns(group):
        return pl.ds(pl.multiple_of(group * share, share), share)

    def out_copy(group, slot):
        rows = pl.ds(pl.multiple_of(group * share, share), share)
        return pltpu.make_async_copy(out_rows.at[rows, :], out_w.at[slot], out_sem.at[slot])

    def collect(step):
        other = place.line_at(step)
        return remote(
            context_heads.at[other], context.at[:, group_columns(seq)], col_send.at[step - 1], col_recv.at[step - 1],
            place.line_device(other),
        )

    def came_from(step):
        return lax.rem(seq + groups - step, groups)

    place.barrier()
    for step in range(1, groups):
        collect(step).start()
    own_columns = pltpu.make_async_copy(context_heads.at[seq], context.at[:, group_columns(seq)], col_own)
    own_columns.start()
    out_copy(seq, 0).start()
    hidden_copy = pltpu.make_async_copy(hidden, ffn_in, own_sem)
    hidden_copy.start()
    for i in range(3):
        weight_copy(i).start()
        if padded > unit_rows:
            kept[i][unit_rows:, :] = jnp.zeros((padded - unit_rows, width), BF16)

    def act_gradients(dy_buf, out_buf):
        def dy_copy(dp, slot):
            return pltpu.make_async_copy(all_grad.at[dp], dy_buf.at[slot], dy_sem.at[slot])

        def store(dp, slot):
            return pltpu.make_async_copy(out_buf.at[slot], grad_acts.at[dp], act_sem.at[slot, 0])

        dy_copy(0, 0).start()
        weight_copy(2).wait()

        def one(dp, _):
            slot = dp % 2

            @pl.when(dp + 1 < dp_count)
            def _():
                dy_copy(dp + 1, 1 - slot).start()

            dy_copy(dp, slot).wait()

            @pl.when(dp >= 2)
            def _():
                store(dp - 2, slot).wait()

            out_buf[slot] = mxu(dy_buf[slot], down_w[...], NT)
            store(dp, slot).start()
            return 0

        lax.fori_loop(0, dp_count, one, 0)
        for dp in range(dp_count - 2, dp_count):
            store(dp, dp % 2).wait()

    pl.run_scoped(act_gradients, pltpu.VMEM((2, piece, width), BF16), pltpu.VMEM((2, piece, padded), F32))

    for step in range(groups):
        slot = step % 2
        group = came_from(step)
        if step + 1 < groups:
            out_copy(came_from(step + 1), 1 - slot).start()
        if step == 0:
            own_columns.wait()
        else:
            columns = context.at[:, group_columns(group)]
            remote(columns, columns, col_send.at[step - 1], col_recv.at[step - 1], place.sibling).wait_recv()
        out_copy(group, slot).wait()
        left = context[:, group_columns(group)]
        if step == 0:
            hidden_copy.wait()

        def project(part, _, left=left, slot=slot, step=step):
            columns = pl.ds(pl.multiple_of(part * share, share), share)
            value = mxu(left, out_w[slot, :, columns], NN)
            if step == 0:
                mid[:, columns] = ffn_in[:, columns].astype(F32) + value
            else:
                mid[:, columns] += value
            return 0

        lax.fori_loop(0, groups, project, 0)

    some = min(64, piece)
    batches = piece // some

    def batch(index):
        return pl.ds(pl.multiple_of(index * some, some), some)

    def normalize(index, _):
        rows = batch(index)
        x = mid[rows, :]
        rstd = lax.rsqrt(jnp.mean(x * x, axis=-1, keepdims=True) + EPSILON)
        ffn_in[rows, :] = (x * rstd * gain_rows[1:2, :]).astype(BF16)
        return 0

    lax.fori_loop(0, batches, normalize, 0)

    def to_chip(step):
        return remote(
            ffn_in, all_ffn.at[place.dp], chip_send.at[step - 1], chip_recv.at[step - 1],
            place.chip_device(place.chip_at(step)),
        )

    def to_sibling(step):
        dp = 2 * place.chip_at(step) + core
        return remote(all_ffn.at[dp], all_ffn.at[dp], core_send.at[step], core_recv.at[step], place.sibling)

    own_ffn = pltpu.make_async_copy(ffn_in, all_ffn.at[place.dp], own_sem)
    own_ffn.start()
    square = chips == 4
    for step in range(1, 3 if square else chips):
        to_chip(step).start()
    own_ffn.wait()
    to_sibling(0).start()
    for i in range(2):
        weight_copy(i).wait()

    def hand_on(step):
        half = piece // 2
        dp = 2 * place.chip_at(step) + core
        rows = all_ffn.at[dp, pl.ds((step - 1) * half, half), :]
        return remote(rows, rows, chip_send.at[2], chip_recv.at[2], place.chip_device(place.chip_at(3 - step)))

    pieces = 2 * chips
    stored = (acts, grad_gates, grad_ups)

    def piece_of(u, own_first):
        step, which = u // 2, u % 2
        mine = 1 - which if own_first else which
        return step, which, 2 * place.chip_at(step) + mine * core + (1 - mine) * (1 - core)

    def hidden_units(x_buf, da_buf, act_buf):
        def x_copy(u):
            dp = piece_of(u, True)[2]
            return pltpu.make_async_copy(all_ffn.at[dp], x_buf.at[u % 2], x_sem.at[u % 2])

        def da_copy(u):
            dp = piece_of(u, True)[2]
            return pltpu.make_async_copy(grad_acts.at[dp], da_buf.at[u % 2], dy_sem.at[u % 2])

        def act_copy(u, i):
            dp = piece_of(u, True)[2]
            return pltpu.make_async_copy(act_buf.at[u % 2, i], stored[i].at[dp], act_sem.at[u % 2, i])

        def fetch(u):
            step, which, _ = piece_of(u, True)
            if square:

                @pl.when(u == 2)
                def _():
                    for near in (1, 2):
                        to_chip(near).wait_recv()
                        to_sibling(near).start()
                        hand_on(near).start()

                @pl.when(u == 6)
                def _():
                    to_chip(3).wait_recv()
                    to_sibling(3).start()

            else:

                @pl.when((which == 0) & (step > 0))
                def _():
                    to_chip(step).wait_recv()
                    to_sibling(step).start()

            @pl.when(which == 1)
            def _():
                to_sibling(step).wait_recv()

            x_copy(u).start()

        da_copy(0).start()

        def one(u, _):
            slot = u % 2
            ahead = u % 2 == 1
            if square:
                ahead = ahead | (u == 4)
            next_ahead = (u + 1 < pieces) & (u % 2 == 0)
            if square:
                next_ahead = next_ahead | (u == 3)

            @pl.when(jnp.logical_not(ahead))
            def _():
                fetch(u)

            @pl.when(next_ahead)
            def _():
                fetch(u + 1)

            @pl.when(u + 1 < pieces)
            def _():
                da_copy(u + 1).start()

            @pl.when(u >= 2)
            def _():
                for i in range(3):
                    act_copy(u - 2, i).wait()

            x_copy(u).wait()
            gate = mxu(x_buf[slot], gate_w[...], NT)
            up = mxu(x_buf[slot], up_w[...], NT)
            sig = 1.0 / (1.0 + jnp.exp(-gate))
            da_copy(u).wait()
            grad_act = da_buf[slot]
            act_buf[slot, 0] = (gate * sig * up).astype(BF16)
            act_buf[slot, 1] = (grad_act * up * sig * (1.0 + gate * (1.0 - sig))).astype(BF16)
            act_buf[slot, 2] = (grad_act * gate * sig).astype(BF16)
            for i in range(3):
                act_copy(u, i).start()
            return 0

        lax.fori_loop(0, pieces, one, 0)
        for u in range(max(pieces - 2, 0), pieces):
            for i in range(3):
                act_copy(u, i).wait()

    pl.run_scoped(
        hidden_units,
        pltpu.VMEM((2, piece, width), BF16), pltpu.VMEM((2, piece, padded), F32),
        pltpu.VMEM((2, 3, piece, padded), BF16),
    )

    def far_copy(step):
        return remote(
            chip_out.at[step - 1], chip_in.at[step - 1], far_send.at[step - 1],
            far_recv.at[step - 1], place.chip_device(place.chip_at(step)),
        )

    def input_sum(act_buf, core_out, load_buf):
        sources, rights, own = (grad_gates, grad_ups), (gate_w, up_w), own_total
        used = len(sources)

        def place_of(u):
            _, which, dp = piece_of(pieces - 2 + u - 4 * (u // 2), False)
            return chips - 1 - u // 2, which, dp

        def act_copy(u, i):
            dp = place_of(u)[2]
            return pltpu.make_async_copy(sources[i].at[dp], act_buf.at[u % 2, i], act_sem.at[u % 2, i])

        def sum_copy(step):
            return remote(
                core_out, core_in.at[step], sum_send, sum_recv.at[step], place.sibling
            )

        def load_copy(step):
            return pltpu.make_async_copy(core_in.at[step], load_buf, load_sem)

        for i in range(used):
            act_copy(0, i).start()

        def one(u, _):
            step, which, dp = place_of(u)
            slot = u % 2

            @pl.when(u + 1 < pieces)
            def _():
                for i in range(used):
                    act_copy(u + 1, i).start()

            for i in range(used):
                act_copy(u, i).wait()

            @pl.when((which == 0) & (u >= 2))
            def _():
                sum_copy(step + 1).wait_send()

            @pl.when(which == 1)
            def _():
                sum_copy(step).wait_recv()
                load_copy(step).start()
                load_copy(step).wait()

            def columns_of(part, _):
                columns = group_columns(part)
                value = mxu(act_buf[slot, 0], rights[0][:, columns], NN)
                for i in range(1, used):
                    value = value + mxu(act_buf[slot, i], rights[i][:, columns], NN)

                @pl.when(which == 0)
                def _():
                    core_out[:, columns] = value.astype(BF16)

                @pl.when((which == 1) & (step > 0))
                def _():
                    chip_out[step - 1, :, columns] = (value + load_buf[:, columns].astype(F32)).astype(BF16)

                @pl.when((which == 1) & (step == 0))
                def _():
                    own[:, columns] = value + load_buf[:, columns].astype(F32)

                return 0

            lax.fori_loop(0, groups, columns_of, 0)

            @pl.when(which == 0)
            def _():
                sum_copy(step).start()

            @pl.when((which == 1) & (step > 0))
            def _():
                far_copy(step).start()

            return 0

        lax.fori_loop(0, pieces, one, 0)
        sum_copy(0).wait_send()

    block = unit_rows // groups

    paired = groups == 4
    side = seq // 2
    inner = (seq == 1) | (seq == 2)
    partner = seq + 1 - 2 * (seq % 2)

    def across(j):
        return 2 * (1 - side) + j

    def term_rows(i, owner):
        return term_buf.at[i, pl.ds(pl.multiple_of(owner * block, block), block), :]

    def term_copy(i, step):
        other = place.line_at(step)
        return remote(
            term_rows(i, other), term_in.at[i, step - 1], term_send.at[i, step - 1], term_recv.at[i, step - 1],
            place.line_device(other),
        )

    def near_copy(i):
        return remote(
            term_rows(i, partner), term_in.at[i, 0], term_send.at[i, 0], term_recv.at[i, 0], place.line_device(partner)
        )

    def relay_copy(i, j):
        return remote(
            term_rows(i, across(j)), term_in.at[i, 2 + j], term_send.at[i, 1 + j], term_recv.at[i, 2 + j],
            place.line_device(partner),
        )

    def across_copy(i, j):
        return remote(
            term_rows(i, across(j)), term_in.at[i, 1], term_send.at[i, 1 + j], term_recv.at[i, 1],
            place.line_device(across(j)),
        )

    def send_term(i):
        if paired:
            near_copy(i).start()

            @pl.when(jnp.logical_not(inner))
            def _():
                for j in range(2):
                    relay_copy(i, j).start()

        else:
            for step in range(1, groups):
                term_copy(i, step).start()

    def relay_term(i, buf):
        if not paired:
            return

        @pl.when(inner)
        def _():
            for j in range(2):
                relay_copy(i, j).wait_recv()
                load = pltpu.make_async_copy(term_in.at[i, 2 + j], buf, left_sem.at[0])
                load.start()
                load.wait()
                rows = pl.ds(pl.multiple_of(across(j) * block, block), block)
                term_buf[i, rows, :] = (term_buf[i, rows, :].astype(F32) + buf[...].astype(F32)).astype(BF16)
                across_copy(i, j).start()

    def arrived_terms(i):
        if not paired:
            for step in range(1, groups):
                term_copy(i, step).wait()
            return range(groups - 1)
        near_copy(i).wait()
        across_copy(i, 0).wait_recv()
        for j in range(2):
            across_copy(i, j).wait_send()
        return range(2)

    def weight_terms(left_buf, acc):
        for i, (lefts, rights) in enumerate(((acts, all_grad), (grad_gates, all_ffn), (grad_ups, all_ffn))):

            def copies(dp, slot, lefts=lefts, rights=rights):
                return (
                    pltpu.make_async_copy(lefts.at[dp], left_buf.at[slot], left_sem.at[slot]),
                    pltpu.make_async_copy(rights.at[dp], out_w.at[slot], right_sem.at[slot]),
                )

            for copy in copies(0, 0):
                copy.start()

            def one(dp, _, copies=copies):
                slot = dp % 2

                @pl.when(dp + 1 < dp_count)
                def _():
                    for copy in copies(dp + 1, 1 - slot):
                        copy.start()

                for copy in copies(dp, slot):
                    copy.wait()
                left = left_buf[slot].T


                @pl.when(dp == 0)
                def _():
                    acc[...] = jnp.zeros_like(acc)

                acc[...] += jnp.dot(left, out_w[slot], preferred_element_type=F32)
                return 0

            lax.fori_loop(0, dp_count, one, 0)
            term_buf[i] = acc[0:unit_rows, :].astype(BF16)
            send_term(i)

    pl.run_scoped(weight_terms, pltpu.VMEM((2, piece, padded), BF16), pltpu.VMEM((padded, width), F32))

    pl.run_scoped(
        input_sum,
        pltpu.VMEM((2, 2, piece, padded), BF16), pltpu.VMEM((piece, width), BF16), pltpu.VMEM((piece, width), BF16),
    )

    def plane_copy(step):
        return remote(
            branch_out.at[step], branch_in.at[step - 1], plane_send.at[step - 1], plane_recv.at[step - 1],
            place.chip_device(place.chip_at(step)),
        )

    def branch_parts(relay_buf, act_buf, branch_buf, core_out, load_buf):
        relay_term(0, relay_buf)

        def act_copy(u):
            return pltpu.make_async_copy(acts.at[piece_of(u, False)[2]], act_buf.at[u % 2], act_sem.at[u % 2, 0])

        def part_copy(step):
            return remote(core_out, branch_core.at[step], part_send, part_recv.at[step], place.sibling)

        def load_copy(step):
            return pltpu.make_async_copy(branch_core.at[step], load_buf, load_sem)

        def store(step):
            return pltpu.make_async_copy(branch_buf.at[step % 2], branch_out.at[step], branch_sem.at[step % 2])

        act_copy(0).start()

        def one(u, _):
            step, which, dp = piece_of(u, False)
            slot = u % 2

            @pl.when(u + 1 < pieces)
            def _():
                act_copy(u + 1).start()

            act_copy(u).wait()

            @pl.when((which == 0) & (step > 0))
            def _():
                part_copy(step - 1).wait_send()

            @pl.when(which == 1)
            def _():
                part_copy(step).wait_recv()
                load_copy(step).start()

                @pl.when(step > 1)
                def _():
                    store(step - 2).wait()

                load_copy(step).wait()

            def part_of(part, _):
                columns = group_columns(part)
                value = mxu(act_buf[slot], down_w[:, columns], NN)

                @pl.when(which == 0)
                def _():
                    core_out[:, columns] = value.astype(BF16)

                @pl.when(which == 1)
                def _():
                    branch_buf[step % 2, :, columns] = (value + load_buf[:, columns].astype(F32)).astype(BF16)

                return 0

            lax.fori_loop(0, groups, part_of, 0)

            @pl.when(which == 0)
            def _():
                part_copy(step).start()

            @pl.when(which == 1)
            def _():
                store(step).start()

            return 0

        lax.fori_loop(0, pieces, one, 0)
        part_copy(chips - 1).wait_send()
        for step in range(max(chips - 2, 0), chips):
            store(step).wait()
        relay_term(1, relay_buf)

    pl.run_scoped(
        branch_parts,
        pltpu.VMEM((block, width), BF16), pltpu.VMEM((2, piece, padded), BF16), pltpu.VMEM((2, piece, width), BF16),
        pltpu.VMEM((piece, width), BF16), pltpu.VMEM((piece, width), BF16),
    )

    for step in range(1, chips):
        landed = chip_in.at[step - 1]
        remote(landed, landed, far_send.at[step - 1], far_recv.at[step - 1], place.sibling).wait_recv()
    for step in range(1, chips):
        plane_copy(step).start()
    for step in range(1, chips):
        to_chip(step).wait_send()
    gain_term[...] = jnp.zeros_like(gain_term)

    def norm_and_heads(rows_buf, mid_buf, layer_buf, heads_buf, sum_buf):
        def rows_copy(index, step, slot):
            source = grad_own.at[batch(index), :] if step == 0 else chip_in.at[step - 1, batch(index), :]
            return pltpu.make_async_copy(source, rows_buf.at[slot, step], rows_sem.at[slot, step])

        def layer_rows(index, step, slot):
            source = branch_out.at[0] if step == 0 else branch_in.at[step - 1]
            return pltpu.make_async_copy(
                source.at[batch(index), :], rows_buf.at[slot, step], rows_sem.at[slot, step]
            )

        def layer_copy(index, slot):
            return pltpu.make_async_copy(layer_buf.at[slot], layer_out.at[batch(index), :], gm_sem.at[slot])

        def grad_mid_copy(index, slot):
            return pltpu.make_async_copy(mid_buf.at[slot], grad_mid.at[batch(index), :], gm_sem.at[slot])

        for step in range(chips):
            rows_copy(0, step, 0).start()

        def norm_back(index, _):
            slot = index % 2

            @pl.when(index + 1 < batches)
            def _():
                for step in range(chips):
                    rows_copy(index + 1, step, 1 - slot).start()

            for step in range(chips):
                rows_copy(index, step, slot).wait()

            @pl.when(index >= 2)
            def _():
                grad_mid_copy(index - 2, slot).wait()

            rows = batch(index)
            grad = own_total[rows, :]
            for step in range(1, chips):
                grad = grad + rows_buf[slot, step].astype(F32)
            x = mid[rows, :]
            rstd = lax.rsqrt(jnp.mean(x * x, axis=-1, keepdims=True) + EPSILON)
            normed = x * rstd
            gain_term[0:1, :] += jnp.sum(normed * grad, axis=0, keepdims=True)
            scaled = grad * gain_rows[1:2, :]
            shift = jnp.mean(scaled * normed, axis=-1, keepdims=True)
            total = rows_buf[slot, 0].astype(F32) + rstd * (scaled - normed * shift)
            mid_buf[slot] = total
            ffn_in[rows, :] = total.astype(BF16)
            grad_mid_copy(index, slot).start()
            return 0

        lax.fori_loop(0, batches, norm_back, 0)
        grad_branch_copy = pltpu.make_async_copy(ffn_in, grad_branch, gb_sem)
        grad_branch_copy.start()
        for index in range(max(batches - 2, 0), batches):
            grad_mid_copy(index, index % 2).wait()

        def head_copy(step):
            other = place.line_at(step)
            return remote(
                heads_buf.at[other], grad_heads.at[seq], head_send.at[step - 1], head_recv.at[step - 1],
                place.line_device(other),
            )

        own_heads = pltpu.make_async_copy(heads_buf.at[seq], grad_heads.at[seq], head_own)
        order = tuple(range(1, groups)) + (0,)
        out_copy(place.line_at(order[0]), 0).start()
        for at, step in enumerate(order):
            group = place.line_at(step)
            if at + 1 < groups:
                out_copy(place.line_at(order[at + 1]), (at + 1) % 2).start()
            out_copy(group, at % 2).wait()
            heads_buf[group] = mxu(ffn_in[...], out_w[at % 2], NT).astype(BF16)
            if step > 0:
                head_copy(step).start()
            else:
                own_heads.start()

        relay_term(2, sum_buf.at[0])

        for i, target in enumerate((grad_down, grad_gate, grad_up)):
            landed = arrived_terms(i)
            for j in landed:
                load = pltpu.make_async_copy(term_in.at[i, j], sum_buf.at[j], rows_sem.at[0, 0])
                load.start()
                load.wait()
            total = term_buf[i, pl.ds(pl.multiple_of(seq * block, block), block), :].astype(F32)
            for j in landed:
                total = total + sum_buf[j].astype(F32)
            own_total[0:block, :] = total
            store = pltpu.make_async_copy(own_total.at[pl.ds(0, block), :], target, gm_sem.at[0])
            store.start()
            store.wait()
        for step in range(1, chips):
            plane_copy(step).wait()
        for step in range(chips):
            layer_rows(0, step, 0).start()

        def layer(index, _):
            slot = index % 2

            @pl.when(index + 1 < batches)
            def _():
                for step in range(chips):
                    layer_rows(index + 1, step, 1 - slot).start()

            for step in range(chips):
                layer_rows(index, step, slot).wait()

            @pl.when(index >= 2)
            def _():
                layer_copy(index - 2, slot).wait()

            total = mid[batch(index), :]
            for step in range(chips):
                total = total + rows_buf[slot, step].astype(F32)
            layer_buf[slot] = total.astype(BF16)
            layer_copy(index, slot).start()
            return 0

        lax.fori_loop(0, batches, layer, 0)
        for index in range(max(batches - 2, 0), batches):
            layer_copy(index, index % 2).wait()
        grad_branch_copy.wait()
        own_heads.wait()
        for step in range(1, groups):
            head_copy(step).wait()

    pl.run_scoped(
        norm_and_heads,
        pltpu.VMEM((2, chips, some, width), BF16), pltpu.VMEM((2, some, width), F32),
        pltpu.VMEM((2, some, width), BF16), pltpu.VMEM((groups, piece, share), BF16), pltpu.VMEM((groups - 1, block, width), BF16),
    )
    for step in range(1, groups):
        collect(step).wait_send()
    for step in range(chips):
        to_sibling(step).wait_send()
    for step in range(1, chips):
        far_copy(step).wait_send()


def middle_call(dp_count, groups, piece, width, unit_rows):
    chips = dp_count // 2
    share = width // groups
    assert share == piece
    padded = -(-unit_rows // 128) * 128
    block = unit_rows // groups
    others = max(chips - 1, 1)
    hbm = pl.BlockSpec(memory_space=pl.ANY)
    vmem = pl.BlockSpec(memory_space=pltpu.VMEM)
    dma = pltpu.SemaphoreType.DMA
    shape = jax.ShapeDtypeStruct
    return pl.pallas_call(
        functools.partial(middle_kernel, dp_count, groups),
        in_specs=[vmem] + [hbm] * 8,
        out_specs=[vmem, vmem] + [hbm] * 18,
        out_shape=(
            shape((piece, width), BF16),
            shape((8, width), F32),
            shape((piece, width), BF16),
            shape((piece, width), F32),
            shape((piece, width), BF16),
            shape((groups, piece, share), BF16),
            shape((block, width), F32),
            shape((block, width), F32),
            shape((block, width), F32),
            shape((dp_count, piece, width), BF16),
            shape((dp_count, piece, padded), F32),
            shape((dp_count, piece, padded), BF16),
            shape((dp_count, piece, padded), BF16),
            shape((dp_count, piece, padded), BF16),
            shape((chips, piece, width), BF16),
            shape((others, piece, width), BF16),
            shape((chips, piece, width), BF16),
            shape((chips, piece, width), BF16),
            shape((others, piece, width), BF16),
            shape((3, max(groups - 1, 4), block, width), BF16),
        ),
        scratch_shapes=[
            pltpu.VMEM((padded, width), BF16), pltpu.VMEM((padded, width), BF16), pltpu.VMEM((padded, width), BF16),
            pltpu.VMEM((2, share, width), BF16),
            pltpu.VMEM((piece, width), F32),
            pltpu.VMEM((piece, width), BF16),
            pltpu.VMEM((piece, width), F32),
            pltpu.VMEM((others, piece, width), BF16),
            pltpu.VMEM((3, unit_rows, width), BF16),
            dma((groups - 1,)), dma((groups - 1,)), dma, dma((3,)), dma((2,)),
            dma((others,)), dma((others,)), dma((chips,)), dma((chips,)), dma,
            dma((2,)), dma((2,)), dma((2, 3)),
            dma, dma((chips,)), dma, dma((others,)), dma((others,)),
            dma((2,)), dma((2,)), dma((2,)),
            dma, dma((chips,)), dma((others,)), dma((others,)), dma((3, max(groups - 1, 4))), dma((3, max(groups - 1, 4))),
            dma((2, chips)), dma((2,)), dma,
            dma((groups - 1,)), dma((groups - 1,)), dma,
        ],
        compiler_params=pltpu.CompilerParams(
            collective_id=5, has_side_effects=True, vmem_limit_bytes=63 * 1024 * 1024
        ),
        cost_estimate=pl.CostEstimate(
            flops=128 * piece * width * width, transcendentals=0, bytes_accessed=64 * width * width
        ),
        name="feed_forward",
    )


def shards(
    hidden_in, memory, segments, gain_attn, w_query, w_key, w_value, w_out, gain_ffn, w_gate, w_up, w_down, cotangent
):
    seqs, piece, width = hidden_in.shape
    groups = lax.axis_size("seq")
    dp_count = lax.axis_size("dp")
    assert seqs == 1
    length = piece * groups
    share = width // groups
    heads = share // HEAD_DIM
    here = w_query.shape[0]
    block = min(512, length)
    tokens = hidden_in.reshape(piece, width)
    mem = memory.reshape(piece, width)
    grad_out = cotangent.reshape(piece, width)

    attend_forward, attend_backward = attention_calls(length, heads, block)
    start, low, high = document_bounds(segments[0], block)
    flat = (length, share)
    split = (groups, piece, share)

    units = w_gate.shape[0]
    padded = -(-units // 16) * 16
    own_units = [jnp.pad(weight, ((0, padded - units), (0, 0))) for weight in (w_gate, w_up, w_down)]
    (
        attn_in, gain_rows, key, value, query, _, key_rows, value_rows, query_rows, out_rows,
        gate_rows, up_rows, down_rows, dy,
    ) = project_call(dp_count, groups, piece, width, here, padded, 1)(
        tokens, mem, gain_tile(gain_attn, gain_ffn), w_key, w_value, w_query, w_out, *own_units, grad_out
    )
    gate_rows, up_rows, down_rows = [
        rows.reshape(groups * padded, width) for rows in (gate_rows, up_rows, down_rows)
    ]
    key, value, query = [part.reshape(flat) for part in (key, value, query)]
    key_rows, value_rows, query_rows, out_rows = [
        rows.reshape(width, width) for rows in (key_rows, value_rows, query_rows, out_rows)
    ]
    context_heads, lse = attend_forward(low, start, query, key, value)
    (
        context, gain_term, layer_out, grad_mid, grad_branch, grad_context_heads, grad_w_down, grad_w_gate, grad_w_up, *_
    ) = middle_call(dp_count, groups, piece, width, groups * padded)(
        gain_rows, tokens, context_heads.reshape(split), grad_out, out_rows, gate_rows, up_rows, down_rows,
        dy.reshape(dp_count, piece, width),
    )
    grad_context_heads = grad_context_heads.reshape(flat)
    dq, dk, dv = attend_backward(high, start, query, key, value, context_heads, grad_context_heads, lse)

    grad_w_out, grad_w_value, grad_w_key, grad_w_query, grad_memory, grad_hidden, gains = reduce_call(
        dp_count, groups, piece, width, here
    )(
        context, mem, attn_in, gain_rows, gain_term, grad_branch, dv.reshape(split), dk.reshape(split),
        dq.reshape(split), value_rows, key_rows, query_rows, tokens, grad_mid,
    )
    grad_w_down, grad_w_gate, grad_w_up = [grad[:units] for grad in (grad_w_down, grad_w_gate, grad_w_up)]
    grad_gain_attn, grad_gain_ffn = gains[0, :here], gains[1, :here]
    cube = (seqs, piece, width)
    return (
        layer_out.reshape(cube),
        grad_hidden.reshape(cube),
        grad_memory.reshape(cube),
        grad_gain_attn,
        grad_w_query,
        grad_w_key,
        grad_w_value,
        grad_w_out,
        grad_gain_ffn,
        grad_w_gate,
        grad_w_up,
        grad_w_down,
    )


def solution(mesh):
    tokens = P("dp", "seq", None)
    rows = P(ALL, None)
    gain = P(ALL)
    in_specs = (tokens, tokens, P("dp", None), gain, rows, rows, rows, rows, gain, rows, rows, rows, tokens)
    out_specs = (tokens, tokens, tokens, gain, rows, rows, rows, rows, gain, rows, rows, rows)
    return jax.shard_map(shards, mesh=mesh, in_specs=in_specs, out_specs=out_specs, check_vma=False)
```

```python
import functools
import math

import jax
import jax.numpy as jnp
from jax import lax
from jax.experimental import pallas as pl
from jax.experimental.pallas import tpu as pltpu
from jax.sharding import PartitionSpec as P

HEAD_DIM = 128
DOCS = 4
EPSILON = 1e-06
MASKED = -1e30
ALL = ("dp", "seq")
F32 = jnp.float32
BF16 = jnp.bfloat16
EXP2_SCALE = HEAD_DIM ** (-0.5) * math.log2(math.e)
NT = (((1,), (1,)), ((), ()))
TN = (((0,), (0,)), ((), ()))
NN = (((1,), (0,)), ((), ()))
BY_MESH = pl.DeviceIdType.MESH


def mxu(left, right, dims):
    return lax.dot_general(left, right, dims, preferred_element_type=F32)


def rms_scale(values):
    return lax.rsqrt(jnp.mean(values * values, axis=-1, keepdims=True) + EPSILON)


def norm_back(grad_normed, normed, rstd, gain):
    scaled = grad_normed * gain
    return rstd * (scaled - normed * jnp.mean(scaled * normed, axis=-1, keepdims=True))


def forward_kernel(block, low_ref, start_ref, q_ref, k_ref, v_ref, out_ref, lse_ref):
    length, width = q_ref.shape
    heads = range(width // HEAD_DIM)
    columns = [slice(h * HEAD_DIM, (h + 1) * HEAD_DIM) for h in heads]

    def one_query_block(qb, _):
        q0 = pl.multiple_of(qb * block, block)
        rows = pl.ds(q0, block)
        start = start_ref[:, rows]
        query_pos = q0 + lax.broadcasted_iota(jnp.int32, (block, block), 1)

        def one_key_block(kb, carry):
            k0 = pl.multiple_of(kb * block, block)
            keys = pl.ds(k0, block)
            key_pos = k0 + lax.broadcasted_iota(jnp.int32, (block, block), 0)
            seen = (key_pos >= start) & (key_pos <= query_pos)
            scores = [mxu(k_ref[keys, columns[h]], q_ref[rows, columns[h]], NT) for h in heads]
            after = []
            for h in heads:
                top, total, acc = carry[h]
                score = jnp.where(seen, scores[h], MASKED)
                new_top = jnp.maximum(top, jnp.max(score, axis=0, keepdims=True))
                shrink = jnp.exp2((top - new_top) * EXP2_SCALE)
                raised = jnp.exp2((score - new_top) * EXP2_SCALE)
                total = total * shrink + jnp.sum(raised, axis=0, keepdims=True)
                acc = acc * shrink + mxu(v_ref[keys, columns[h]], raised.astype(BF16), TN)
                after.append((new_top, total, acc))
            return tuple(after)

        first = (
            jnp.full((1, block), MASKED, F32),
            jnp.zeros((1, block), F32),
            jnp.zeros((HEAD_DIM, block), F32),
        )
        done = lax.fori_loop(low_ref[qb], qb + 1, one_key_block, tuple(first for _ in heads))
        for h in heads:
            top, total, acc = done[h]
            out_ref[rows, columns[h]] = (acc / total).T.astype(BF16)
            lse_ref[h, :, rows] = top * EXP2_SCALE + jnp.log2(total)
        return 0

    lax.fori_loop(0, length // block, one_query_block, 0)


def backward_kernel(
    block, high_ref, start_ref, q_ref, k_ref, v_ref, ctx_ref, grad_ref, lse_ref,
    dq_ref, dk_ref, dv_ref, dq_acc, delta_acc,
):
    length, width = q_ref.shape
    heads = range(width // HEAD_DIM)
    columns = [slice(h * HEAD_DIM, (h + 1) * HEAD_DIM) for h in heads]
    blocks = length // block
    scale = HEAD_DIM ** (-0.5)
    dq_acc[...] = jnp.zeros_like(dq_acc)

    def one_delta(qb, _):
        rows = pl.ds(pl.multiple_of(qb * block, block), block)
        for h in heads:
            both = ctx_ref[rows, columns[h]].astype(F32) * grad_ref[rows, columns[h]].astype(F32)
            delta_acc[h, :, rows] = jnp.sum(both.T, axis=0, keepdims=True)
        return 0

    lax.fori_loop(0, blocks, one_delta, 0)

    def one_key_block(kb, _):
        k0 = pl.multiple_of(kb * block, block)
        keys = pl.ds(k0, block)
        key_pos = k0 + lax.broadcasted_iota(jnp.int32, (block, block), 0)

        def one_query_block(qb, carry):
            q0 = pl.multiple_of(qb * block, block)
            rows = pl.ds(q0, block)
            start = start_ref[:, rows]
            query_pos = q0 + lax.broadcasted_iota(jnp.int32, (block, block), 1)
            seen = (key_pos >= start) & (key_pos <= query_pos)
            scores = [mxu(k_ref[keys, columns[h]], q_ref[rows, columns[h]], NT) for h in heads]
            grad_probs = [mxu(v_ref[keys, columns[h]], grad_ref[rows, columns[h]], NT) for h in heads]
            after = []
            for h in heads:
                dk, dv = carry[h]
                prob = jnp.exp2(scores[h] * EXP2_SCALE - lse_ref[h, :, rows])
                prob = jnp.where(seen, prob, 0.0)
                grad_score = (prob * (grad_probs[h] - delta_acc[h, :, rows])).astype(BF16)
                dv = dv + mxu(prob.astype(BF16), grad_ref[rows, columns[h]], NN)
                dk = dk + mxu(grad_score, q_ref[rows, columns[h]], NN)
                dq_acc[rows, columns[h]] += mxu(grad_score, k_ref[keys, columns[h]], TN)
                after.append((dk, dv))
            return tuple(after)

        zeros = jnp.zeros((block, HEAD_DIM), F32)
        done = lax.fori_loop(kb, high_ref[kb], one_query_block, tuple((zeros, zeros) for _ in heads))
        for h in heads:
            dk_ref[keys, columns[h]] = (done[h][0] * scale).astype(BF16)
            dv_ref[keys, columns[h]] = done[h][1].astype(BF16)
        return 0

    lax.fori_loop(0, blocks, one_key_block, 0)
    dq_ref[...] = (dq_acc[...] * scale).astype(BF16)


def attention_calls(length, heads, block):
    together = math.gcd(heads, 4)
    wide = together * HEAD_DIM
    column = pl.BlockSpec((length, wide), lambda h, *_: (0, h))
    row = pl.BlockSpec((1, length), lambda h, *_: (0, 0))
    stat = pl.BlockSpec((together, 1, length), lambda h, *_: (h, 0, 0))
    flat = jax.ShapeDtypeStruct((length, heads * HEAD_DIM), BF16)
    pairs = heads * length * length // 4
    params = pltpu.CompilerParams(vmem_limit_bytes=56 * 1024 * 1024)
    forward = pl.pallas_call(
        functools.partial(forward_kernel, block),
        grid_spec=pltpu.PrefetchScalarGridSpec(
            num_scalar_prefetch=1,
            grid=(heads // together,),
            in_specs=[row, column, column, column],
            out_specs=[column, stat],
        ),
        out_shape=(flat, jax.ShapeDtypeStruct((heads, 1, length), F32)),
        compiler_params=params,
        cost_estimate=pl.CostEstimate(
            flops=64 * pairs * HEAD_DIM, transcendentals=pairs, bytes_accessed=8 * length * heads * HEAD_DIM
        ),
        name="attend_forward",
    )
    backward = pl.pallas_call(
        functools.partial(backward_kernel, block),
        grid_spec=pltpu.PrefetchScalarGridSpec(
            num_scalar_prefetch=1,
            grid=(heads // together,),
            in_specs=[row, column, column, column, column, column, stat],
            out_specs=[column, column, column],
            scratch_shapes=[pltpu.VMEM((length, wide), F32), pltpu.VMEM((together, 1, length), F32)],
        ),
        out_shape=(flat, flat, flat),
        compiler_params=params,
        cost_estimate=pl.CostEstimate(
            flops=96 * pairs * HEAD_DIM, transcendentals=pairs, bytes_accessed=16 * length * heads * HEAD_DIM
        ),
        name="attend_backward",
    )
    return forward, backward


def document_bounds(segment_ids, block):
    first = jnp.zeros_like(segment_ids)
    last = jnp.zeros_like(segment_ids)
    for number in range(DOCS):
        below = jnp.sum((segment_ids < number).astype(jnp.int32))
        upto = jnp.sum((segment_ids <= number).astype(jnp.int32))
        first = jnp.where(segment_ids == number, below, first)
        last = jnp.where(segment_ids == number, upto - 1, last)
    low = first[::block] // block
    high = last[block - 1 :: block] // block + 1
    return first[None, :], low, high


def remote(src, dst, send, recv, device):
    return pltpu.make_async_remote_copy(
        src_ref=src, dst_ref=dst, send_sem=send, recv_sem=recv, device_id=device, device_id_type=BY_MESH
    )


class Place:
    def __init__(self, dp_count, groups):
        self.groups = groups
        self.chips = dp_count // 2
        self.dp = lax.axis_index("dp")
        self.seq = lax.axis_index("seq")
        self.core = lax.rem(self.dp, 2)
        self.chip = self.dp // 2
        self.sibling = {"dp": self.dp + 1 - 2 * self.core, "seq": self.seq}

    def chip_at(self, step):
        chip, bit = self.chip, 1
        while bit < self.chips:
            chip = chip + (step // bit % 2) * bit * (1 - 2 * lax.rem(self.chip // bit, 2))
            bit *= 2
        return chip

    def chip_device(self, chip):
        return {"dp": 2 * chip + self.core, "seq": self.seq}

    def line_at(self, step):
        return lax.rem(self.seq + step, self.groups)

    def line_device(self, seq):
        return {"dp": self.dp, "seq": seq}

    def barrier(self):
        everyone = pltpu.get_barrier_semaphore()
        for step in range(1, self.groups):
            pl.semaphore_signal(everyone, inc=1, device_id=self.line_device(self.line_at(step)), device_id_type=BY_MESH)
        for step in range(1, self.chips):
            pl.semaphore_signal(everyone, inc=1, device_id=self.chip_device(self.chip_at(step)), device_id_type=BY_MESH)
        pl.semaphore_signal(everyone, inc=1, device_id=self.sibling, device_id_type=BY_MESH)
        pl.semaphore_wait(everyone, self.groups + self.chips - 1)


def project_kernel(
    dp_count, groups, hidden, memory, gains, w_key, w_value, w_query, w_out, w_gate, w_up, w_down, grad,
    attn_in, gain_rows, key, value, query, all_gains, all_key, all_value, all_query, all_out,
    all_gate, all_up, all_down, all_grad,
    weight, parts, line_send, line_recv, chip_send, chip_recv, core_send, core_recv,
    own_sem, load_sem, part_send, part_recv, part_own,
    dy_own, dy_chip_send, dy_chip_recv, dy_core_send, dy_core_recv,
):
    place = Place(dp_count, groups)
    chips, seq = place.chips, place.seq
    shards = (gains, w_key, w_value, w_query, w_out, w_gate, w_up, w_down)
    wholes = (all_gains, all_key, all_value, all_query, all_out, all_gate, all_up, all_down)
    count = 5
    whole_own = place.dp * groups + seq

    def own_block(m):
        return whole_own if m < count else seq

    above, below = seq < groups - 1, seq > 0
    up, down = place.line_device(lax.rem(seq + 1, groups)), place.line_device(lax.rem(seq + groups - 1, groups))

    def line(m, dp):
        return wholes[m].at[pl.ds(dp * groups, groups)]

    def along(m, src, block, distance, upward):
        slot = 0 if upward else 1
        return remote(
            src, wholes[m].at[block], line_send.at[m, slot, distance - 1], line_recv.at[m, slot, distance - 1],
            up if upward else down,
        )

    def to_chip(m, src, block, step):
        return remote(
            src, wholes[m].at[block], chip_send.at[m, step - 1], chip_recv.at[m, step - 1],
            place.chip_device(place.chip_at(step)),
        )

    def to_sibling(m, src, dst, step):
        return remote(src, dst, core_send.at[m, step], core_recv.at[m, step], place.sibling)

    def spread(m, src, block):
        for step in range(1, chips):
            to_chip(m, src, block, step).start()
        to_sibling(m, src, wholes[m].at[block], 0).start()

    def own_copy(m):
        return pltpu.make_async_copy(shards[m], wholes[m].at[own_block(m)], own_sem.at[m])

    def start_own(m):
        own = own_block(m)
        own_copy(m).start()

        @pl.when(above)
        def _():
            along(m, shards[m], own, 1, True).start()

        @pl.when(below)
        def _():
            along(m, shards[m], own, 1, False).start()

        if m < count:
            spread(m, shards[m], own)

    def serve_line(m):
        for distance in range(1, groups):
            for upward in (True, False):
                block = own_block(m) - distance if upward else own_block(m) + distance
                there = seq >= distance if upward else seq < groups - distance
                onward = above if upward else below

                @pl.when(there)
                def _():
                    landed = wholes[m].at[block]
                    along(m, landed, block, distance, upward).wait_recv()

                    @pl.when(onward)
                    def _():
                        along(m, landed, block, distance + 1, upward).start()

                    if m < count:
                        spread(m, landed, block)

    chunks = all_grad.shape[0]
    chunk_rows = grad.shape[0] // chunks

    def grad_rows(chunk):
        return grad.at[pl.ds(chunk * chunk_rows, chunk_rows), :]

    def grad_own(chunk):
        return pltpu.make_async_copy(grad_rows(chunk), all_grad.at[chunk, place.dp], dy_own.at[chunk])

    def grad_to_chip(chunk, step):
        return remote(
            grad_rows(chunk), all_grad.at[chunk, place.dp], dy_chip_send.at[chunk, step - 1],
            dy_chip_recv.at[chunk, step - 1], place.chip_device(place.chip_at(step)),
        )

    def grad_to_sibling(chunk, step):
        dp = 2 * place.chip_at(step) + place.core
        src = all_grad.at[chunk, dp] if step > 0 else grad_rows(chunk)
        return remote(
            src, all_grad.at[chunk, dp], dy_core_send.at[chunk, step], dy_core_recv.at[chunk, step], place.sibling
        )

    def start_grad(chunk):
        grad_own(chunk).start()
        for step in range(1, chips):
            grad_to_chip(chunk, step).start()
        grad_to_sibling(chunk, 0).start()

    def serve_grad(chunk):
        for step in range(1, chips):
            grad_to_chip(chunk, step).wait_recv()
            grad_to_sibling(chunk, step).start()

    def finish_grad(chunk):
        grad_own(chunk).wait()
        for step in range(1, chips):
            grad_to_chip(chunk, step).wait_send()
        for step in range(chips):
            grad_to_sibling(chunk, step).wait()

    def serve_chips(m):
        for step in range(1, chips):
            dp = 2 * place.chip_at(step) + place.core
            remote(
                line(m, dp), line(m, dp), chip_send.at[m, step - 1], chip_recv.at[m, step - 1], place.sibling
            ).wait_recv()
            to_sibling(m, line(m, dp), line(m, dp), step).start()

    def finish(m):
        for step in range(chips):
            dp = 2 * place.chip_at(step) + 1 - place.core
            to_sibling(m, line(m, dp), line(m, dp), step).wait_recv()
        own_copy(m).wait()

    targets = (None, key, value, query, None)
    lefts = (None, memory, memory, attn_in, None)
    share = weight.shape[2] // groups

    def part_copy(m, step):
        other = place.line_at(step)
        return remote(
            parts.at[m - 1, other], targets[m].at[seq], part_send.at[m - 1, step - 1], part_recv.at[m - 1, step - 1],
            place.line_device(other),
        )

    def own_part(m):
        return pltpu.make_async_copy(parts.at[m - 1, seq], targets[m].at[seq], part_own.at[m - 1])

    def load(m):
        return pltpu.make_async_copy(wholes[m], weight, load_sem)

    def project(m):
        load(m).start()
        load(m).wait()
        rows = weight.shape[0] * weight.shape[1]
        left = lefts[m][...]

        def one(step, _):
            group = place.line_at(step)
            columns = pl.ds(pl.multiple_of(group * share, share), share)
            right = weight[:, :, columns].reshape(rows, share)
            parts[m - 1, group] = jnp.dot(left, right, preferred_element_type=F32).astype(BF16)

            @pl.when(step > 0)
            def _():
                remote(
                    parts.at[m - 1, group], targets[m].at[seq], part_send.at[m - 1, step - 1],
                    part_recv.at[m - 1, step - 1], place.line_device(group),
                ).start()

            return 0

        lax.fori_loop(1, groups, one, 0)
        one(0, 0)
        own_part(m).start()

    def normalize():
        here = 128 // (weight.shape[1])
        tiles = weight.shape[2] // 128
        for tile in range(tiles):
            total = all_gains_v[tile * here]
            for i in range(1, here):
                total = total + pltpu.roll(all_gains_v[tile * here + i], i * weight.shape[1], 1)
            gain_rows[:, tile * 128 : (tile + 1) * 128] = total
        step_rows = 128 if hidden.shape[0] % 128 == 0 else hidden.shape[0]

        def some(i, _):
            rows = pl.ds(pl.multiple_of(i * step_rows, step_rows), step_rows)
            x = hidden[rows, :].astype(F32)
            normed = x * lax.rsqrt(jnp.mean(x * x, axis=-1, keepdims=True) + EPSILON)
            attn_in[rows, :] = (normed * gain_rows[0:1, :]).astype(BF16)
            return 0

        lax.fori_loop(0, hidden.shape[0] // step_rows, some, 0)

    all_gains_v = all_gains
    place.barrier()
    start_own(0)
    start_own(1)
    serve_line(0)
    start_own(2)
    serve_line(1)
    start_own(3)
    serve_chips(0)
    serve_line(2)
    start_own(4)
    serve_chips(1)
    finish(0)
    normalize()
    serve_line(3)
    start_own(5)
    finish(1)
    project(1)
    serve_line(4)
    start_own(6)
    for chunk in range(chunks):
        start_grad(chunk)
    serve_chips(2)
    finish(2)
    project(2)
    serve_line(5)
    start_own(7)
    serve_chips(3)
    finish(3)
    project(3)
    serve_line(6)
    serve_chips(4)
    serve_line(7)
    for chunk in range(chunks):
        serve_grad(chunk)
    finish(4)
    for chunk in range(chunks):
        finish_grad(chunk)
    for m in range(count, len(shards)):
        own_copy(m).wait()
    for m in range(len(shards)):
        for distance in range(1, groups):
            for upward in (True, False):
                came = seq >= distance - 1 if upward else seq < groups - distance + 1
                onward = above if upward else below

                @pl.when(came & onward)
                def _():
                    along(m, wholes[m].at[own_block(m)], own_block(m), distance, upward).wait_send()

        if m >= count:
            continue
        mine = line(m, place.dp)
        for step in range(1, chips):
            remote(
                mine, mine, chip_send.at[m, step - 1], chip_recv.at[m, step - 1], place.sibling
            ).wait_send()
        for step in range(chips):
            to_sibling(m, mine, mine, step).wait_send()
    for m in (1, 2, 3):
        own_part(m).wait()
        for step in range(1, groups):
            part_copy(m, step).wait()


def project_call(dp_count, groups, piece, width, here, padded, chunks):
    chips = dp_count // 2
    blocks = dp_count * groups
    share = width // groups
    hbm = pl.BlockSpec(memory_space=pl.ANY)
    vmem = pl.BlockSpec(memory_space=pltpu.VMEM)
    heads = jax.ShapeDtypeStruct((groups, piece, share), BF16)
    whole = jax.ShapeDtypeStruct((blocks, here, width), BF16)
    units = jax.ShapeDtypeStruct((groups, padded, width), BF16)
    dma = pltpu.SemaphoreType.DMA
    others = max(chips - 1, 1)
    return pl.pallas_call(
        functools.partial(project_kernel, dp_count, groups),
        in_specs=[vmem, vmem] + [hbm] * 9,
        out_specs=[vmem, vmem, hbm, hbm, hbm, vmem] + [hbm] * 8,
        out_shape=(
            jax.ShapeDtypeStruct((piece, width), BF16),
            jax.ShapeDtypeStruct((8, width), F32),
            heads, heads, heads,
            jax.ShapeDtypeStruct((blocks, 8, 128), F32),
            whole, whole, whole, whole, units, units, units,
            jax.ShapeDtypeStruct((chunks, dp_count, piece // chunks, width), BF16),
        ),
        scratch_shapes=[
            pltpu.VMEM((blocks, here, width), BF16),
            pltpu.VMEM((3, groups, piece, share), BF16),
            dma((8, 2, groups)), dma((8, 2, groups)),
            dma((5, others)), dma((5, others)),
            dma((5, chips)), dma((5, chips)),
            dma((8,)), dma, dma((3, groups - 1)), dma((3, groups - 1)), dma((3,)),
            dma((chunks,)), dma((chunks, others)), dma((chunks, others)), dma((chunks, chips)), dma((chunks, chips)),
        ],
        compiler_params=pltpu.CompilerParams(
            collective_id=1, has_side_effects=True, vmem_limit_bytes=48 * 1024 * 1024
        ),
        cost_estimate=pl.CostEstimate(
            flops=128 * piece * width * width, transcendentals=0, bytes_accessed=16 * width * width
        ),
        name="gather_project",
    )


def gain_tile(gain_attn, gain_ffn):
    here = gain_attn.shape[0]
    both = jnp.stack((gain_attn, gain_ffn)).astype(F32)
    return jnp.pad(both, ((0, 6), (0, 128 - here)))


def reduce_kernel(
    dp_count, groups, here, context, memory, attn_in, gain_rows, gain_ffn_term, grad_branch, dv, dk, dq,
    all_value, all_key, all_query, hidden, grad_mid,
    grad_out, grad_value, grad_key, grad_query, grad_memory, grad_hidden, grad_gains,
    right, core_buf, core_in, chip_buf, chip_in, kept, line_buf, line_in, line_own,
    part_send, part_recv, part_own, load_sem, core_send, core_recv, chip_send, chip_recv,
    line_send, line_recv, store_sem, core_free, chip_free,
    weight, panel_out, grad_attn_in, mid_buf, hidden_buf, gain_term, gain_buf, gain_in,
    weight_sem, panel_sem, mid_sem, hidden_sem, gain_send, gain_recv,
):
    place = Place(dp_count, groups)
    chips, seq = place.chips, place.seq
    panel = groups * here
    share = right.shape[3]
    lefts = (context, memory, memory, attn_in)
    parts = (None, dv, dk, dq)
    grads = (grad_out, grad_value, grad_key, grad_query)
    half = share // 2
    count = 8

    def half_columns(job, group=0):
        return pl.ds(group * share + job % 2 * half, half)

    def part_copy(job, step):
        other = place.line_at(step)
        return remote(
            parts[job // 2].at[other, :, half_columns(job)], right.at[job // 2, seq, :, half_columns(job)],
            part_send.at[job, step - 1], part_recv.at[job, step - 1], place.line_device(other),
        )

    def own_part(job):
        return pltpu.make_async_copy(
            parts[job // 2].at[seq, :, half_columns(job)], right.at[job // 2, seq, :, half_columns(job)],
            part_own.at[job],
        )

    def send_parts(job):
        own_part(job).start()
        for step in range(1, groups):
            part_copy(job, step).start()

    def sent_parts(job):
        for step in range(1, groups):
            part_copy(job, step).wait_send()

    def arrived_parts(job):
        own_part(job).wait()
        for step in range(1, groups):
            part_copy(job, step).wait_recv()

    def branch_copy(group):
        return pltpu.make_async_copy(
            grad_branch.at[:, pl.ds(group * share, share)], right.at[0, group], load_sem.at[group]
        )

    def product(job, dp, store):
        rows = pl.ds(pl.multiple_of(dp * panel, panel), panel)
        left = lefts[job // 2][:, rows].T
        for group in range(groups):
            store(
                slice(group * half, (group + 1) * half),
                jnp.dot(left, right[job // 2, group, :, half_columns(job)], preferred_element_type=F32),
            )

    def core_copy(m, step):
        return remote(
            core_buf.at[step], core_in.at[m % 2, step], core_send.at[step], core_recv.at[m % 2, step], place.sibling
        )

    def chip_copy(m, step):
        return remote(
            chip_buf.at[m % 2, step - 1], chip_in.at[m % 2, step - 1], chip_send.at[m % 2, step - 1],
            chip_recv.at[m % 2, step - 1], place.chip_device(place.chip_at(step)),
        )

    def line_copy(m, step):
        return remote(
            line_buf.at[m, step - 1], line_in.at[m, step - 1], line_send.at[m, step - 1], line_recv.at[m, step - 1],
            place.line_device(place.line_at(step)),
        )

    paired = groups == 4
    inner = (seq == 1) | (seq == 2)
    mate = seq + 1 - 2 * (seq % 2)

    def across(j):
        return 2 * (1 - seq // 2) + j

    def near_copy(m):
        return remote(
            line_buf.at[m, 0], line_in.at[m, 0], line_send.at[m, 0], line_recv.at[m, 0], place.line_device(mate)
        )

    def relay_copy(m, j):
        return remote(
            line_buf.at[m, 1 + j], line_in.at[m, 2 + j], line_send.at[m, 1 + j], line_recv.at[m, 2 + j],
            place.line_device(mate),
        )

    def across_copy(m, j):
        return remote(
            line_buf.at[m, 1 + j], line_in.at[m, 1], line_send.at[m, 1 + j], line_recv.at[m, 1],
            place.line_device(across(j)),
        )

    order = tuple(range(1, chips)) + (0,)

    def to_sibling(m):
        if m >= 2:
            pl.semaphore_wait(core_free, 1)
        for step in order:
            if m >= 1:
                core_copy(m - 1, step).wait_send()
            dp = 2 * place.chip_at(step) + 1 - place.core

            def store(columns, value, step=step):
                core_buf[step, :, columns] = value.astype(BF16)

            product(m, dp, store)
            core_copy(m, step).start()

    def to_chips(m):
        for step in order:
            dp = 2 * place.chip_at(step) + place.core
            core_copy(m, step).wait_recv()
            if step > 0:
                if m >= 2:
                    chip_copy(m - 2, step).wait_send()
                    pl.semaphore_wait(chip_free.at[step - 1], 1)

                def store(columns, value, step=step):
                    total = value + core_in[m % 2, step, :, columns].astype(F32)
                    chip_buf[m % 2, step - 1, :, columns] = total.astype(BF16)

            else:

                def store(columns, value):
                    kept[m % 2, :, columns] = value + core_in[m % 2, 0, :, columns].astype(F32)

            product(m, dp, store)
            if step > 0:
                chip_copy(m, step).start()
        if m + 2 < count:
            pl.semaphore_signal(core_free, inc=1, device_id=place.sibling, device_id_type=BY_MESH)

    def sum_chips(m):
        for step in range(1, chips):
            chip_copy(m, step).wait_recv()

        def block_sum(block):
            rows = pl.ds(pl.multiple_of(block * here, here), here)
            total = kept[m % 2, rows, :]
            for other in range(1, chips):
                total = total + chip_in[m % 2, other - 1, rows, :].astype(F32)
            return total

        if paired:
            line_buf[m, 0] = block_sum(mate).astype(BF16)
            for j in range(2):
                line_buf[m, 1 + j] = block_sum(across(j)).astype(BF16)
        else:
            for step in range(1, groups):
                line_buf[m, step - 1] = block_sum(place.line_at(step)).astype(BF16)
        line_own[m] = block_sum(seq)
        if m + 2 < count:
            for step in range(1, chips):
                pl.semaphore_signal(
                    chip_free.at[step - 1], inc=1, device_id=place.chip_device(place.chip_at(step)),
                    device_id_type=BY_MESH,
                )

    def send_line(m):
        if paired:
            near_copy(m).start()

            @pl.when(jnp.logical_not(inner))
            def _():
                for j in range(2):
                    relay_copy(m, j).start()

        else:
            for step in range(1, groups):
                line_copy(m, step).start()

    def relay(m):
        if not paired:
            return

        @pl.when(inner)
        def _():
            for j in range(2):
                relay_copy(m, j).wait_recv()
                line_buf[m, 1 + j] = (line_buf[m, 1 + j].astype(F32) + line_in[m, 2 + j].astype(F32)).astype(BF16)
                across_copy(m, j).start()

    def store_grad(m, group):
        return pltpu.make_async_copy(
            line_own.at[m, :, pl.ds(group * half, half)], grads[m // 2].at[:, half_columns(m, group)],
            store_sem.at[m, group],
        )

    def settle(m):
        total = line_own[m]
        if paired:
            near_copy(m).wait_recv()
            across_copy(m, 0).wait_recv()
            total = total + line_in[m, 0].astype(F32) + line_in[m, 1].astype(F32)
        else:
            for step in range(1, groups):
                line_copy(m, step).wait_recv()
                total = total + line_in[m, step - 1].astype(F32)
        line_own[m] = total
        for group in range(groups):
            store_grad(m, group).start()

    width = memory.shape[1]
    panels = width // panel
    piece = memory.shape[0]

    def weight_copy(slot, which, source, index):
        rows = pl.ds(pl.multiple_of(index * panel, panel), panel)
        return pltpu.make_async_copy(source.at[rows, :], weight.at[slot, which], weight_sem.at[slot, which])

    def panel_copy(slot, index):
        columns = pl.ds(pl.multiple_of(index * panel, panel), panel)
        return pltpu.make_async_copy(panel_out.at[slot], grad_memory.at[:, columns], panel_sem.at[slot])

    def back(slot, which, m):
        total = jnp.zeros((piece, panel), F32)
        for group in range(groups):
            columns = slice(group * share, (group + 1) * share)
            total = total + lax.dot_general(
                right[m, group], weight[slot, which, :, columns], NT, preferred_element_type=F32
            )
        return total

    def memory_gradient():
        weight_copy(0, 0, all_value, 0).start()
        weight_copy(0, 1, all_key, 0).start()

        def one(index, _):
            slot = lax.rem(index, 2)

            @pl.when(index + 1 < panels)
            def _():
                weight_copy(1 - slot, 0, all_value, index + 1).start()
                weight_copy(1 - slot, 1, all_key, index + 1).start()

            weight_copy(slot, 0, all_value, index).wait()
            weight_copy(slot, 1, all_key, index).wait()

            @pl.when(index >= 2)
            def _():
                panel_copy(slot, index - 2).wait()

            panel_out[slot] = back(slot, 0, 1) + back(slot, 1, 2)
            panel_copy(slot, index).start()
            return 0

        lax.fori_loop(0, panels, one, 0)
        for index in range(max(panels - 2, 0), panels):
            panel_copy(index % 2, index).wait()

    def query_gradient():
        weight_copy(0, 0, all_query, 0).start()

        def one(index, _):
            slot = lax.rem(index, 2)

            @pl.when(index + 1 < panels)
            def _():
                weight_copy(1 - slot, 0, all_query, index + 1).start()

            weight_copy(slot, 0, all_query, index).wait()
            columns = pl.ds(pl.multiple_of(index * panel, panel), panel)
            grad_attn_in[:, columns] = back(slot, 0, 3)
            return 0

        lax.fori_loop(0, panels, one, 0)

    some = mid_buf.shape[1]
    batches = piece // some

    def batch_rows(index):
        return pl.ds(pl.multiple_of(index * some, some), some)

    def mid_copy(slot, index):
        return pltpu.make_async_copy(grad_mid.at[batch_rows(index), :], mid_buf.at[slot], mid_sem.at[slot])

    def hidden_copy(slot, index):
        return pltpu.make_async_copy(hidden.at[batch_rows(index), :], hidden_buf.at[slot], hidden_sem.at[slot])

    def hidden_store(index):
        rows = batch_rows(index)
        return pltpu.make_async_copy(grad_attn_in.at[rows, :], grad_hidden.at[rows, :], panel_sem.at[0])

    def hidden_gradient():
        gain_term[...] = jnp.zeros_like(gain_term)
        mid_copy(0, 0).start()
        hidden_copy(0, 0).start()

        def one(index, _):
            slot = lax.rem(index, 2)

            @pl.when(index + 1 < batches)
            def _():
                mid_copy(1 - slot, index + 1).start()
                hidden_copy(1 - slot, index + 1).start()

            mid_copy(slot, index).wait()
            hidden_copy(slot, index).wait()
            rows = batch_rows(index)
            x = hidden_buf[slot].astype(F32)
            rstd = lax.rsqrt(jnp.mean(x * x, axis=-1, keepdims=True) + EPSILON)
            normed = x * rstd
            grad = grad_attn_in[rows, :]
            gain_term[0:1, :] += jnp.sum(normed * grad, axis=0, keepdims=True)
            scaled = grad * gain_rows[0:1, :]
            shift = jnp.mean(scaled * normed, axis=-1, keepdims=True)
            grad_attn_in[rows, :] = mid_buf[slot] + rstd * (scaled - normed * shift)
            hidden_store(index).start()
            return 0

        lax.fori_loop(0, batches, one, 0)

    devices = dp_count * groups
    me = place.dp * groups + seq

    def gain_copy(step):
        owner = lax.rem(me + step, devices)
        return remote(
            gain_buf.at[owner], gain_in.at[step], gain_send, gain_recv, {"dp": owner // groups, "seq": owner % groups}
        )

    def send_gains():
        gain_term[1:2, :] = gain_ffn_term[0:1, :]
        per = 128 // here
        for owner in range(devices):
            tile = gain_term[:, owner // per * 128 : (owner // per + 1) * 128]
            shift = owner % per * here
            gain_buf[owner] = pltpu.roll(tile, 128 - shift, 1) if shift else tile

        def one(step, _):
            gain_copy(step).start()
            return 0

        lax.fori_loop(1, devices, one, 0)

    def sum_gains():
        remote(
            gain_buf.at[pl.ds(0, devices - 1)], gain_in.at[pl.ds(1, devices - 1)], gain_send, gain_recv, place.sibling
        ).wait()
        total = gain_buf[me]
        for step in range(1, devices):
            total = total + gain_in[step]
        grad_gains[...] = total

    everyone = pltpu.get_barrier_semaphore()

    def greet(step, _):
        other = lax.rem(me + step, devices)
        pl.semaphore_signal(
            everyone, inc=1, device_id={"dp": other // groups, "seq": other % groups}, device_id_type=BY_MESH
        )
        return 0

    lax.fori_loop(1, devices, greet, 0)
    pl.semaphore_wait(everyone, devices - 1)
    send_parts(2)
    send_parts(3)
    for group in range(groups):
        branch_copy(group).start()
    for group in range(groups):
        branch_copy(group).wait()
    for job in range(2):
        to_sibling(job)
        to_chips(job)
    for job in range(2, count):
        sent_parts(job)
        if job + 2 < count:
            send_parts(job + 2)
        if job == count - 1:
            for earlier in range(job - 2):
                send_line(earlier)
        arrived_parts(job)
        to_sibling(job)
        sum_chips(job - 2)
        if job == count - 1:
            send_line(job - 2)
        to_chips(job)
        if job == 5:
            memory_gradient()
    sum_chips(6)
    send_line(6)
    query_gradient()
    relay(0)
    relay(1)
    relay(2)
    hidden_gradient()
    relay(3)
    relay(4)
    relay(5)
    send_gains()
    sum_chips(7)
    send_line(7)
    for job in range(6):
        settle(job)
    relay(6)
    settle(6)
    relay(7)
    settle(7)
    sum_gains()
    pltpu.make_async_copy(grad_attn_in, grad_hidden, panel_sem.at[0]).wait()
    for step in range(chips):
        core_copy(count - 1, step).wait_send()
    for job in range(count):
        if job >= count - 2:
            for step in range(1, chips):
                chip_copy(job, step).wait_send()
        if paired:
            near_copy(job).wait_send()
            for j in range(2):
                across_copy(job, j).wait_send()
        else:
            for step in range(1, groups):
                line_copy(job, step).wait_send()
        for group in range(groups):
            store_grad(job, group).wait()


def reduce_call(dp_count, groups, piece, width, here):
    chips = dp_count // 2
    share = width // groups
    panel = groups * here
    hbm = pl.BlockSpec(memory_space=pl.ANY)
    vmem = pl.BlockSpec(memory_space=pltpu.VMEM)
    grad = jax.ShapeDtypeStruct((here, width), F32)
    tokens = jax.ShapeDtypeStruct((piece, width), F32)
    some = min(64, piece)
    devices = dp_count * groups
    dma = pltpu.SemaphoreType.DMA
    others = max(chips - 1, 1)
    return pl.pallas_call(
        functools.partial(reduce_kernel, dp_count, groups, here),
        in_specs=[vmem] * 5 + [hbm] * 9,
        out_specs=[hbm] * 6 + [vmem],
        out_shape=(grad, grad, grad, grad, tokens, tokens, jax.ShapeDtypeStruct((8, 128), F32)),
        scratch_shapes=[
            pltpu.VMEM((4, groups, piece, share), BF16),
            pltpu.VMEM((chips, panel, width // 2), BF16),
            pltpu.VMEM((2, chips, panel, width // 2), BF16),
            pltpu.VMEM((2, others, panel, width // 2), BF16),
            pltpu.VMEM((2, others, panel, width // 2), BF16),
            pltpu.VMEM((2, panel, width // 2), F32),
            pltpu.VMEM((8, max(groups - 1, 3), here, width // 2), BF16),
            pltpu.VMEM((8, max(groups - 1, 4), here, width // 2), BF16),
            pltpu.VMEM((8, here, width // 2), F32),
            dma((8, groups - 1)), dma((8, groups - 1)), dma((8,)), dma((groups,)),
            dma((chips,)), dma((2, chips)),
            dma((2, others)), dma((2, others)),
            dma((8, max(groups - 1, 3))), dma((8, max(groups - 1, 4))), dma((8, groups)),
            pltpu.SemaphoreType.REGULAR, pltpu.SemaphoreType.REGULAR((others,)),
            pltpu.VMEM((2, 2, panel, width), BF16),
            pltpu.VMEM((2, piece, panel), F32),
            pltpu.VMEM((piece, width), F32),
            pltpu.VMEM((2, some, width), F32),
            pltpu.VMEM((2, some, width), BF16),
            pltpu.VMEM((8, width), F32),
            pltpu.VMEM((devices, 8, 128), F32),
            pltpu.VMEM((devices, 8, 128), F32),
            dma((2, 2)), dma((2,)), dma((2,)), dma((2,)), dma, dma,
        ],
        compiler_params=pltpu.CompilerParams(
            collective_id=2, has_side_effects=True, vmem_limit_bytes=63 * 1024 * 1024
        ),
        cost_estimate=pl.CostEstimate(
            flops=128 * piece * width * width, transcendentals=0, bytes_accessed=16 * width * width
        ),
        name="weight_gradients",
    )


def middle_kernel(
    dp_count, groups,
    gain_rows, hidden, context_heads, grad_own, out_rows, gate_rows, up_rows, down_rows, all_grad,
    context, gain_term, layer_out, grad_mid, grad_branch, grad_heads, grad_down, grad_gate, grad_up,
    all_ffn, grad_acts, acts, grad_gates, grad_ups, core_in, chip_in, branch_core, branch_out, branch_in, term_in,
    gate_w, up_w, down_w, out_w, mid, ffn_in, own_total, chip_out, term_buf,
    col_send, col_recv, col_own, weight_sem, out_sem, chip_send, chip_recv, core_send, core_recv, own_sem,
    x_sem, dy_sem, act_sem, sum_send, sum_recv, load_sem, far_send, far_recv, left_sem, right_sem, branch_sem,
    part_send, part_recv, plane_send, plane_recv,
    term_send, term_recv, rows_sem, gm_sem, gb_sem, head_send, head_recv, head_own,
):
    place = Place(dp_count, groups)
    chips, seq, core = place.chips, place.seq, place.core
    piece, width = hidden.shape
    share = width // groups
    unit_rows = gate_rows.shape[0]
    padded = gate_w.shape[0]
    wide = (gate_rows, up_rows, down_rows)
    kept = (gate_w, up_w, down_w)

    def weight_copy(i):
        return pltpu.make_async_copy(wide[i], kept[i].at[pl.ds(0, unit_rows), :], weight_sem.at[i])

    def group_columns(group):
        return pl.ds(pl.multiple_of(group * share, share), share)

    def out_copy(group, slot):
        rows = pl.ds(pl.multiple_of(group * share, share), share)
        return pltpu.make_async_copy(out_rows.at[rows, :], out_w.at[slot], out_sem.at[slot])

    def collect(step):
        other = place.line_at(step)
        return remote(
            context_heads.at[other], context.at[:, group_columns(seq)], col_send.at[step - 1], col_recv.at[step - 1],
            place.line_device(other),
        )

    def came_from(step):
        return lax.rem(seq + groups - step, groups)

    place.barrier()
    for step in range(1, groups):
        collect(step).start()
    own_columns = pltpu.make_async_copy(context_heads.at[seq], context.at[:, group_columns(seq)], col_own)
    own_columns.start()
    out_copy(seq, 0).start()
    hidden_copy = pltpu.make_async_copy(hidden, ffn_in, own_sem)
    hidden_copy.start()
    for i in range(3):
        weight_copy(i).start()
        if padded > unit_rows:
            kept[i][unit_rows:, :] = jnp.zeros((padded - unit_rows, width), BF16)

    def act_gradients(dy_buf, out_buf):
        def dy_copy(dp, slot):
            return pltpu.make_async_copy(all_grad.at[dp], dy_buf.at[slot], dy_sem.at[slot])

        def store(dp, slot):
            return pltpu.make_async_copy(out_buf.at[slot], grad_acts.at[dp], act_sem.at[slot, 0])

        dy_copy(0, 0).start()
        weight_copy(2).wait()

        def one(dp, _):
            slot = dp % 2

            @pl.when(dp + 1 < dp_count)
            def _():
                dy_copy(dp + 1, 1 - slot).start()

            dy_copy(dp, slot).wait()

            @pl.when(dp >= 2)
            def _():
                store(dp - 2, slot).wait()

            out_buf[slot] = mxu(dy_buf[slot], down_w[...], NT)
            store(dp, slot).start()
            return 0

        lax.fori_loop(0, dp_count, one, 0)
        for dp in range(dp_count - 2, dp_count):
            store(dp, dp % 2).wait()

    pl.run_scoped(act_gradients, pltpu.VMEM((2, piece, width), BF16), pltpu.VMEM((2, piece, padded), F32))

    for step in range(groups):
        slot = step % 2
        group = came_from(step)
        if step + 1 < groups:
            out_copy(came_from(step + 1), 1 - slot).start()
        if step == 0:
            own_columns.wait()
        else:
            columns = context.at[:, group_columns(group)]
            remote(columns, columns, col_send.at[step - 1], col_recv.at[step - 1], place.sibling).wait_recv()
        out_copy(group, slot).wait()
        left = context[:, group_columns(group)]
        if step == 0:
            hidden_copy.wait()

        def project(part, _, left=left, slot=slot, step=step):
            columns = pl.ds(pl.multiple_of(part * share, share), share)
            value = mxu(left, out_w[slot, :, columns], NN)
            if step == 0:
                mid[:, columns] = ffn_in[:, columns].astype(F32) + value
            else:
                mid[:, columns] += value
            return 0

        lax.fori_loop(0, groups, project, 0)

    some = min(64, piece)
    batches = piece // some

    def batch(index):
        return pl.ds(pl.multiple_of(index * some, some), some)

    def normalize(index, _):
        rows = batch(index)
        x = mid[rows, :]
        rstd = lax.rsqrt(jnp.mean(x * x, axis=-1, keepdims=True) + EPSILON)
        ffn_in[rows, :] = (x * rstd * gain_rows[1:2, :]).astype(BF16)
        return 0

    lax.fori_loop(0, batches, normalize, 0)

    def to_chip(step):
        return remote(
            ffn_in, all_ffn.at[place.dp], chip_send.at[step - 1], chip_recv.at[step - 1],
            place.chip_device(place.chip_at(step)),
        )

    def to_sibling(step):
        dp = 2 * place.chip_at(step) + core
        return remote(all_ffn.at[dp], all_ffn.at[dp], core_send.at[step], core_recv.at[step], place.sibling)

    own_ffn = pltpu.make_async_copy(ffn_in, all_ffn.at[place.dp], own_sem)
    own_ffn.start()
    square = chips == 4
    for step in range(1, 3 if square else chips):
        to_chip(step).start()
    own_ffn.wait()
    to_sibling(0).start()
    for i in range(2):
        weight_copy(i).wait()

    def hand_on(step):
        half = piece // 2
        dp = 2 * place.chip_at(step) + core
        rows = all_ffn.at[dp, pl.ds((step - 1) * half, half), :]
        return remote(rows, rows, chip_send.at[2], chip_recv.at[2], place.chip_device(place.chip_at(3 - step)))

    pieces = 2 * chips
    stored = (acts, grad_gates, grad_ups)

    def piece_of(u, own_first):
        step, which = u // 2, u % 2
        mine = 1 - which if own_first else which
        return step, which, 2 * place.chip_at(step) + mine * core + (1 - mine) * (1 - core)

    def hidden_units(x_buf, da_buf, act_buf):
        def x_copy(u):
            dp = piece_of(u, True)[2]
            return pltpu.make_async_copy(all_ffn.at[dp], x_buf.at[u % 2], x_sem.at[u % 2])

        def da_copy(u):
            dp = piece_of(u, True)[2]
            return pltpu.make_async_copy(grad_acts.at[dp], da_buf.at[u % 2], dy_sem.at[u % 2])

        def act_copy(u, i):
            dp = piece_of(u, True)[2]
            return pltpu.make_async_copy(act_buf.at[u % 2, i], stored[i].at[dp], act_sem.at[u % 2, i])

        def fetch(u):
            step, which, _ = piece_of(u, True)
            if square:

                @pl.when(u == 2)
                def _():
                    for near in (1, 2):
                        to_chip(near).wait_recv()
                        to_sibling(near).start()
                        hand_on(near).start()

                @pl.when(u == 6)
                def _():
                    to_chip(3).wait_recv()
                    to_sibling(3).start()

            else:

                @pl.when((which == 0) & (step > 0))
                def _():
                    to_chip(step).wait_recv()
                    to_sibling(step).start()

            @pl.when(which == 1)
            def _():
                to_sibling(step).wait_recv()

            x_copy(u).start()

        da_copy(0).start()

        def one(u, _):
            slot = u % 2
            ahead = u % 2 == 1
            if square:
                ahead = ahead | (u == 4)
            next_ahead = (u + 1 < pieces) & (u % 2 == 0)
            if square:
                next_ahead = next_ahead | (u == 3)

            @pl.when(jnp.logical_not(ahead))
            def _():
                fetch(u)

            @pl.when(next_ahead)
            def _():
                fetch(u + 1)

            @pl.when(u + 1 < pieces)
            def _():
                da_copy(u + 1).start()

            @pl.when(u >= 2)
            def _():
                for i in range(3):
                    act_copy(u - 2, i).wait()

            x_copy(u).wait()
            gate = mxu(x_buf[slot], gate_w[...], NT)
            up = mxu(x_buf[slot], up_w[...], NT)
            sig = 1.0 / (1.0 + jnp.exp(-gate))
            da_copy(u).wait()
            grad_act = da_buf[slot]
            act_buf[slot, 0] = (gate * sig * up).astype(BF16)
            act_buf[slot, 1] = (grad_act * up * sig * (1.0 + gate * (1.0 - sig))).astype(BF16)
            act_buf[slot, 2] = (grad_act * gate * sig).astype(BF16)
            for i in range(3):
                act_copy(u, i).start()
            return 0

        lax.fori_loop(0, pieces, one, 0)
        for u in range(max(pieces - 2, 0), pieces):
            for i in range(3):
                act_copy(u, i).wait()

    pl.run_scoped(
        hidden_units,
        pltpu.VMEM((2, piece, width), BF16), pltpu.VMEM((2, piece, padded), F32),
        pltpu.VMEM((2, 3, piece, padded), BF16),
    )

    def far_copy(step):
        return remote(
            chip_out.at[step - 1], chip_in.at[step - 1], far_send.at[step - 1],
            far_recv.at[step - 1], place.chip_device(place.chip_at(step)),
        )

    def input_sum(act_buf, core_out, load_buf):
        sources, rights, own = (grad_gates, grad_ups), (gate_w, up_w), own_total
        used = len(sources)

        def place_of(u):
            _, which, dp = piece_of(pieces - 2 + u - 4 * (u // 2), False)
            return chips - 1 - u // 2, which, dp

        def act_copy(u, i):
            dp = place_of(u)[2]
            return pltpu.make_async_copy(sources[i].at[dp], act_buf.at[u % 2, i], act_sem.at[u % 2, i])

        def sum_copy(step):
            return remote(
                core_out, core_in.at[step], sum_send, sum_recv.at[step], place.sibling
            )

        def load_copy(step):
            return pltpu.make_async_copy(core_in.at[step], load_buf, load_sem)

        for i in range(used):
            act_copy(0, i).start()

        def one(u, _):
            step, which, dp = place_of(u)
            slot = u % 2

            @pl.when(u + 1 < pieces)
            def _():
                for i in range(used):
                    act_copy(u + 1, i).start()

            for i in range(used):
                act_copy(u, i).wait()

            @pl.when((which == 0) & (u >= 2))
            def _():
                sum_copy(step + 1).wait_send()

            @pl.when(which == 1)
            def _():
                sum_copy(step).wait_recv()
                load_copy(step).start()
                load_copy(step).wait()

            def columns_of(part, _):
                columns = group_columns(part)
                value = mxu(act_buf[slot, 0], rights[0][:, columns], NN)
                for i in range(1, used):
                    value = value + mxu(act_buf[slot, i], rights[i][:, columns], NN)

                @pl.when(which == 0)
                def _():
                    core_out[:, columns] = value.astype(BF16)

                @pl.when((which == 1) & (step > 0))
                def _():
                    chip_out[step - 1, :, columns] = (value + load_buf[:, columns].astype(F32)).astype(BF16)

                @pl.when((which == 1) & (step == 0))
                def _():
                    own[:, columns] = value + load_buf[:, columns].astype(F32)

                return 0

            lax.fori_loop(0, groups, columns_of, 0)

            @pl.when(which == 0)
            def _():
                sum_copy(step).start()

            @pl.when((which == 1) & (step > 0))
            def _():
                far_copy(step).start()

            return 0

        lax.fori_loop(0, pieces, one, 0)
        sum_copy(0).wait_send()

    block = unit_rows // groups

    paired = groups == 4
    side = seq // 2
    inner = (seq == 1) | (seq == 2)
    partner = seq + 1 - 2 * (seq % 2)

    def across(j):
        return 2 * (1 - side) + j

    def term_rows(i, owner):
        return term_buf.at[i, pl.ds(pl.multiple_of(owner * block, block), block), :]

    def term_copy(i, step):
        other = place.line_at(step)
        return remote(
            term_rows(i, other), term_in.at[i, step - 1], term_send.at[i, step - 1], term_recv.at[i, step - 1],
            place.line_device(other),
        )

    def near_copy(i):
        return remote(
            term_rows(i, partner), term_in.at[i, 0], term_send.at[i, 0], term_recv.at[i, 0], place.line_device(partner)
        )

    def relay_copy(i, j):
        return remote(
            term_rows(i, across(j)), term_in.at[i, 2 + j], term_send.at[i, 1 + j], term_recv.at[i, 2 + j],
            place.line_device(partner),
        )

    def across_copy(i, j):
        return remote(
            term_rows(i, across(j)), term_in.at[i, 1], term_send.at[i, 1 + j], term_recv.at[i, 1],
            place.line_device(across(j)),
        )

    def send_term(i):
        if paired:
            near_copy(i).start()

            @pl.when(jnp.logical_not(inner))
            def _():
                for j in range(2):
                    relay_copy(i, j).start()

        else:
            for step in range(1, groups):
                term_copy(i, step).start()

    def relay_term(i, buf):
        if not paired:
            return

        @pl.when(inner)
        def _():
            for j in range(2):
                relay_copy(i, j).wait_recv()
                load = pltpu.make_async_copy(term_in.at[i, 2 + j], buf, left_sem.at[0])
                load.start()
                load.wait()
                rows = pl.ds(pl.multiple_of(across(j) * block, block), block)
                term_buf[i, rows, :] = (term_buf[i, rows, :].astype(F32) + buf[...].astype(F32)).astype(BF16)
                across_copy(i, j).start()

    def arrived_terms(i):
        if not paired:
            for step in range(1, groups):
                term_copy(i, step).wait()
            return range(groups - 1)
        near_copy(i).wait()
        across_copy(i, 0).wait_recv()
        for j in range(2):
            across_copy(i, j).wait_send()
        return range(2)

    def weight_terms(left_buf, acc):
        for i, (lefts, rights) in enumerate(((acts, all_grad), (grad_gates, all_ffn), (grad_ups, all_ffn))):

            def copies(dp, slot, lefts=lefts, rights=rights):
                return (
                    pltpu.make_async_copy(lefts.at[dp], left_buf.at[slot], left_sem.at[slot]),
                    pltpu.make_async_copy(rights.at[dp], out_w.at[slot], right_sem.at[slot]),
                )

            for copy in copies(0, 0):
                copy.start()

            def one(dp, _, copies=copies):
                slot = dp % 2

                @pl.when(dp + 1 < dp_count)
                def _():
                    for copy in copies(dp + 1, 1 - slot):
                        copy.start()

                for copy in copies(dp, slot):
                    copy.wait()
                left = left_buf[slot].T


                @pl.when(dp == 0)
                def _():
                    acc[...] = jnp.zeros_like(acc)

                acc[...] += jnp.dot(left, out_w[slot], preferred_element_type=F32)
                return 0

            lax.fori_loop(0, dp_count, one, 0)
            term_buf[i] = acc[0:unit_rows, :].astype(BF16)
            send_term(i)

    pl.run_scoped(weight_terms, pltpu.VMEM((2, piece, padded), BF16), pltpu.VMEM((padded, width), F32))

    pl.run_scoped(
        input_sum,
        pltpu.VMEM((2, 2, piece, padded), BF16), pltpu.VMEM((piece, width), BF16), pltpu.VMEM((piece, width), BF16),
    )

    def plane_copy(step):
        return remote(
            branch_out.at[step], branch_in.at[step - 1], plane_send.at[step - 1], plane_recv.at[step - 1],
            place.chip_device(place.chip_at(step)),
        )

    def branch_parts(relay_buf, act_buf, branch_buf, core_out, load_buf):
        relay_term(0, relay_buf)

        def act_copy(u):
            return pltpu.make_async_copy(acts.at[piece_of(u, False)[2]], act_buf.at[u % 2], act_sem.at[u % 2, 0])

        def part_copy(step):
            return remote(core_out, branch_core.at[step], part_send, part_recv.at[step], place.sibling)

        def load_copy(step):
            return pltpu.make_async_copy(branch_core.at[step], load_buf, load_sem)

        def store(step):
            return pltpu.make_async_copy(branch_buf.at[step % 2], branch_out.at[step], branch_sem.at[step % 2])

        act_copy(0).start()

        def one(u, _):
            step, which, dp = piece_of(u, False)
            slot = u % 2

            @pl.when(u + 1 < pieces)
            def _():
                act_copy(u + 1).start()

            act_copy(u).wait()

            @pl.when((which == 0) & (step > 0))
            def _():
                part_copy(step - 1).wait_send()

            @pl.when(which == 1)
            def _():
                part_copy(step).wait_recv()
                load_copy(step).start()

                @pl.when(step > 1)
                def _():
                    store(step - 2).wait()

                load_copy(step).wait()

            def part_of(part, _):
                columns = group_columns(part)
                value = mxu(act_buf[slot], down_w[:, columns], NN)

                @pl.when(which == 0)
                def _():
                    core_out[:, columns] = value.astype(BF16)

                @pl.when(which == 1)
                def _():
                    branch_buf[step % 2, :, columns] = (value + load_buf[:, columns].astype(F32)).astype(BF16)

                return 0

            lax.fori_loop(0, groups, part_of, 0)

            @pl.when(which == 0)
            def _():
                part_copy(step).start()

            @pl.when(which == 1)
            def _():
                store(step).start()

            return 0

        lax.fori_loop(0, pieces, one, 0)
        part_copy(chips - 1).wait_send()
        for step in range(max(chips - 2, 0), chips):
            store(step).wait()
        relay_term(1, relay_buf)

    pl.run_scoped(
        branch_parts,
        pltpu.VMEM((block, width), BF16), pltpu.VMEM((2, piece, padded), BF16), pltpu.VMEM((2, piece, width), BF16),
        pltpu.VMEM((piece, width), BF16), pltpu.VMEM((piece, width), BF16),
    )

    for step in range(1, chips):
        landed = chip_in.at[step - 1]
        remote(landed, landed, far_send.at[step - 1], far_recv.at[step - 1], place.sibling).wait_recv()
    for step in range(1, chips):
        plane_copy(step).start()
    for step in range(1, chips):
        to_chip(step).wait_send()
    gain_term[...] = jnp.zeros_like(gain_term)

    def norm_and_heads(rows_buf, mid_buf, layer_buf, heads_buf, sum_buf):
        def rows_copy(index, step, slot):
            source = grad_own.at[batch(index), :] if step == 0 else chip_in.at[step - 1, batch(index), :]
            return pltpu.make_async_copy(source, rows_buf.at[slot, step], rows_sem.at[slot, step])

        def layer_rows(index, step, slot):
            source = branch_out.at[0] if step == 0 else branch_in.at[step - 1]
            return pltpu.make_async_copy(
                source.at[batch(index), :], rows_buf.at[slot, step], rows_sem.at[slot, step]
            )

        def layer_copy(index, slot):
            return pltpu.make_async_copy(layer_buf.at[slot], layer_out.at[batch(index), :], gm_sem.at[slot])

        def grad_mid_copy(index, slot):
            return pltpu.make_async_copy(mid_buf.at[slot], grad_mid.at[batch(index), :], gm_sem.at[slot])

        for step in range(chips):
            rows_copy(0, step, 0).start()

        def norm_back(index, _):
            slot = index % 2

            @pl.when(index + 1 < batches)
            def _():
                for step in range(chips):
                    rows_copy(index + 1, step, 1 - slot).start()

            for step in range(chips):
                rows_copy(index, step, slot).wait()

            @pl.when(index >= 2)
            def _():
                grad_mid_copy(index - 2, slot).wait()

            rows = batch(index)
            grad = own_total[rows, :]
            for step in range(1, chips):
                grad = grad + rows_buf[slot, step].astype(F32)
            x = mid[rows, :]
            rstd = lax.rsqrt(jnp.mean(x * x, axis=-1, keepdims=True) + EPSILON)
            normed = x * rstd
            gain_term[0:1, :] += jnp.sum(normed * grad, axis=0, keepdims=True)
            scaled = grad * gain_rows[1:2, :]
            shift = jnp.mean(scaled * normed, axis=-1, keepdims=True)
            total = rows_buf[slot, 0].astype(F32) + rstd * (scaled - normed * shift)
            mid_buf[slot] = total
            ffn_in[rows, :] = total.astype(BF16)
            grad_mid_copy(index, slot).start()
            return 0

        lax.fori_loop(0, batches, norm_back, 0)
        grad_branch_copy = pltpu.make_async_copy(ffn_in, grad_branch, gb_sem)
        grad_branch_copy.start()
        for index in range(max(batches - 2, 0), batches):
            grad_mid_copy(index, index % 2).wait()

        def head_copy(step):
            other = place.line_at(step)
            return remote(
                heads_buf.at[other], grad_heads.at[seq], head_send.at[step - 1], head_recv.at[step - 1],
                place.line_device(other),
            )

        own_heads = pltpu.make_async_copy(heads_buf.at[seq], grad_heads.at[seq], head_own)
        order = tuple(range(1, groups)) + (0,)
        out_copy(place.line_at(order[0]), 0).start()
        for at, step in enumerate(order):
            group = place.line_at(step)
            if at + 1 < groups:
                out_copy(place.line_at(order[at + 1]), (at + 1) % 2).start()
            out_copy(group, at % 2).wait()
            heads_buf[group] = mxu(ffn_in[...], out_w[at % 2], NT).astype(BF16)
            if step > 0:
                head_copy(step).start()
            else:
                own_heads.start()

        relay_term(2, sum_buf.at[0])

        for i, target in enumerate((grad_down, grad_gate, grad_up)):
            landed = arrived_terms(i)
            for j in landed:
                load = pltpu.make_async_copy(term_in.at[i, j], sum_buf.at[j], rows_sem.at[0, 0])
                load.start()
                load.wait()
            total = term_buf[i, pl.ds(pl.multiple_of(seq * block, block), block), :].astype(F32)
            for j in landed:
                total = total + sum_buf[j].astype(F32)
            own_total[0:block, :] = total
            store = pltpu.make_async_copy(own_total.at[pl.ds(0, block), :], target, gm_sem.at[0])
            store.start()
            store.wait()
        for step in range(1, chips):
            plane_copy(step).wait()
        for step in range(chips):
            layer_rows(0, step, 0).start()

        def layer(index, _):
            slot = index % 2

            @pl.when(index + 1 < batches)
            def _():
                for step in range(chips):
                    layer_rows(index + 1, step, 1 - slot).start()

            for step in range(chips):
                layer_rows(index, step, slot).wait()

            @pl.when(index >= 2)
            def _():
                layer_copy(index - 2, slot).wait()

            total = mid[batch(index), :]
            for step in range(chips):
                total = total + rows_buf[slot, step].astype(F32)
            layer_buf[slot] = total.astype(BF16)
            layer_copy(index, slot).start()
            return 0

        lax.fori_loop(0, batches, layer, 0)
        for index in range(max(batches - 2, 0), batches):
            layer_copy(index, index % 2).wait()
        grad_branch_copy.wait()
        own_heads.wait()
        for step in range(1, groups):
            head_copy(step).wait()

    pl.run_scoped(
        norm_and_heads,
        pltpu.VMEM((2, chips, some, width), BF16), pltpu.VMEM((2, some, width), F32),
        pltpu.VMEM((2, some, width), BF16), pltpu.VMEM((groups, piece, share), BF16), pltpu.VMEM((groups - 1, block, width), BF16),
    )
    for step in range(1, groups):
        collect(step).wait_send()
    for step in range(chips):
        to_sibling(step).wait_send()
    for step in range(1, chips):
        far_copy(step).wait_send()


def middle_call(dp_count, groups, piece, width, unit_rows):
    chips = dp_count // 2
    share = width // groups
    assert share == piece
    padded = -(-unit_rows // 128) * 128
    block = unit_rows // groups
    others = max(chips - 1, 1)
    hbm = pl.BlockSpec(memory_space=pl.ANY)
    vmem = pl.BlockSpec(memory_space=pltpu.VMEM)
    dma = pltpu.SemaphoreType.DMA
    shape = jax.ShapeDtypeStruct
    return pl.pallas_call(
        functools.partial(middle_kernel, dp_count, groups),
        in_specs=[vmem] + [hbm] * 8,
        out_specs=[vmem, vmem] + [hbm] * 18,
        out_shape=(
            shape((piece, width), BF16),
            shape((8, width), F32),
            shape((piece, width), BF16),
            shape((piece, width), F32),
            shape((piece, width), BF16),
            shape((groups, piece, share), BF16),
            shape((block, width), F32),
            shape((block, width), F32),
            shape((block, width), F32),
            shape((dp_count, piece, width), BF16),
            shape((dp_count, piece, padded), F32),
            shape((dp_count, piece, padded), BF16),
            shape((dp_count, piece, padded), BF16),
            shape((dp_count, piece, padded), BF16),
            shape((chips, piece, width), BF16),
            shape((others, piece, width), BF16),
            shape((chips, piece, width), BF16),
            shape((chips, piece, width), BF16),
            shape((others, piece, width), BF16),
            shape((3, max(groups - 1, 4), block, width), BF16),
        ),
        scratch_shapes=[
            pltpu.VMEM((padded, width), BF16), pltpu.VMEM((padded, width), BF16), pltpu.VMEM((padded, width), BF16),
            pltpu.VMEM((2, share, width), BF16),
            pltpu.VMEM((piece, width), F32),
            pltpu.VMEM((piece, width), BF16),
            pltpu.VMEM((piece, width), F32),
            pltpu.VMEM((others, piece, width), BF16),
            pltpu.VMEM((3, unit_rows, width), BF16),
            dma((groups - 1,)), dma((groups - 1,)), dma, dma((3,)), dma((2,)),
            dma((others,)), dma((others,)), dma((chips,)), dma((chips,)), dma,
            dma((2,)), dma((2,)), dma((2, 3)),
            dma, dma((chips,)), dma, dma((others,)), dma((others,)),
            dma((2,)), dma((2,)), dma((2,)),
            dma, dma((chips,)), dma((others,)), dma((others,)), dma((3, max(groups - 1, 4))), dma((3, max(groups - 1, 4))),
            dma((2, chips)), dma((2,)), dma,
            dma((groups - 1,)), dma((groups - 1,)), dma,
        ],
        compiler_params=pltpu.CompilerParams(
            collective_id=5, has_side_effects=True, vmem_limit_bytes=63 * 1024 * 1024
        ),
        cost_estimate=pl.CostEstimate(
            flops=128 * piece * width * width, transcendentals=0, bytes_accessed=64 * width * width
        ),
        name="feed_forward",
    )


def shards(
    hidden_in, memory, segments, gain_attn, w_query, w_key, w_value, w_out, gain_ffn, w_gate, w_up, w_down, cotangent
):
    seqs, piece, width = hidden_in.shape
    groups = lax.axis_size("seq")
    dp_count = lax.axis_size("dp")
    assert seqs == 1
    length = piece * groups
    share = width // groups
    heads = share // HEAD_DIM
    here = w_query.shape[0]
    block = min(256, length)
    tokens = hidden_in.reshape(piece, width)
    mem = memory.reshape(piece, width)
    grad_out = cotangent.reshape(piece, width)

    attend_forward, attend_backward = attention_calls(length, heads, block)
    start, low, high = document_bounds(segments[0], block)
    flat = (length, share)
    split = (groups, piece, share)

    units = w_gate.shape[0]
    padded = -(-units // 16) * 16
    own_units = [jnp.pad(weight, ((0, padded - units), (0, 0))) for weight in (w_gate, w_up, w_down)]
    (
        attn_in, gain_rows, key, value, query, _, key_rows, value_rows, query_rows, out_rows,
        gate_rows, up_rows, down_rows, dy,
    ) = project_call(dp_count, groups, piece, width, here, padded, 1)(
        tokens, mem, gain_tile(gain_attn, gain_ffn), w_key, w_value, w_query, w_out, *own_units, grad_out
    )
    gate_rows, up_rows, down_rows = [
        rows.reshape(groups * padded, width) for rows in (gate_rows, up_rows, down_rows)
    ]
    key, value, query = [part.reshape(flat) for part in (key, value, query)]
    key_rows, value_rows, query_rows, out_rows = [
        rows.reshape(width, width) for rows in (key_rows, value_rows, query_rows, out_rows)
    ]
    context_heads, lse = attend_forward(low, start, query, key, value)
    (
        context, gain_term, layer_out, grad_mid, grad_branch, grad_context_heads, grad_w_down, grad_w_gate, grad_w_up, *_
    ) = middle_call(dp_count, groups, piece, width, groups * padded)(
        gain_rows, tokens, context_heads.reshape(split), grad_out, out_rows, gate_rows, up_rows, down_rows,
        dy.reshape(dp_count, piece, width),
    )
    grad_context_heads = grad_context_heads.reshape(flat)
    dq, dk, dv = attend_backward(high, start, query, key, value, context_heads, grad_context_heads, lse)

    grad_w_out, grad_w_value, grad_w_key, grad_w_query, grad_memory, grad_hidden, gains = reduce_call(
        dp_count, groups, piece, width, here
    )(
        context, mem, attn_in, gain_rows, gain_term, grad_branch, dv.reshape(split), dk.reshape(split),
        dq.reshape(split), value_rows, key_rows, query_rows, tokens, grad_mid,
    )
    grad_w_down, grad_w_gate, grad_w_up = [grad[:units] for grad in (grad_w_down, grad_w_gate, grad_w_up)]
    grad_gain_attn, grad_gain_ffn = gains[0, :here], gains[1, :here]
    cube = (seqs, piece, width)
    return (
        layer_out.reshape(cube),
        grad_hidden.reshape(cube),
        grad_memory.reshape(cube),
        grad_gain_attn,
        grad_w_query,
        grad_w_key,
        grad_w_value,
        grad_w_out,
        grad_gain_ffn,
        grad_w_gate,
        grad_w_up,
        grad_w_down,
    )


def solution(mesh):
    tokens = P("dp", "seq", None)
    rows = P(ALL, None)
    gain = P(ALL)
    in_specs = (tokens, tokens, P("dp", None), gain, rows, rows, rows, rows, gain, rows, rows, rows, tokens)
    out_specs = (tokens, tokens, tokens, gain, rows, rows, rows, rows, gain, rows, rows, rows)
    return jax.shard_map(shards, mesh=mesh, in_specs=in_specs, out_specs=out_specs, check_vma=False)
```

```python
import functools
import math

import jax
import jax.numpy as jnp
from jax import lax
from jax.experimental import pallas as pl
from jax.experimental.pallas import tpu as pltpu
from jax.sharding import PartitionSpec as P

HEAD_DIM = 128
DOCS = 4
EPSILON = 1e-06
MASKED = -1e30
ALL = ("dp", "seq")
F32 = jnp.float32
BF16 = jnp.bfloat16
EXP2_SCALE = HEAD_DIM ** (-0.5) * math.log2(math.e)
NT = (((1,), (1,)), ((), ()))
TN = (((0,), (0,)), ((), ()))
NN = (((1,), (0,)), ((), ()))
BY_MESH = pl.DeviceIdType.MESH


def mxu(left, right, dims):
    return lax.dot_general(left, right, dims, preferred_element_type=F32)


def rms_scale(values):
    return lax.rsqrt(jnp.mean(values * values, axis=-1, keepdims=True) + EPSILON)


def norm_back(grad_normed, normed, rstd, gain):
    scaled = grad_normed * gain
    return rstd * (scaled - normed * jnp.mean(scaled * normed, axis=-1, keepdims=True))


def forward_kernel(block, low_ref, start_ref, q_ref, k_ref, v_ref, out_ref, lse_ref):
    length, width = q_ref.shape
    heads = range(width // HEAD_DIM)
    columns = [slice(h * HEAD_DIM, (h + 1) * HEAD_DIM) for h in heads]

    def one_query_block(qb, _):
        q0 = pl.multiple_of(qb * block, block)
        rows = pl.ds(q0, block)
        start = start_ref[:, rows]
        query_pos = q0 + lax.broadcasted_iota(jnp.int32, (block, block), 1)

        def one_key_block(kb, carry):
            k0 = pl.multiple_of(kb * block, block)
            keys = pl.ds(k0, block)
            key_pos = k0 + lax.broadcasted_iota(jnp.int32, (block, block), 0)
            seen = (key_pos >= start) & (key_pos <= query_pos)
            scores = [mxu(k_ref[keys, columns[h]], q_ref[rows, columns[h]], NT) for h in heads]
            after = []
            for h in heads:
                top, total, acc = carry[h]
                score = jnp.where(seen, scores[h], MASKED)
                new_top = jnp.maximum(top, jnp.max(score, axis=0, keepdims=True))
                shrink = jnp.exp2((top - new_top) * EXP2_SCALE)
                raised = jnp.exp2((score - new_top) * EXP2_SCALE)
                total = total * shrink + jnp.sum(raised, axis=0, keepdims=True)
                acc = acc * shrink + mxu(v_ref[keys, columns[h]], raised.astype(BF16), TN)
                after.append((new_top, total, acc))
            return tuple(after)

        first = (
            jnp.full((1, block), MASKED, F32),
            jnp.zeros((1, block), F32),
            jnp.zeros((HEAD_DIM, block), F32),
        )
        done = lax.fori_loop(low_ref[qb], qb + 1, one_key_block, tuple(first for _ in heads))
        for h in heads:
            top, total, acc = done[h]
            out_ref[rows, columns[h]] = (acc / total).T.astype(BF16)
            lse_ref[h, :, rows] = top * EXP2_SCALE + jnp.log2(total)
        return 0

    lax.fori_loop(0, length // block, one_query_block, 0)


def backward_kernel(
    block, high_ref, start_ref, q_ref, k_ref, v_ref, ctx_ref, grad_ref, lse_ref,
    dq_ref, dk_ref, dv_ref, dq_acc, delta_acc,
):
    length, width = q_ref.shape
    heads = range(width // HEAD_DIM)
    columns = [slice(h * HEAD_DIM, (h + 1) * HEAD_DIM) for h in heads]
    blocks = length // block
    scale = HEAD_DIM ** (-0.5)
    dq_acc[...] = jnp.zeros_like(dq_acc)

    def one_delta(qb, _):
        rows = pl.ds(pl.multiple_of(qb * block, block), block)
        for h in heads:
            both = ctx_ref[rows, columns[h]].astype(F32) * grad_ref[rows, columns[h]].astype(F32)
            delta_acc[h, :, rows] = jnp.sum(both.T, axis=0, keepdims=True)
        return 0

    lax.fori_loop(0, blocks, one_delta, 0)

    def one_key_block(kb, _):
        k0 = pl.multiple_of(kb * block, block)
        keys = pl.ds(k0, block)
        key_pos = k0 + lax.broadcasted_iota(jnp.int32, (block, block), 0)

        def one_query_block(qb, carry):
            q0 = pl.multiple_of(qb * block, block)
            rows = pl.ds(q0, block)
            start = start_ref[:, rows]
            query_pos = q0 + lax.broadcasted_iota(jnp.int32, (block, block), 1)
            seen = (key_pos >= start) & (key_pos <= query_pos)
            scores = [mxu(k_ref[keys, columns[h]], q_ref[rows, columns[h]], NT) for h in heads]
            grad_probs = [mxu(v_ref[keys, columns[h]], grad_ref[rows, columns[h]], NT) for h in heads]
            after = []
            for h in heads:
                dk, dv = carry[h]
                prob = jnp.exp2(scores[h] * EXP2_SCALE - lse_ref[h, :, rows])
                prob = jnp.where(seen, prob, 0.0)
                grad_score = (prob * (grad_probs[h] - delta_acc[h, :, rows])).astype(BF16)
                dv = dv + mxu(prob.astype(BF16), grad_ref[rows, columns[h]], NN)
                dk = dk + mxu(grad_score, q_ref[rows, columns[h]], NN)
                dq_acc[rows, columns[h]] += mxu(grad_score, k_ref[keys, columns[h]], TN)
                after.append((dk, dv))
            return tuple(after)

        zeros = jnp.zeros((block, HEAD_DIM), F32)
        done = lax.fori_loop(kb, high_ref[kb], one_query_block, tuple((zeros, zeros) for _ in heads))
        for h in heads:
            dk_ref[keys, columns[h]] = (done[h][0] * scale).astype(BF16)
            dv_ref[keys, columns[h]] = done[h][1].astype(BF16)
        return 0

    lax.fori_loop(0, blocks, one_key_block, 0)
    dq_ref[...] = (dq_acc[...] * scale).astype(BF16)


def attention_calls(length, heads, block):
    together = math.gcd(heads, 4)
    wide = together * HEAD_DIM
    column = pl.BlockSpec((length, wide), lambda h, *_: (0, h))
    row = pl.BlockSpec((1, length), lambda h, *_: (0, 0))
    stat = pl.BlockSpec((together, 1, length), lambda h, *_: (h, 0, 0))
    flat = jax.ShapeDtypeStruct((length, heads * HEAD_DIM), BF16)
    pairs = heads * length * length // 4
    params = pltpu.CompilerParams(vmem_limit_bytes=56 * 1024 * 1024)
    forward = pl.pallas_call(
        functools.partial(forward_kernel, block),
        grid_spec=pltpu.PrefetchScalarGridSpec(
            num_scalar_prefetch=1,
            grid=(heads // together,),
            in_specs=[row, column, column, column],
            out_specs=[column, stat],
        ),
        out_shape=(flat, jax.ShapeDtypeStruct((heads, 1, length), F32)),
        compiler_params=params,
        cost_estimate=pl.CostEstimate(
            flops=64 * pairs * HEAD_DIM, transcendentals=pairs, bytes_accessed=8 * length * heads * HEAD_DIM
        ),
        name="attend_forward",
    )
    backward = pl.pallas_call(
        functools.partial(backward_kernel, block),
        grid_spec=pltpu.PrefetchScalarGridSpec(
            num_scalar_prefetch=1,
            grid=(heads // together,),
            in_specs=[row, column, column, column, column, column, stat],
            out_specs=[column, column, column],
            scratch_shapes=[pltpu.VMEM((length, wide), F32), pltpu.VMEM((together, 1, length), F32)],
        ),
        out_shape=(flat, flat, flat),
        compiler_params=params,
        cost_estimate=pl.CostEstimate(
            flops=96 * pairs * HEAD_DIM, transcendentals=pairs, bytes_accessed=16 * length * heads * HEAD_DIM
        ),
        name="attend_backward",
    )
    return forward, backward


def document_bounds(segment_ids, block):
    first = jnp.zeros_like(segment_ids)
    last = jnp.zeros_like(segment_ids)
    for number in range(DOCS):
        below = jnp.sum((segment_ids < number).astype(jnp.int32))
        upto = jnp.sum((segment_ids <= number).astype(jnp.int32))
        first = jnp.where(segment_ids == number, below, first)
        last = jnp.where(segment_ids == number, upto - 1, last)
    low = first[::block] // block
    high = last[block - 1 :: block] // block + 1
    return first[None, :], low, high


def remote(src, dst, send, recv, device):
    return pltpu.make_async_remote_copy(
        src_ref=src, dst_ref=dst, send_sem=send, recv_sem=recv, device_id=device, device_id_type=BY_MESH
    )


class Place:
    def __init__(self, dp_count, groups):
        self.groups = groups
        self.chips = dp_count // 2
        self.dp = lax.axis_index("dp")
        self.seq = lax.axis_index("seq")
        self.core = lax.rem(self.dp, 2)
        self.chip = self.dp // 2
        self.sibling = {"dp": self.dp + 1 - 2 * self.core, "seq": self.seq}

    def chip_at(self, step):
        chip, bit = self.chip, 1
        while bit < self.chips:
            chip = chip + (step // bit % 2) * bit * (1 - 2 * lax.rem(self.chip // bit, 2))
            bit *= 2
        return chip

    def chip_device(self, chip):
        return {"dp": 2 * chip + self.core, "seq": self.seq}

    def line_at(self, step):
        return lax.rem(self.seq + step, self.groups)

    def line_device(self, seq):
        return {"dp": self.dp, "seq": seq}

    def barrier(self):
        everyone = pltpu.get_barrier_semaphore()
        for step in range(1, self.groups):
            pl.semaphore_signal(everyone, inc=1, device_id=self.line_device(self.line_at(step)), device_id_type=BY_MESH)
        for step in range(1, self.chips):
            pl.semaphore_signal(everyone, inc=1, device_id=self.chip_device(self.chip_at(step)), device_id_type=BY_MESH)
        pl.semaphore_signal(everyone, inc=1, device_id=self.sibling, device_id_type=BY_MESH)
        pl.semaphore_wait(everyone, self.groups + self.chips - 1)


def project_kernel(
    dp_count, groups, hidden, memory, gains, w_key, w_value, w_query, w_out, w_gate, w_up, w_down, grad,
    attn_in, gain_rows, key, value, query, all_gains, all_key, all_value, all_query, all_out,
    all_gate, all_up, all_down, all_grad,
    weight, parts, line_send, line_recv, chip_send, chip_recv, core_send, core_recv,
    own_sem, load_sem, part_send, part_recv, part_own,
    dy_own, dy_chip_send, dy_chip_recv, dy_core_send, dy_core_recv,
):
    place = Place(dp_count, groups)
    chips, seq = place.chips, place.seq
    shards = (gains, w_key, w_value, w_query, w_out, w_gate, w_up, w_down)
    wholes = (all_gains, all_key, all_value, all_query, all_out, all_gate, all_up, all_down)
    count = 5
    whole_own = place.dp * groups + seq

    def own_block(m):
        return whole_own if m < count else seq

    above, below = seq < groups - 1, seq > 0
    up, down = place.line_device(lax.rem(seq + 1, groups)), place.line_device(lax.rem(seq + groups - 1, groups))

    def line(m, dp):
        return wholes[m].at[pl.ds(dp * groups, groups)]

    def along(m, src, block, distance, upward):
        slot = 0 if upward else 1
        return remote(
            src, wholes[m].at[block], line_send.at[m, slot, distance - 1], line_recv.at[m, slot, distance - 1],
            up if upward else down,
        )

    def to_chip(m, src, block, step):
        return remote(
            src, wholes[m].at[block], chip_send.at[m, step - 1], chip_recv.at[m, step - 1],
            place.chip_device(place.chip_at(step)),
        )

    def to_sibling(m, src, dst, step):
        return remote(src, dst, core_send.at[m, step], core_recv.at[m, step], place.sibling)

    def spread(m, src, block):
        for step in range(1, chips):
            to_chip(m, src, block, step).start()
        to_sibling(m, src, wholes[m].at[block], 0).start()

    def own_copy(m):
        return pltpu.make_async_copy(shards[m], wholes[m].at[own_block(m)], own_sem.at[m])

    def start_own(m):
        own = own_block(m)
        own_copy(m).start()

        @pl.when(above)
        def _():
            along(m, shards[m], own, 1, True).start()

        @pl.when(below)
        def _():
            along(m, shards[m], own, 1, False).start()

        if m < count:
            spread(m, shards[m], own)

    def serve_line(m):
        for distance in range(1, groups):
            for upward in (True, False):
                block = own_block(m) - distance if upward else own_block(m) + distance
                there = seq >= distance if upward else seq < groups - distance
                onward = above if upward else below

                @pl.when(there)
                def _():
                    landed = wholes[m].at[block]
                    along(m, landed, block, distance, upward).wait_recv()

                    @pl.when(onward)
                    def _():
                        along(m, landed, block, distance + 1, upward).start()

                    if m < count:
                        spread(m, landed, block)

    chunks = all_grad.shape[0]
    chunk_rows = grad.shape[0] // chunks

    def grad_rows(chunk):
        return grad.at[pl.ds(chunk * chunk_rows, chunk_rows), :]

    def grad_own(chunk):
        return pltpu.make_async_copy(grad_rows(chunk), all_grad.at[chunk, place.dp], dy_own.at[chunk])

    def grad_to_chip(chunk, step):
        return remote(
            grad_rows(chunk), all_grad.at[chunk, place.dp], dy_chip_send.at[chunk, step - 1],
            dy_chip_recv.at[chunk, step - 1], place.chip_device(place.chip_at(step)),
        )

    def grad_to_sibling(chunk, step):
        dp = 2 * place.chip_at(step) + place.core
        src = all_grad.at[chunk, dp] if step > 0 else grad_rows(chunk)
        return remote(
            src, all_grad.at[chunk, dp], dy_core_send.at[chunk, step], dy_core_recv.at[chunk, step], place.sibling
        )

    def start_grad(chunk):
        grad_own(chunk).start()
        for step in range(1, chips):
            grad_to_chip(chunk, step).start()
        grad_to_sibling(chunk, 0).start()

    def serve_grad(chunk):
        for step in range(1, chips):
            grad_to_chip(chunk, step).wait_recv()
            grad_to_sibling(chunk, step).start()

    def finish_grad(chunk):
        grad_own(chunk).wait()
        for step in range(1, chips):
            grad_to_chip(chunk, step).wait_send()
        for step in range(chips):
            grad_to_sibling(chunk, step).wait()

    def serve_chips(m):
        for step in range(1, chips):
            dp = 2 * place.chip_at(step) + place.core
            remote(
                line(m, dp), line(m, dp), chip_send.at[m, step - 1], chip_recv.at[m, step - 1], place.sibling
            ).wait_recv()
            to_sibling(m, line(m, dp), line(m, dp), step).start()

    def finish(m):
        for step in range(chips):
            dp = 2 * place.chip_at(step) + 1 - place.core
            to_sibling(m, line(m, dp), line(m, dp), step).wait_recv()
        own_copy(m).wait()

    targets = (None, key, value, query, None)
    lefts = (None, memory, memory, attn_in, None)
    share = weight.shape[2] // groups

    def part_copy(m, step):
        other = place.line_at(step)
        return remote(
            parts.at[m - 1, other], targets[m].at[seq], part_send.at[m - 1, step - 1], part_recv.at[m - 1, step - 1],
            place.line_device(other),
        )

    def own_part(m):
        return pltpu.make_async_copy(parts.at[m - 1, seq], targets[m].at[seq], part_own.at[m - 1])

    def load(m):
        return pltpu.make_async_copy(wholes[m], weight, load_sem)

    def project(m):
        load(m).start()
        load(m).wait()
        rows = weight.shape[0] * weight.shape[1]
        left = lefts[m][...]

        def one(step, _):
            group = place.line_at(step)
            columns = pl.ds(pl.multiple_of(group * share, share), share)
            right = weight[:, :, columns].reshape(rows, share)
            parts[m - 1, group] = jnp.dot(left, right, preferred_element_type=F32).astype(BF16)

            @pl.when(step > 0)
            def _():
                remote(
                    parts.at[m - 1, group], targets[m].at[seq], part_send.at[m - 1, step - 1],
                    part_recv.at[m - 1, step - 1], place.line_device(group),
                ).start()

            return 0

        lax.fori_loop(1, groups, one, 0)
        one(0, 0)
        own_part(m).start()

    def normalize():
        here = 128 // (weight.shape[1])
        tiles = weight.shape[2] // 128
        for tile in range(tiles):
            total = all_gains_v[tile * here]
            for i in range(1, here):
                total = total + pltpu.roll(all_gains_v[tile * here + i], i * weight.shape[1], 1)
            gain_rows[:, tile * 128 : (tile + 1) * 128] = total
        step_rows = 128 if hidden.shape[0] % 128 == 0 else hidden.shape[0]

        def some(i, _):
            rows = pl.ds(pl.multiple_of(i * step_rows, step_rows), step_rows)
            x = hidden[rows, :].astype(F32)
            normed = x * lax.rsqrt(jnp.mean(x * x, axis=-1, keepdims=True) + EPSILON)
            attn_in[rows, :] = (normed * gain_rows[0:1, :]).astype(BF16)
            return 0

        lax.fori_loop(0, hidden.shape[0] // step_rows, some, 0)

    all_gains_v = all_gains
    place.barrier()
    start_own(0)
    start_own(1)
    serve_line(0)
    start_own(2)
    serve_line(1)
    start_own(3)
    serve_chips(0)
    serve_line(2)
    start_own(4)
    serve_chips(1)
    finish(0)
    normalize()
    serve_line(3)
    start_own(5)
    finish(1)
    project(1)
    serve_line(4)
    start_own(6)
    for chunk in range(chunks):
        start_grad(chunk)
    serve_chips(2)
    finish(2)
    project(2)
    serve_line(5)
    start_own(7)
    serve_chips(3)
    finish(3)
    project(3)
    serve_line(6)
    serve_chips(4)
    serve_line(7)
    for chunk in range(chunks):
        serve_grad(chunk)
    finish(4)
    for chunk in range(chunks):
        finish_grad(chunk)
    for m in range(count, len(shards)):
        own_copy(m).wait()
    for m in range(len(shards)):
        for distance in range(1, groups):
            for upward in (True, False):
                came = seq >= distance - 1 if upward else seq < groups - distance + 1
                onward = above if upward else below

                @pl.when(came & onward)
                def _():
                    along(m, wholes[m].at[own_block(m)], own_block(m), distance, upward).wait_send()

        if m >= count:
            continue
        mine = line(m, place.dp)
        for step in range(1, chips):
            remote(
                mine, mine, chip_send.at[m, step - 1], chip_recv.at[m, step - 1], place.sibling
            ).wait_send()
        for step in range(chips):
            to_sibling(m, mine, mine, step).wait_send()
    for m in (1, 2, 3):
        own_part(m).wait()
        for step in range(1, groups):
            part_copy(m, step).wait()


def project_call(dp_count, groups, piece, width, here, padded, chunks):
    chips = dp_count // 2
    blocks = dp_count * groups
    share = width // groups
    hbm = pl.BlockSpec(memory_space=pl.ANY)
    vmem = pl.BlockSpec(memory_space=pltpu.VMEM)
    heads = jax.ShapeDtypeStruct((groups, piece, share), BF16)
    whole = jax.ShapeDtypeStruct((blocks, here, width), BF16)
    units = jax.ShapeDtypeStruct((groups, padded, width), BF16)
    dma = pltpu.SemaphoreType.DMA
    others = max(chips - 1, 1)
    return pl.pallas_call(
        functools.partial(project_kernel, dp_count, groups),
        in_specs=[vmem, vmem] + [hbm] * 9,
        out_specs=[vmem, vmem, hbm, hbm, hbm, vmem] + [hbm] * 8,
        out_shape=(
            jax.ShapeDtypeStruct((piece, width), BF16),
            jax.ShapeDtypeStruct((8, width), F32),
            heads, heads, heads,
            jax.ShapeDtypeStruct((blocks, 8, 128), F32),
            whole, whole, whole, whole, units, units, units,
            jax.ShapeDtypeStruct((chunks, dp_count, piece // chunks, width), BF16),
        ),
        scratch_shapes=[
            pltpu.VMEM((blocks, here, width), BF16),
            pltpu.VMEM((3, groups, piece, share), BF16),
            dma((8, 2, groups)), dma((8, 2, groups)),
            dma((5, others)), dma((5, others)),
            dma((5, chips)), dma((5, chips)),
            dma((8,)), dma, dma((3, groups - 1)), dma((3, groups - 1)), dma((3,)),
            dma((chunks,)), dma((chunks, others)), dma((chunks, others)), dma((chunks, chips)), dma((chunks, chips)),
        ],
        compiler_params=pltpu.CompilerParams(
            collective_id=1, has_side_effects=True, vmem_limit_bytes=48 * 1024 * 1024
        ),
        cost_estimate=pl.CostEstimate(
            flops=128 * piece * width * width, transcendentals=0, bytes_accessed=16 * width * width
        ),
        name="gather_project",
    )


def gain_tile(gain_attn, gain_ffn):
    here = gain_attn.shape[0]
    both = jnp.stack((gain_attn, gain_ffn)).astype(F32)
    return jnp.pad(both, ((0, 6), (0, 128 - here)))


def reduce_kernel(
    dp_count, groups, here, context, memory, attn_in, gain_rows, gain_ffn_term, grad_branch, dv, dk, dq,
    all_value, all_key, all_query, hidden, grad_mid,
    grad_out, grad_value, grad_key, grad_query, grad_memory, grad_hidden, grad_gains,
    right, core_buf, core_in, chip_buf, chip_in, kept, line_buf, line_in, line_own,
    part_send, part_recv, part_own, load_sem, core_send, core_recv, chip_send, chip_recv,
    line_send, line_recv, store_sem, core_free, chip_free,
    weight, panel_out, grad_attn_in, mid_buf, hidden_buf, gain_term, gain_buf, gain_in,
    weight_sem, panel_sem, mid_sem, hidden_sem, gain_send, gain_recv,
):
    place = Place(dp_count, groups)
    chips, seq = place.chips, place.seq
    panel = groups * here
    share = right.shape[3]
    lefts = (context, memory, memory, attn_in)
    parts = (None, dv, dk, dq)
    grads = (grad_out, grad_value, grad_key, grad_query)
    half = share // 2
    count = 8

    def half_columns(job, group=0):
        return pl.ds(group * share + job % 2 * half, half)

    def part_copy(job, step):
        other = place.line_at(step)
        return remote(
            parts[job // 2].at[other, :, half_columns(job)], right.at[job // 2, seq, :, half_columns(job)],
            part_send.at[job, step - 1], part_recv.at[job, step - 1], place.line_device(other),
        )

    def own_part(job):
        return pltpu.make_async_copy(
            parts[job // 2].at[seq, :, half_columns(job)], right.at[job // 2, seq, :, half_columns(job)],
            part_own.at[job],
        )

    def send_parts(job):
        own_part(job).start()
        for step in range(1, groups):
            part_copy(job, step).start()

    def sent_parts(job):
        for step in range(1, groups):
            part_copy(job, step).wait_send()

    def arrived_parts(job):
        own_part(job).wait()
        for step in range(1, groups):
            part_copy(job, step).wait_recv()

    def branch_copy(group):
        return pltpu.make_async_copy(
            grad_branch.at[:, pl.ds(group * share, share)], right.at[0, group], load_sem.at[group]
        )

    def product(job, dp, store):
        rows = pl.ds(pl.multiple_of(dp * panel, panel), panel)
        left = lefts[job // 2][:, rows].T
        for group in range(groups):
            store(
                slice(group * half, (group + 1) * half),
                jnp.dot(left, right[job // 2, group, :, half_columns(job)], preferred_element_type=F32),
            )

    def core_copy(m, step):
        return remote(
            core_buf.at[step], core_in.at[m % 2, step], core_send.at[step], core_recv.at[m % 2, step], place.sibling
        )

    def chip_copy(m, step):
        return remote(
            chip_buf.at[m % 2, step - 1], chip_in.at[m % 2, step - 1], chip_send.at[m % 2, step - 1],
            chip_recv.at[m % 2, step - 1], place.chip_device(place.chip_at(step)),
        )

    def line_copy(m, step):
        return remote(
            line_buf.at[m, step - 1], line_in.at[m, step - 1], line_send.at[m, step - 1], line_recv.at[m, step - 1],
            place.line_device(place.line_at(step)),
        )

    paired = groups == 4
    inner = (seq == 1) | (seq == 2)
    mate = seq + 1 - 2 * (seq % 2)

    def across(j):
        return 2 * (1 - seq // 2) + j

    def near_copy(m):
        return remote(
            line_buf.at[m, 0], line_in.at[m, 0], line_send.at[m, 0], line_recv.at[m, 0], place.line_device(mate)
        )

    def relay_copy(m, j):
        return remote(
            line_buf.at[m, 1 + j], line_in.at[m, 2 + j], line_send.at[m, 1 + j], line_recv.at[m, 2 + j],
            place.line_device(mate),
        )

    def across_copy(m, j):
        return remote(
            line_buf.at[m, 1 + j], line_in.at[m, 1], line_send.at[m, 1 + j], line_recv.at[m, 1],
            place.line_device(across(j)),
        )

    order = tuple(range(1, chips)) + (0,)

    def to_sibling(m):
        if m >= 2:
            pl.semaphore_wait(core_free, 1)
        for step in order:
            if m >= 1:
                core_copy(m - 1, step).wait_send()
            dp = 2 * place.chip_at(step) + 1 - place.core

            def store(columns, value, step=step):
                core_buf[step, :, columns] = value.astype(BF16)

            product(m, dp, store)
            core_copy(m, step).start()

    def to_chips(m):
        for step in order:
            dp = 2 * place.chip_at(step) + place.core
            core_copy(m, step).wait_recv()
            if step > 0:
                if m >= 2:
                    chip_copy(m - 2, step).wait_send()
                    pl.semaphore_wait(chip_free.at[step - 1], 1)

                def store(columns, value, step=step):
                    total = value + core_in[m % 2, step, :, columns].astype(F32)
                    chip_buf[m % 2, step - 1, :, columns] = total.astype(BF16)

            else:

                def store(columns, value):
                    kept[m % 2, :, columns] = value + core_in[m % 2, 0, :, columns].astype(F32)

            product(m, dp, store)
            if step > 0:
                chip_copy(m, step).start()
        if m + 2 < count:
            pl.semaphore_signal(core_free, inc=1, device_id=place.sibling, device_id_type=BY_MESH)

    def sum_chips(m):
        for step in range(1, chips):
            chip_copy(m, step).wait_recv()

        def block_sum(block):
            rows = pl.ds(pl.multiple_of(block * here, here), here)
            total = kept[m % 2, rows, :]
            for other in range(1, chips):
                total = total + chip_in[m % 2, other - 1, rows, :].astype(F32)
            return total

        if paired:
            line_buf[m, 0] = block_sum(mate).astype(BF16)
            for j in range(2):
                line_buf[m, 1 + j] = block_sum(across(j)).astype(BF16)
        else:
            for step in range(1, groups):
                line_buf[m, step - 1] = block_sum(place.line_at(step)).astype(BF16)
        line_own[m] = block_sum(seq)
        if m + 2 < count:
            for step in range(1, chips):
                pl.semaphore_signal(
                    chip_free.at[step - 1], inc=1, device_id=place.chip_device(place.chip_at(step)),
                    device_id_type=BY_MESH,
                )

    def send_line(m):
        if paired:
            near_copy(m).start()

            @pl.when(jnp.logical_not(inner))
            def _():
                for j in range(2):
                    relay_copy(m, j).start()

        else:
            for step in range(1, groups):
                line_copy(m, step).start()

    def relay(m):
        if not paired:
            return

        @pl.when(inner)
        def _():
            for j in range(2):
                relay_copy(m, j).wait_recv()
                line_buf[m, 1 + j] = (line_buf[m, 1 + j].astype(F32) + line_in[m, 2 + j].astype(F32)).astype(BF16)
                across_copy(m, j).start()

    def store_grad(m, group):
        return pltpu.make_async_copy(
            line_own.at[m, :, pl.ds(group * half, half)], grads[m // 2].at[:, half_columns(m, group)],
            store_sem.at[m, group],
        )

    def settle(m):
        total = line_own[m]
        if paired:
            near_copy(m).wait_recv()
            across_copy(m, 0).wait_recv()
            total = total + line_in[m, 0].astype(F32) + line_in[m, 1].astype(F32)
        else:
            for step in range(1, groups):
                line_copy(m, step).wait_recv()
                total = total + line_in[m, step - 1].astype(F32)
        line_own[m] = total
        for group in range(groups):
            store_grad(m, group).start()

    width = memory.shape[1]
    panels = width // panel
    piece = memory.shape[0]

    def weight_copy(slot, which, source, index):
        rows = pl.ds(pl.multiple_of(index * panel, panel), panel)
        return pltpu.make_async_copy(source.at[rows, :], weight.at[slot, which], weight_sem.at[slot, which])

    def panel_copy(slot, index):
        columns = pl.ds(pl.multiple_of(index * panel, panel), panel)
        return pltpu.make_async_copy(panel_out.at[slot], grad_memory.at[:, columns], panel_sem.at[slot])

    def back(slot, which, m):
        total = jnp.zeros((piece, panel), F32)
        for group in range(groups):
            columns = slice(group * share, (group + 1) * share)
            total = total + lax.dot_general(
                right[m, group], weight[slot, which, :, columns], NT, preferred_element_type=F32
            )
        return total

    def memory_gradient():
        weight_copy(0, 0, all_value, 0).start()
        weight_copy(0, 1, all_key, 0).start()

        def one(index, _):
            slot = lax.rem(index, 2)

            @pl.when(index + 1 < panels)
            def _():
                weight_copy(1 - slot, 0, all_value, index + 1).start()
                weight_copy(1 - slot, 1, all_key, index + 1).start()

            weight_copy(slot, 0, all_value, index).wait()
            weight_copy(slot, 1, all_key, index).wait()

            @pl.when(index >= 2)
            def _():
                panel_copy(slot, index - 2).wait()

            panel_out[slot] = back(slot, 0, 1) + back(slot, 1, 2)
            panel_copy(slot, index).start()
            return 0

        lax.fori_loop(0, panels, one, 0)
        for index in range(max(panels - 2, 0), panels):
            panel_copy(index % 2, index).wait()

    def query_gradient():
        weight_copy(0, 0, all_query, 0).start()

        def one(index, _):
            slot = lax.rem(index, 2)

            @pl.when(index + 1 < panels)
            def _():
                weight_copy(1 - slot, 0, all_query, index + 1).start()

            weight_copy(slot, 0, all_query, index).wait()
            columns = pl.ds(pl.multiple_of(index * panel, panel), panel)
            grad_attn_in[:, columns] = back(slot, 0, 3)
            return 0

        lax.fori_loop(0, panels, one, 0)

    some = mid_buf.shape[1]
    batches = piece // some

    def batch_rows(index):
        return pl.ds(pl.multiple_of(index * some, some), some)

    def mid_copy(slot, index):
        return pltpu.make_async_copy(grad_mid.at[batch_rows(index), :], mid_buf.at[slot], mid_sem.at[slot])

    def hidden_copy(slot, index):
        return pltpu.make_async_copy(hidden.at[batch_rows(index), :], hidden_buf.at[slot], hidden_sem.at[slot])

    def hidden_store(index):
        rows = batch_rows(index)
        return pltpu.make_async_copy(grad_attn_in.at[rows, :], grad_hidden.at[rows, :], panel_sem.at[0])

    def hidden_gradient():
        gain_term[...] = jnp.zeros_like(gain_term)
        mid_copy(0, 0).start()
        hidden_copy(0, 0).start()

        def one(index, _):
            slot = lax.rem(index, 2)

            @pl.when(index + 1 < batches)
            def _():
                mid_copy(1 - slot, index + 1).start()
                hidden_copy(1 - slot, index + 1).start()

            mid_copy(slot, index).wait()
            hidden_copy(slot, index).wait()
            rows = batch_rows(index)
            x = hidden_buf[slot].astype(F32)
            rstd = lax.rsqrt(jnp.mean(x * x, axis=-1, keepdims=True) + EPSILON)
            normed = x * rstd
            grad = grad_attn_in[rows, :]
            gain_term[0:1, :] += jnp.sum(normed * grad, axis=0, keepdims=True)
            scaled = grad * gain_rows[0:1, :]
            shift = jnp.mean(scaled * normed, axis=-1, keepdims=True)
            grad_attn_in[rows, :] = mid_buf[slot] + rstd * (scaled - normed * shift)
            hidden_store(index).start()
            return 0

        lax.fori_loop(0, batches, one, 0)

    devices = dp_count * groups
    me = place.dp * groups + seq

    def gain_copy(step):
        owner = lax.rem(me + step, devices)
        return remote(
            gain_buf.at[owner], gain_in.at[step], gain_send, gain_recv, {"dp": owner // groups, "seq": owner % groups}
        )

    def send_gains():
        gain_term[1:2, :] = gain_ffn_term[0:1, :]
        per = 128 // here
        for owner in range(devices):
            tile = gain_term[:, owner // per * 128 : (owner // per + 1) * 128]
            shift = owner % per * here
            gain_buf[owner] = pltpu.roll(tile, 128 - shift, 1) if shift else tile

        def one(step, _):
            gain_copy(step).start()
            return 0

        lax.fori_loop(1, devices, one, 0)

    def sum_gains():
        remote(
            gain_buf.at[pl.ds(0, devices - 1)], gain_in.at[pl.ds(1, devices - 1)], gain_send, gain_recv, place.sibling
        ).wait()
        total = gain_buf[me]
        for step in range(1, devices):
            total = total + gain_in[step]
        grad_gains[...] = total

    everyone = pltpu.get_barrier_semaphore()

    def greet(step, _):
        other = lax.rem(me + step, devices)
        pl.semaphore_signal(
            everyone, inc=1, device_id={"dp": other // groups, "seq": other % groups}, device_id_type=BY_MESH
        )
        return 0

    lax.fori_loop(1, devices, greet, 0)
    pl.semaphore_wait(everyone, devices - 1)
    send_parts(2)
    send_parts(3)
    for group in range(groups):
        branch_copy(group).start()
    for group in range(groups):
        branch_copy(group).wait()
    for job in range(2):
        to_sibling(job)
        to_chips(job)
    for job in range(2, count):
        sent_parts(job)
        if job + 2 < count:
            send_parts(job + 2)
        arrived_parts(job)
        to_sibling(job)
        sum_chips(job - 2)
        send_line(job - 2)
        to_chips(job)
        if job >= 4:
            relay(job - 4)
        if job == 5:
            memory_gradient()
    sum_chips(6)
    send_line(6)
    query_gradient()
    relay(4)
    hidden_gradient()
    relay(5)
    send_gains()
    sum_chips(7)
    send_line(7)
    for job in range(6):
        settle(job)
    relay(6)
    settle(6)
    relay(7)
    settle(7)
    sum_gains()
    pltpu.make_async_copy(grad_attn_in, grad_hidden, panel_sem.at[0]).wait()
    for step in range(chips):
        core_copy(count - 1, step).wait_send()
    for job in range(count):
        if job >= count - 2:
            for step in range(1, chips):
                chip_copy(job, step).wait_send()
        if paired:
            near_copy(job).wait_send()
            for j in range(2):
                across_copy(job, j).wait_send()
        else:
            for step in range(1, groups):
                line_copy(job, step).wait_send()
        for group in range(groups):
            store_grad(job, group).wait()


def reduce_call(dp_count, groups, piece, width, here):
    chips = dp_count // 2
    share = width // groups
    panel = groups * here
    hbm = pl.BlockSpec(memory_space=pl.ANY)
    vmem = pl.BlockSpec(memory_space=pltpu.VMEM)
    grad = jax.ShapeDtypeStruct((here, width), F32)
    tokens = jax.ShapeDtypeStruct((piece, width), F32)
    some = min(64, piece)
    devices = dp_count * groups
    dma = pltpu.SemaphoreType.DMA
    others = max(chips - 1, 1)
    return pl.pallas_call(
        functools.partial(reduce_kernel, dp_count, groups, here),
        in_specs=[vmem] * 5 + [hbm] * 9,
        out_specs=[hbm] * 6 + [vmem],
        out_shape=(grad, grad, grad, grad, tokens, tokens, jax.ShapeDtypeStruct((8, 128), F32)),
        scratch_shapes=[
            pltpu.VMEM((4, groups, piece, share), BF16),
            pltpu.VMEM((chips, panel, width // 2), BF16),
            pltpu.VMEM((2, chips, panel, width // 2), BF16),
            pltpu.VMEM((2, others, panel, width // 2), BF16),
            pltpu.VMEM((2, others, panel, width // 2), BF16),
            pltpu.VMEM((2, panel, width // 2), F32),
            pltpu.VMEM((8, max(groups - 1, 3), here, width // 2), BF16),
            pltpu.VMEM((8, max(groups - 1, 4), here, width // 2), BF16),
            pltpu.VMEM((8, here, width // 2), F32),
            dma((8, groups - 1)), dma((8, groups - 1)), dma((8,)), dma((groups,)),
            dma((chips,)), dma((2, chips)),
            dma((2, others)), dma((2, others)),
            dma((8, max(groups - 1, 3))), dma((8, max(groups - 1, 4))), dma((8, groups)),
            pltpu.SemaphoreType.REGULAR, pltpu.SemaphoreType.REGULAR((others,)),
            pltpu.VMEM((2, 2, panel, width), BF16),
            pltpu.VMEM((2, piece, panel), F32),
            pltpu.VMEM((piece, width), F32),
            pltpu.VMEM((2, some, width), F32),
            pltpu.VMEM((2, some, width), BF16),
            pltpu.VMEM((8, width), F32),
            pltpu.VMEM((devices, 8, 128), F32),
            pltpu.VMEM((devices, 8, 128), F32),
            dma((2, 2)), dma((2,)), dma((2,)), dma((2,)), dma, dma,
        ],
        compiler_params=pltpu.CompilerParams(
            collective_id=2, has_side_effects=True, vmem_limit_bytes=63 * 1024 * 1024
        ),
        cost_estimate=pl.CostEstimate(
            flops=128 * piece * width * width, transcendentals=0, bytes_accessed=16 * width * width
        ),
        name="weight_gradients",
    )


def middle_kernel(
    dp_count, groups,
    gain_rows, hidden, context_heads, grad_own, out_rows, gate_rows, up_rows, down_rows, all_grad,
    context, gain_term, layer_out, grad_mid, grad_branch, grad_heads, grad_down, grad_gate, grad_up,
    all_ffn, grad_acts, acts, grad_gates, grad_ups, core_in, chip_in, branch_core, branch_out, branch_in, term_in,
    gate_w, up_w, down_w, out_w, mid, ffn_in, own_total, chip_out, term_buf,
    col_send, col_recv, col_own, weight_sem, out_sem, chip_send, chip_recv, core_send, core_recv, own_sem,
    x_sem, dy_sem, act_sem, sum_send, sum_recv, load_sem, far_send, far_recv, left_sem, right_sem, branch_sem,
    part_send, part_recv, plane_send, plane_recv,
    term_send, term_recv, rows_sem, gm_sem, gb_sem, head_send, head_recv, head_own,
):
    place = Place(dp_count, groups)
    chips, seq, core = place.chips, place.seq, place.core
    piece, width = hidden.shape
    share = width // groups
    unit_rows = gate_rows.shape[0]
    padded = gate_w.shape[0]
    wide = (gate_rows, up_rows, down_rows)
    kept = (gate_w, up_w, down_w)

    def weight_copy(i):
        return pltpu.make_async_copy(wide[i], kept[i].at[pl.ds(0, unit_rows), :], weight_sem.at[i])

    def group_columns(group):
        return pl.ds(pl.multiple_of(group * share, share), share)

    def out_copy(group, slot):
        rows = pl.ds(pl.multiple_of(group * share, share), share)
        return pltpu.make_async_copy(out_rows.at[rows, :], out_w.at[slot], out_sem.at[slot])

    def collect(step):
        other = place.line_at(step)
        return remote(
            context_heads.at[other], context.at[:, group_columns(seq)], col_send.at[step - 1], col_recv.at[step - 1],
            place.line_device(other),
        )

    def came_from(step):
        return lax.rem(seq + groups - step, groups)

    place.barrier()
    for step in range(1, groups):
        collect(step).start()
    own_columns = pltpu.make_async_copy(context_heads.at[seq], context.at[:, group_columns(seq)], col_own)
    own_columns.start()
    out_copy(seq, 0).start()
    hidden_copy = pltpu.make_async_copy(hidden, ffn_in, own_sem)
    hidden_copy.start()
    for i in range(3):
        weight_copy(i).start()
        if padded > unit_rows:
            kept[i][unit_rows:, :] = jnp.zeros((padded - unit_rows, width), BF16)

    def act_gradients(dy_buf, out_buf):
        def dy_copy(dp, slot):
            return pltpu.make_async_copy(all_grad.at[dp], dy_buf.at[slot], dy_sem.at[slot])

        def store(dp, slot):
            return pltpu.make_async_copy(out_buf.at[slot], grad_acts.at[dp], act_sem.at[slot, 0])

        dy_copy(0, 0).start()
        weight_copy(2).wait()

        def one(dp, _):
            slot = dp % 2

            @pl.when(dp + 1 < dp_count)
            def _():
                dy_copy(dp + 1, 1 - slot).start()

            dy_copy(dp, slot).wait()

            @pl.when(dp >= 2)
            def _():
                store(dp - 2, slot).wait()

            out_buf[slot] = mxu(dy_buf[slot], down_w[...], NT)
            store(dp, slot).start()
            return 0

        lax.fori_loop(0, dp_count, one, 0)
        for dp in range(dp_count - 2, dp_count):
            store(dp, dp % 2).wait()

    pl.run_scoped(act_gradients, pltpu.VMEM((2, piece, width), BF16), pltpu.VMEM((2, piece, padded), F32))

    for step in range(groups):
        slot = step % 2
        group = came_from(step)
        if step + 1 < groups:
            out_copy(came_from(step + 1), 1 - slot).start()
        if step == 0:
            own_columns.wait()
        else:
            columns = context.at[:, group_columns(group)]
            remote(columns, columns, col_send.at[step - 1], col_recv.at[step - 1], place.sibling).wait_recv()
        out_copy(group, slot).wait()
        left = context[:, group_columns(group)]
        if step == 0:
            hidden_copy.wait()

        def project(part, _, left=left, slot=slot, step=step):
            columns = pl.ds(pl.multiple_of(part * share, share), share)
            value = mxu(left, out_w[slot, :, columns], NN)
            if step == 0:
                mid[:, columns] = ffn_in[:, columns].astype(F32) + value
            else:
                mid[:, columns] += value
            return 0

        lax.fori_loop(0, groups, project, 0)

    some = min(64, piece)
    batches = piece // some

    def batch(index):
        return pl.ds(pl.multiple_of(index * some, some), some)

    def normalize(index, _):
        rows = batch(index)
        x = mid[rows, :]
        rstd = lax.rsqrt(jnp.mean(x * x, axis=-1, keepdims=True) + EPSILON)
        ffn_in[rows, :] = (x * rstd * gain_rows[1:2, :]).astype(BF16)
        return 0

    lax.fori_loop(0, batches, normalize, 0)

    def to_chip(step):
        return remote(
            ffn_in, all_ffn.at[place.dp], chip_send.at[step - 1], chip_recv.at[step - 1],
            place.chip_device(place.chip_at(step)),
        )

    def to_sibling(step):
        dp = 2 * place.chip_at(step) + core
        return remote(all_ffn.at[dp], all_ffn.at[dp], core_send.at[step], core_recv.at[step], place.sibling)

    own_ffn = pltpu.make_async_copy(ffn_in, all_ffn.at[place.dp], own_sem)
    own_ffn.start()
    square = chips == 4
    for step in range(1, 3 if square else chips):
        to_chip(step).start()
    own_ffn.wait()
    to_sibling(0).start()
    for i in range(2):
        weight_copy(i).wait()

    def hand_on(step):
        half = piece // 2
        dp = 2 * place.chip_at(step) + core
        rows = all_ffn.at[dp, pl.ds((step - 1) * half, half), :]
        return remote(rows, rows, chip_send.at[2], chip_recv.at[2], place.chip_device(place.chip_at(3 - step)))

    pieces = 2 * chips
    stored = (acts, grad_gates, grad_ups)

    def piece_of(u, own_first):
        step, which = u // 2, u % 2
        mine = 1 - which if own_first else which
        return step, which, 2 * place.chip_at(step) + mine * core + (1 - mine) * (1 - core)

    def hidden_units(x_buf, da_buf, act_buf):
        def x_copy(u):
            dp = piece_of(u, True)[2]
            return pltpu.make_async_copy(all_ffn.at[dp], x_buf.at[u % 2], x_sem.at[u % 2])

        def da_copy(u):
            dp = piece_of(u, True)[2]
            return pltpu.make_async_copy(grad_acts.at[dp], da_buf.at[u % 2], dy_sem.at[u % 2])

        def act_copy(u, i):
            dp = piece_of(u, True)[2]
            return pltpu.make_async_copy(act_buf.at[u % 2, i], stored[i].at[dp], act_sem.at[u % 2, i])

        def fetch(u):
            step, which, _ = piece_of(u, True)
            if square:

                @pl.when(u == 2)
                def _():
                    for near in (1, 2):
                        to_chip(near).wait_recv()
                        to_sibling(near).start()
                        hand_on(near).start()

                @pl.when(u == 6)
                def _():
                    to_chip(3).wait_recv()
                    to_sibling(3).start()

            else:

                @pl.when((which == 0) & (step > 0))
                def _():
                    to_chip(step).wait_recv()
                    to_sibling(step).start()

            @pl.when(which == 1)
            def _():
                to_sibling(step).wait_recv()

            x_copy(u).start()

        da_copy(0).start()

        def one(u, _):
            slot = u % 2
            ahead = u % 2 == 1
            if square:
                ahead = ahead | (u == 4)
            next_ahead = (u + 1 < pieces) & (u % 2 == 0)
            if square:
                next_ahead = next_ahead | (u == 3)

            @pl.when(jnp.logical_not(ahead))
            def _():
                fetch(u)

            @pl.when(next_ahead)
            def _():
                fetch(u + 1)

            @pl.when(u + 1 < pieces)
            def _():
                da_copy(u + 1).start()

            @pl.when(u >= 2)
            def _():
                for i in range(3):
                    act_copy(u - 2, i).wait()

            x_copy(u).wait()
            gate = mxu(x_buf[slot], gate_w[...], NT)
            up = mxu(x_buf[slot], up_w[...], NT)
            sig = 1.0 / (1.0 + jnp.exp(-gate))
            da_copy(u).wait()
            grad_act = da_buf[slot]
            act_buf[slot, 0] = (gate * sig * up).astype(BF16)
            act_buf[slot, 1] = (grad_act * up * sig * (1.0 + gate * (1.0 - sig))).astype(BF16)
            act_buf[slot, 2] = (grad_act * gate * sig).astype(BF16)
            for i in range(3):
                act_copy(u, i).start()
            return 0

        lax.fori_loop(0, pieces, one, 0)
        for u in range(max(pieces - 2, 0), pieces):
            for i in range(3):
                act_copy(u, i).wait()

    pl.run_scoped(
        hidden_units,
        pltpu.VMEM((2, piece, width), BF16), pltpu.VMEM((2, piece, padded), F32),
        pltpu.VMEM((2, 3, piece, padded), BF16),
    )

    def far_copy(step):
        return remote(
            chip_out.at[step - 1], chip_in.at[step - 1], far_send.at[step - 1],
            far_recv.at[step - 1], place.chip_device(place.chip_at(step)),
        )

    def input_sum(act_buf, core_out, load_buf):
        sources, rights, own = (grad_gates, grad_ups), (gate_w, up_w), own_total
        used = len(sources)

        def place_of(u):
            _, which, dp = piece_of(pieces - 2 + u - 4 * (u // 2), False)
            return chips - 1 - u // 2, which, dp

        def act_copy(u, i):
            dp = place_of(u)[2]
            return pltpu.make_async_copy(sources[i].at[dp], act_buf.at[u % 2, i], act_sem.at[u % 2, i])

        def sum_copy(step):
            return remote(
                core_out, core_in.at[step], sum_send, sum_recv.at[step], place.sibling
            )

        def load_copy(step):
            return pltpu.make_async_copy(core_in.at[step], load_buf, load_sem)

        for i in range(used):
            act_copy(0, i).start()

        def one(u, _):
            step, which, dp = place_of(u)
            slot = u % 2

            @pl.when(u + 1 < pieces)
            def _():
                for i in range(used):
                    act_copy(u + 1, i).start()

            for i in range(used):
                act_copy(u, i).wait()

            @pl.when((which == 0) & (u >= 2))
            def _():
                sum_copy(step + 1).wait_send()

            @pl.when(which == 1)
            def _():
                sum_copy(step).wait_recv()
                load_copy(step).start()
                load_copy(step).wait()

            def columns_of(part, _):
                columns = group_columns(part)
                value = mxu(act_buf[slot, 0], rights[0][:, columns], NN)
                for i in range(1, used):
                    value = value + mxu(act_buf[slot, i], rights[i][:, columns], NN)

                @pl.when(which == 0)
                def _():
                    core_out[:, columns] = value.astype(BF16)

                @pl.when((which == 1) & (step > 0))
                def _():
                    chip_out[step - 1, :, columns] = (value + load_buf[:, columns].astype(F32)).astype(BF16)

                @pl.when((which == 1) & (step == 0))
                def _():
                    own[:, columns] = value + load_buf[:, columns].astype(F32)

                return 0

            lax.fori_loop(0, groups, columns_of, 0)

            @pl.when(which == 0)
            def _():
                sum_copy(step).start()

            @pl.when((which == 1) & (step > 0))
            def _():
                far_copy(step).start()

            return 0

        lax.fori_loop(0, pieces, one, 0)
        sum_copy(0).wait_send()

    block = unit_rows // groups

    paired = groups == 4
    side = seq // 2
    inner = (seq == 1) | (seq == 2)
    partner = seq + 1 - 2 * (seq % 2)

    def across(j):
        return 2 * (1 - side) + j

    def term_rows(i, owner):
        return term_buf.at[i, pl.ds(pl.multiple_of(owner * block, block), block), :]

    def term_copy(i, step):
        other = place.line_at(step)
        return remote(
            term_rows(i, other), term_in.at[i, step - 1], term_send.at[i, step - 1], term_recv.at[i, step - 1],
            place.line_device(other),
        )

    def near_copy(i):
        return remote(
            term_rows(i, partner), term_in.at[i, 0], term_send.at[i, 0], term_recv.at[i, 0], place.line_device(partner)
        )

    def relay_copy(i, j):
        return remote(
            term_rows(i, across(j)), term_in.at[i, 2 + j], term_send.at[i, 1 + j], term_recv.at[i, 2 + j],
            place.line_device(partner),
        )

    def across_copy(i, j):
        return remote(
            term_rows(i, across(j)), term_in.at[i, 1], term_send.at[i, 1 + j], term_recv.at[i, 1],
            place.line_device(across(j)),
        )

    def send_term(i):
        if paired:
            near_copy(i).start()

            @pl.when(jnp.logical_not(inner))
            def _():
                for j in range(2):
                    relay_copy(i, j).start()

        else:
            for step in range(1, groups):
                term_copy(i, step).start()

    def relay_term(i, buf):
        if not paired:
            return

        @pl.when(inner)
        def _():
            for j in range(2):
                relay_copy(i, j).wait_recv()
                load = pltpu.make_async_copy(term_in.at[i, 2 + j], buf, left_sem.at[0])
                load.start()
                load.wait()
                rows = pl.ds(pl.multiple_of(across(j) * block, block), block)
                term_buf[i, rows, :] = (term_buf[i, rows, :].astype(F32) + buf[...].astype(F32)).astype(BF16)
                across_copy(i, j).start()

    def arrived_terms(i):
        if not paired:
            for step in range(1, groups):
                term_copy(i, step).wait()
            return range(groups - 1)
        near_copy(i).wait()
        across_copy(i, 0).wait_recv()
        for j in range(2):
            across_copy(i, j).wait_send()
        return range(2)

    def weight_terms(left_buf, acc):
        for i, (lefts, rights) in enumerate(((acts, all_grad), (grad_gates, all_ffn), (grad_ups, all_ffn))):

            def copies(dp, slot, lefts=lefts, rights=rights):
                return (
                    pltpu.make_async_copy(lefts.at[dp], left_buf.at[slot], left_sem.at[slot]),
                    pltpu.make_async_copy(rights.at[dp], out_w.at[slot], right_sem.at[slot]),
                )

            for copy in copies(0, 0):
                copy.start()

            def one(dp, _, copies=copies):
                slot = dp % 2

                @pl.when(dp + 1 < dp_count)
                def _():
                    for copy in copies(dp + 1, 1 - slot):
                        copy.start()

                for copy in copies(dp, slot):
                    copy.wait()
                left = left_buf[slot].T


                @pl.when(dp == 0)
                def _():
                    acc[...] = jnp.zeros_like(acc)

                acc[...] += jnp.dot(left, out_w[slot], preferred_element_type=F32)
                return 0

            lax.fori_loop(0, dp_count, one, 0)
            term_buf[i] = acc[0:unit_rows, :].astype(BF16)
            send_term(i)

    pl.run_scoped(weight_terms, pltpu.VMEM((2, piece, padded), BF16), pltpu.VMEM((padded, width), F32))

    pl.run_scoped(
        input_sum,
        pltpu.VMEM((2, 2, piece, padded), BF16), pltpu.VMEM((piece, width), BF16), pltpu.VMEM((piece, width), BF16),
    )

    def plane_copy(step):
        return remote(
            branch_out.at[step], branch_in.at[step - 1], plane_send.at[step - 1], plane_recv.at[step - 1],
            place.chip_device(place.chip_at(step)),
        )

    def branch_parts(relay_buf, act_buf, branch_buf, core_out, load_buf):
        relay_term(0, relay_buf)

        def act_copy(u):
            return pltpu.make_async_copy(acts.at[piece_of(u, False)[2]], act_buf.at[u % 2], act_sem.at[u % 2, 0])

        def part_copy(step):
            return remote(core_out, branch_core.at[step], part_send, part_recv.at[step], place.sibling)

        def load_copy(step):
            return pltpu.make_async_copy(branch_core.at[step], load_buf, load_sem)

        def store(step):
            return pltpu.make_async_copy(branch_buf.at[step % 2], branch_out.at[step], branch_sem.at[step % 2])

        act_copy(0).start()

        def one(u, _):
            step, which, dp = piece_of(u, False)
            slot = u % 2

            @pl.when(u + 1 < pieces)
            def _():
                act_copy(u + 1).start()

            act_copy(u).wait()

            @pl.when((which == 0) & (step > 0))
            def _():
                part_copy(step - 1).wait_send()

            @pl.when(which == 1)
            def _():
                part_copy(step).wait_recv()
                load_copy(step).start()

                @pl.when(step > 1)
                def _():
                    store(step - 2).wait()

                load_copy(step).wait()

            def part_of(part, _):
                columns = group_columns(part)
                value = mxu(act_buf[slot], down_w[:, columns], NN)

                @pl.when(which == 0)
                def _():
                    core_out[:, columns] = value.astype(BF16)

                @pl.when(which == 1)
                def _():
                    branch_buf[step % 2, :, columns] = (value + load_buf[:, columns].astype(F32)).astype(BF16)

                return 0

            lax.fori_loop(0, groups, part_of, 0)

            @pl.when(which == 0)
            def _():
                part_copy(step).start()

            @pl.when(which == 1)
            def _():
                store(step).start()

            return 0

        lax.fori_loop(0, pieces, one, 0)
        part_copy(chips - 1).wait_send()
        for step in range(max(chips - 2, 0), chips):
            store(step).wait()
        relay_term(1, relay_buf)

    pl.run_scoped(
        branch_parts,
        pltpu.VMEM((block, width), BF16), pltpu.VMEM((2, piece, padded), BF16), pltpu.VMEM((2, piece, width), BF16),
        pltpu.VMEM((piece, width), BF16), pltpu.VMEM((piece, width), BF16),
    )

    for step in range(1, chips):
        landed = chip_in.at[step - 1]
        remote(landed, landed, far_send.at[step - 1], far_recv.at[step - 1], place.sibling).wait_recv()
    for step in range(1, chips):
        plane_copy(step).start()
    for step in range(1, chips):
        to_chip(step).wait_send()
    gain_term[...] = jnp.zeros_like(gain_term)

    def norm_and_heads(rows_buf, mid_buf, layer_buf, heads_buf, sum_buf):
        def rows_copy(index, step, slot):
            source = grad_own.at[batch(index), :] if step == 0 else chip_in.at[step - 1, batch(index), :]
            return pltpu.make_async_copy(source, rows_buf.at[slot, step], rows_sem.at[slot, step])

        def layer_rows(index, step, slot):
            source = branch_out.at[0] if step == 0 else branch_in.at[step - 1]
            return pltpu.make_async_copy(
                source.at[batch(index), :], rows_buf.at[slot, step], rows_sem.at[slot, step]
            )

        def layer_copy(index, slot):
            return pltpu.make_async_copy(layer_buf.at[slot], layer_out.at[batch(index), :], gm_sem.at[slot])

        def grad_mid_copy(index, slot):
            return pltpu.make_async_copy(mid_buf.at[slot], grad_mid.at[batch(index), :], gm_sem.at[slot])

        for step in range(chips):
            rows_copy(0, step, 0).start()

        def norm_back(index, _):
            slot = index % 2

            @pl.when(index + 1 < batches)
            def _():
                for step in range(chips):
                    rows_copy(index + 1, step, 1 - slot).start()

            for step in range(chips):
                rows_copy(index, step, slot).wait()

            @pl.when(index >= 2)
            def _():
                grad_mid_copy(index - 2, slot).wait()

            rows = batch(index)
            grad = own_total[rows, :]
            for step in range(1, chips):
                grad = grad + rows_buf[slot, step].astype(F32)
            x = mid[rows, :]
            rstd = lax.rsqrt(jnp.mean(x * x, axis=-1, keepdims=True) + EPSILON)
            normed = x * rstd
            gain_term[0:1, :] += jnp.sum(normed * grad, axis=0, keepdims=True)
            scaled = grad * gain_rows[1:2, :]
            shift = jnp.mean(scaled * normed, axis=-1, keepdims=True)
            total = rows_buf[slot, 0].astype(F32) + rstd * (scaled - normed * shift)
            mid_buf[slot] = total
            ffn_in[rows, :] = total.astype(BF16)
            grad_mid_copy(index, slot).start()
            return 0

        lax.fori_loop(0, batches, norm_back, 0)
        grad_branch_copy = pltpu.make_async_copy(ffn_in, grad_branch, gb_sem)
        grad_branch_copy.start()
        for index in range(max(batches - 2, 0), batches):
            grad_mid_copy(index, index % 2).wait()

        def head_copy(step):
            other = place.line_at(step)
            return remote(
                heads_buf.at[other], grad_heads.at[seq], head_send.at[step - 1], head_recv.at[step - 1],
                place.line_device(other),
            )

        own_heads = pltpu.make_async_copy(heads_buf.at[seq], grad_heads.at[seq], head_own)
        order = tuple(range(1, groups)) + (0,)
        out_copy(place.line_at(order[0]), 0).start()
        for at, step in enumerate(order):
            group = place.line_at(step)
            if at + 1 < groups:
                out_copy(place.line_at(order[at + 1]), (at + 1) % 2).start()
            out_copy(group, at % 2).wait()
            heads_buf[group] = mxu(ffn_in[...], out_w[at % 2], NT).astype(BF16)
            if step > 0:
                head_copy(step).start()
            else:
                own_heads.start()

        relay_term(2, sum_buf.at[0])

        for i, target in enumerate((grad_down, grad_gate, grad_up)):
            landed = arrived_terms(i)
            for j in landed:
                load = pltpu.make_async_copy(term_in.at[i, j], sum_buf.at[j], rows_sem.at[0, 0])
                load.start()
                load.wait()
            total = term_buf[i, pl.ds(pl.multiple_of(seq * block, block), block), :].astype(F32)
            for j in landed:
                total = total + sum_buf[j].astype(F32)
            own_total[0:block, :] = total
            store = pltpu.make_async_copy(own_total.at[pl.ds(0, block), :], target, gm_sem.at[0])
            store.start()
            store.wait()
        for step in range(1, chips):
            plane_copy(step).wait()
        for step in range(chips):
            layer_rows(0, step, 0).start()

        def layer(index, _):
            slot = index % 2

            @pl.when(index + 1 < batches)
            def _():
                for step in range(chips):
                    layer_rows(index + 1, step, 1 - slot).start()

            for step in range(chips):
                layer_rows(index, step, slot).wait()

            @pl.when(index >= 2)
            def _():
                layer_copy(index - 2, slot).wait()

            total = mid[batch(index), :]
            for step in range(chips):
                total = total + rows_buf[slot, step].astype(F32)
            layer_buf[slot] = total.astype(BF16)
            layer_copy(index, slot).start()
            return 0

        lax.fori_loop(0, batches, layer, 0)
        for index in range(max(batches - 2, 0), batches):
            layer_copy(index, index % 2).wait()
        grad_branch_copy.wait()
        own_heads.wait()
        for step in range(1, groups):
            head_copy(step).wait()

    pl.run_scoped(
        norm_and_heads,
        pltpu.VMEM((2, chips, some, width), BF16), pltpu.VMEM((2, some, width), F32),
        pltpu.VMEM((2, some, width), BF16), pltpu.VMEM((groups, piece, share), BF16), pltpu.VMEM((groups - 1, block, width), BF16),
    )
    for step in range(1, groups):
        collect(step).wait_send()
    for step in range(chips):
        to_sibling(step).wait_send()
    for step in range(1, chips):
        far_copy(step).wait_send()


def middle_call(dp_count, groups, piece, width, unit_rows):
    chips = dp_count // 2
    share = width // groups
    assert share == piece
    padded = -(-unit_rows // 128) * 128
    block = unit_rows // groups
    others = max(chips - 1, 1)
    hbm = pl.BlockSpec(memory_space=pl.ANY)
    vmem = pl.BlockSpec(memory_space=pltpu.VMEM)
    dma = pltpu.SemaphoreType.DMA
    shape = jax.ShapeDtypeStruct
    return pl.pallas_call(
        functools.partial(middle_kernel, dp_count, groups),
        in_specs=[vmem] + [hbm] * 8,
        out_specs=[vmem, vmem] + [hbm] * 18,
        out_shape=(
            shape((piece, width), BF16),
            shape((8, width), F32),
            shape((piece, width), BF16),
            shape((piece, width), F32),
            shape((piece, width), BF16),
            shape((groups, piece, share), BF16),
            shape((block, width), F32),
            shape((block, width), F32),
            shape((block, width), F32),
            shape((dp_count, piece, width), BF16),
            shape((dp_count, piece, padded), F32),
            shape((dp_count, piece, padded), BF16),
            shape((dp_count, piece, padded), BF16),
            shape((dp_count, piece, padded), BF16),
            shape((chips, piece, width), BF16),
            shape((others, piece, width), BF16),
            shape((chips, piece, width), BF16),
            shape((chips, piece, width), BF16),
            shape((others, piece, width), BF16),
            shape((3, max(groups - 1, 4), block, width), BF16),
        ),
        scratch_shapes=[
            pltpu.VMEM((padded, width), BF16), pltpu.VMEM((padded, width), BF16), pltpu.VMEM((padded, width), BF16),
            pltpu.VMEM((2, share, width), BF16),
            pltpu.VMEM((piece, width), F32),
            pltpu.VMEM((piece, width), BF16),
            pltpu.VMEM((piece, width), F32),
            pltpu.VMEM((others, piece, width), BF16),
            pltpu.VMEM((3, unit_rows, width), BF16),
            dma((groups - 1,)), dma((groups - 1,)), dma, dma((3,)), dma((2,)),
            dma((others,)), dma((others,)), dma((chips,)), dma((chips,)), dma,
            dma((2,)), dma((2,)), dma((2, 3)),
            dma, dma((chips,)), dma, dma((others,)), dma((others,)),
            dma((2,)), dma((2,)), dma((2,)),
            dma, dma((chips,)), dma((others,)), dma((others,)), dma((3, max(groups - 1, 4))), dma((3, max(groups - 1, 4))),
            dma((2, chips)), dma((2,)), dma,
            dma((groups - 1,)), dma((groups - 1,)), dma,
        ],
        compiler_params=pltpu.CompilerParams(
            collective_id=5, has_side_effects=True, vmem_limit_bytes=63 * 1024 * 1024
        ),
        cost_estimate=pl.CostEstimate(
            flops=128 * piece * width * width, transcendentals=0, bytes_accessed=64 * width * width
        ),
        name="feed_forward",
    )


def shards(
    hidden_in, memory, segments, gain_attn, w_query, w_key, w_value, w_out, gain_ffn, w_gate, w_up, w_down, cotangent
):
    seqs, piece, width = hidden_in.shape
    groups = lax.axis_size("seq")
    dp_count = lax.axis_size("dp")
    assert seqs == 1
    length = piece * groups
    share = width // groups
    heads = share // HEAD_DIM
    here = w_query.shape[0]
    block = min(256, length)
    tokens = hidden_in.reshape(piece, width)
    mem = memory.reshape(piece, width)
    grad_out = cotangent.reshape(piece, width)

    attend_forward, attend_backward = attention_calls(length, heads, block)
    start, low, high = document_bounds(segments[0], block)
    flat = (length, share)
    split = (groups, piece, share)

    units = w_gate.shape[0]
    padded = -(-units // 16) * 16
    own_units = [jnp.pad(weight, ((0, padded - units), (0, 0))) for weight in (w_gate, w_up, w_down)]
    (
        attn_in, gain_rows, key, value, query, _, key_rows, value_rows, query_rows, out_rows,
        gate_rows, up_rows, down_rows, dy,
    ) = project_call(dp_count, groups, piece, width, here, padded, 1)(
        tokens, mem, gain_tile(gain_attn, gain_ffn), w_key, w_value, w_query, w_out, *own_units, grad_out
    )
    gate_rows, up_rows, down_rows = [
        rows.reshape(groups * padded, width) for rows in (gate_rows, up_rows, down_rows)
    ]
    key, value, query = [part.reshape(flat) for part in (key, value, query)]
    key_rows, value_rows, query_rows, out_rows = [
        rows.reshape(width, width) for rows in (key_rows, value_rows, query_rows, out_rows)
    ]
    context_heads, lse = attend_forward(low, start, query, key, value)
    (
        context, gain_term, layer_out, grad_mid, grad_branch, grad_context_heads, grad_w_down, grad_w_gate, grad_w_up, *_
    ) = middle_call(dp_count, groups, piece, width, groups * padded)(
        gain_rows, tokens, context_heads.reshape(split), grad_out, out_rows, gate_rows, up_rows, down_rows,
        dy.reshape(dp_count, piece, width),
    )
    grad_context_heads = grad_context_heads.reshape(flat)
    dq, dk, dv = attend_backward(high, start, query, key, value, context_heads, grad_context_heads, lse)

    grad_w_out, grad_w_value, grad_w_key, grad_w_query, grad_memory, grad_hidden, gains = reduce_call(
        dp_count, groups, piece, width, here
    )(
        context, mem, attn_in, gain_rows, gain_term, grad_branch, dv.reshape(split), dk.reshape(split),
        dq.reshape(split), value_rows, key_rows, query_rows, tokens, grad_mid,
    )
    grad_w_down, grad_w_gate, grad_w_up = [grad[:units] for grad in (grad_w_down, grad_w_gate, grad_w_up)]
    grad_gain_attn, grad_gain_ffn = gains[0, :here], gains[1, :here]
    cube = (seqs, piece, width)
    return (
        layer_out.reshape(cube),
        grad_hidden.reshape(cube),
        grad_memory.reshape(cube),
        grad_gain_attn,
        grad_w_query,
        grad_w_key,
        grad_w_value,
        grad_w_out,
        grad_gain_ffn,
        grad_w_gate,
        grad_w_up,
        grad_w_down,
    )


def solution(mesh):
    tokens = P("dp", "seq", None)
    rows = P(ALL, None)
    gain = P(ALL)
    in_specs = (tokens, tokens, P("dp", None), gain, rows, rows, rows, rows, gain, rows, rows, rows, tokens)
    out_specs = (tokens, tokens, tokens, gain, rows, rows, rows, rows, gain, rows, rows, rows)
    return jax.shard_map(shards, mesh=mesh, in_specs=in_specs, out_specs=out_specs, check_vma=False)
```
